32 devices in a mesh: grp: 2 (over core), dp: 16 (over z, y, x).
Axes of the slice: x: 2, y: 2, z: 4, core: 2. Of those that a mesh axis runs over, the one named last changes fastest.
Arguments:
- layer_input: bfloat16 [49152, 768], P(('grp', 'dp')), may hold values from -6 to 6
- lengths: int32 [32, 3], P(('grp', 'dp')), may hold values from 40 to 512, as said below
- query_weight: bfloat16 [768, 384], replicated, may hold values from -0.21875 to 0.21875
- query_bias: float32 [384], replicated, may hold values from -3 to 3
- key_weight: bfloat16 [768, 384], replicated, may hold values from -0.21875 to 0.21875
- value_weight: bfloat16 [768, 384], replicated, may hold values from -0.21875 to 0.21875
- value_bias: float32 [384], replicated, may hold values from -3 to 3
- depth_kernel: float32 [9, 768], replicated, may hold values from -2 to 2
- point_weight: bfloat16 [768, 384], replicated, may hold values from -0.21875 to 0.21875
- point_bias: float32 [384], replicated, may hold values from -3 to 3
- span_weight: bfloat16 [384, 54], replicated, may hold values from -0.3125 to 0.3125
- span_bias: float32 [54], replicated, may hold values from -6 to 6
- conv_out_weight: bfloat16 [768, 384], replicated, may hold values from -0.21875 to 0.21875
- conv_out_bias: float32 [384], replicated, may hold values from -3 to 3
- dense_weight: bfloat16 [768, 768], replicated, may hold values from -0.875 to 0.875
- dense_bias: float32 [768], replicated, may hold values from -3 to 3
- first_gain: float32 [768], replicated, may hold values from 0.5 to 1.5
- first_shift: float32 [768], replicated, may hold values from -3 to 3
- inter_weight: bfloat16 [2, 384, 1536], P('grp', None, 'dp'), may hold values from -0.3125 to 0.3125
- inter_bias: float32 [2, 1536], P('grp', 'dp'), may hold values from -3 to 3
- grouped_down_weight: bfloat16 [2, 1536, 384], P('grp', 'dp'), may hold values from -0.15625 to 0.15625
- output_bias: float32 [768], replicated, may hold values from -3 to 3
- second_gain: float32 [768], replicated, may hold values from 0.5 to 1.5
- second_shift: float32 [768], replicated, may hold values from -3 to 3
- upstream_grad: bfloat16 [49152, 768], P(('grp', 'dp')), may hold values from -6 to 6
Outputs:
- layer_out: bfloat16 [49152, 768], P(('grp', 'dp'))
- in_grad: bfloat16 [49152, 768], P(('grp', 'dp'))
- grad_query_weight: float32 [768, 384], replicated
- grad_query_bias: float32 [384], replicated
- grad_key_weight: float32 [768, 384], replicated
- grad_value_weight: float32 [768, 384], replicated
- grad_value_bias: float32 [384], replicated
- grad_depth_kernel: float32 [9, 768], replicated
- grad_point_weight: float32 [768, 384], replicated
- grad_point_bias: float32 [384], replicated
- grad_span_weight: float32 [384, 54], replicated
- grad_span_bias: float32 [54], replicated
- grad_conv_out_weight: float32 [768, 384], replicated
- grad_conv_out_bias: float32 [384], replicated
- grad_dense_weight: float32 [768, 768], replicated
- grad_dense_bias: float32 [768], replicated
- grad_first_gain: float32 [768], replicated
- grad_first_shift: float32 [768], replicated
- grad_inter_weight: float32 [2, 384, 1536], P('grp', None, 'dp')
- grad_inter_bias: float32 [2, 1536], P('grp', 'dp')
- grad_output_weight: float32 [2, 1536, 384], P('grp', 'dp')
- grad_output_bias: float32 [768], replicated
- grad_second_gain: float32 [768], replicated
- grad_second_shift: float32 [768], replicated
The draws below stay inside these ranges and needn't reach their ends.
Inputs may be any that keep to these rules, and one draw needn't show every extreme that they name: Row b of lengths holds the 3 sequence lengths of the b-th block of 1536 rows; every draw has a sequence of exactly 512 tokens and one of exactly 40.
All inputs are finite; a program needn't handle non-finite values.
Results may differ from the reference program's by a relative error of at most 0.025.
Values may be sent and summed in bfloat16 or wider, within the bound.
No kernel may reach another device: no remote copies, remote signals or barrier semaphores. Data moves between devices by JAX's collectives and lax.ppermute only.
A program may use at most 320 MiB of HBM per device.

```python
import math
import jax
import jax.numpy as jnp
from jax import lax

D = 768
HEADS = 6
HEAD_DIM = 64
KERNEL = 9
FF = 3072
GROUPS = 2
MAX_LEN = 512
MIN_LEN = 40
SEQ_DEV = 3
ATT = 384
TOK_DEV = 1536
BUFFERS = 32
TOKENS = 49152


def draw_lengths(key, part):
    first_key, second_key, third_key = jax.random.split(jax.random.fold_in(key, 17), 3)
    slots = BUFFERS * SEQ_DEV
    drawn = jax.random.randint(first_key, (slots,), MIN_LEN, MAX_LEN + 1)
    longest = jax.random.randint(second_key, (), 0, slots)
    step_away = jax.random.randint(third_key, (), 1, slots)
    shortest = (longest + step_away) % slots
    places = jnp.arange(slots)
    drawn = jnp.where(places == longest, MAX_LEN, drawn)
    drawn = jnp.where(places == shortest, MIN_LEN, drawn)
    return drawn.reshape(BUFFERS, SEQ_DEV).astype(jnp.int32)


def block_levels(rng, extent, cuts, least, largest):
    loudness, own = 1.0, jax.random.fold_in(rng, 6)
    for dim, parts in cuts:
        steps = jnp.exp(jax.random.uniform(jax.random.fold_in(own, dim), (parts,), jnp.float32, least / len(cuts), largest / len(cuts)))
        loudness = loudness * jnp.repeat(steps, extent[dim] // parts).reshape([-1 if axis == dim else 1 for axis in range(len(extent))])
    return loudness


def normal_values(own_key, dims, width, bound, shards=(), kind=jnp.bfloat16):
    factor_of = block_levels(own_key, dims, shards, -0.22, 0.18) if shards else 1.0
    entries = jax.random.normal(own_key, dims, jnp.float32) * width * factor_of
    return jnp.minimum(jnp.maximum(entries, -bound), bound).astype(kind)


def setup_inputs(seed: int = 0) -> dict:
    key_of = jax.random.split(jax.random.key(seed), 26)
    return {
        "layer_input": normal_values(key_of[0], (TOKENS, D), 1.0, 6.0, ((0, 32),)),
        "lengths": draw_lengths(jax.random.fold_in(key_of[25], 71), 0),
        "query_weight": normal_values(key_of[2], (D, ATT), D ** -0.5, 0.21875),
        "query_bias": normal_values(key_of[3], (ATT,), 0.5, 3.0, (), jnp.float32),
        "key_weight": normal_values(key_of[4], (D, ATT), D ** -0.5, 0.21875),
        "value_weight": normal_values(key_of[5], (D, ATT), D ** -0.5, 0.21875),
        "value_bias": normal_values(key_of[6], (ATT,), 0.5, 3.0, (), jnp.float32),
        "depth_kernel": normal_values(key_of[7], (KERNEL, D), KERNEL ** -0.5, 2.0, (), jnp.float32),
        "point_weight": normal_values(key_of[8], (D, ATT), D ** -0.5, 0.21875),
        "point_bias": normal_values(key_of[9], (ATT,), 0.5, 3.0, (), jnp.float32),
        "span_weight": normal_values(key_of[10], (ATT, HEADS * KERNEL), ATT ** -0.5, 0.3125),
        "span_bias": normal_values(key_of[11], (HEADS * KERNEL,), 1.0, 6.0, (), jnp.float32),
        "conv_out_weight": normal_values(key_of[12], (D, ATT), D ** -0.5, 0.21875),
        "conv_out_bias": normal_values(key_of[13], (ATT,), 0.5, 3.0, (), jnp.float32),
        "dense_weight": normal_values(key_of[14], (D, D), (D // 16) ** -0.5, 0.875),
        "dense_bias": normal_values(key_of[15], (D,), 0.5, 3.0, (), jnp.float32),
        "first_gain": jnp.clip(1.0 + 0.1 * jax.random.normal(key_of[16], (D,), jnp.float32), 0.5, 1.5),
        "first_shift": normal_values(key_of[17], (D,), 0.5, 3.0, (), jnp.float32),
        "inter_weight": normal_values(key_of[18], (GROUPS, D // GROUPS, FF // GROUPS), (D // GROUPS) ** -0.5, 0.3125, ((0, 2), (2, 16))),
        "inter_bias": normal_values(key_of[19], (GROUPS, FF // GROUPS), 0.5, 3.0, ((0, 2), (1, 16)), jnp.float32),
        "grouped_down_weight": normal_values(key_of[20], (GROUPS, FF // GROUPS, D // GROUPS), (FF // GROUPS) ** -0.5, 0.15625, ((0, 2), (1, 16))),
        "output_bias": normal_values(key_of[21], (D,), 0.5, 3.0, (), jnp.float32),
        "second_gain": jnp.clip(1.0 + 0.1 * jax.random.normal(key_of[22], (D,), jnp.float32), 0.5, 1.5),
        "second_shift": normal_values(key_of[23], (D,), 0.5, 3.0, (), jnp.float32),
        "upstream_grad": normal_values(key_of[24], (TOKENS, D), 1.0, 6.0, ((0, 32),)),
    }


FULL_PRECISION = lax.Precision.HIGHEST
NEGATIVE = -1e+30
NORM_EPS = 1e-12

@jax.custom_vjp
def reduced_precision(v):
    return lax.optimization_barrier(v.astype(jnp.bfloat16)).astype(jnp.float32)

@jax.custom_vjp
def reduced_precision_backward(v):
    return v

def low_keep(v):
    return (reduced_precision(v), None)

def low_pass(kept, grad):
    return (grad,)

def back_keep(v):
    return (v, None)

def back_low(kept, grad):
    return (reduced_precision(grad),)
reduced_precision.defvjp(low_keep, low_pass)
reduced_precision_backward.defvjp(back_keep, back_low)

def product(left, right):
    return jnp.dot(left, right, precision=FULL_PRECISION, preferred_element_type=jnp.float32)

def segments(length_row, total_rows):
    ends = jnp.cumsum(length_row).astype(jnp.int32)
    places = jnp.arange(total_rows, dtype=jnp.int32)
    segment = lax.optimization_barrier(jnp.sum((places[:, None] >= ends[None, :]).astype(jnp.int32), axis=1))
    alive = places < ends[-1]
    segment = jnp.where(alive, segment, length_row.shape[0] + places)
    return (segment.astype(jnp.int32), alive)

def shifted(values, segment, offset):
    total_rows = values.shape[0]
    if offset == 0:
        return values
    reach = abs(offset)
    padding = jnp.zeros((reach,) + values.shape[1:], values.dtype)
    outside = jnp.full((reach,), -1, jnp.int32)
    if offset > 0:
        moved = jnp.concatenate([values[reach:], padding], 0)
        moved_segment = jnp.concatenate([segment[reach:], outside], 0)
    else:
        moved = jnp.concatenate([padding, values[:total_rows - reach]], 0)
        moved_segment = jnp.concatenate([outside, segment[:total_rows - reach]], 0)
    matching = (moved_segment == segment).reshape((total_rows,) + (1,) * (values.ndim - 1))
    return jnp.where(matching, moved, jnp.zeros_like(moved))

def layer_norm(summed, gain, shift):
    centred = summed - lax.optimization_barrier(jnp.mean(summed, axis=-1, keepdims=True))
    spread = lax.optimization_barrier(jnp.mean(centred * centred, axis=-1, keepdims=True))
    return centred * lax.rsqrt(spread + NORM_EPS) * gain + shift

def buffer_forward(block_input, length_row, params):
    query_weight, query_bias, key_weight, value_weight, value_bias, depth_kernel, point_weight, point_bias, span_weight, span_bias, conv_out_weight, conv_out_bias, dense_weight, dense_bias, first_gain, first_shift, inter_weight, inter_bias, grouped_down_weight, output_bias, second_gain, second_shift = params
    total_rows = block_input.shape[0]
    reach = KERNEL // 2
    segment, alive = segments(length_row, total_rows)
    query = reduced_precision_backward(reduced_precision(product(block_input, query_weight) + query_bias))
    keys = reduced_precision_backward(reduced_precision(product(block_input, key_weight)))
    values = reduced_precision_backward(reduced_precision(product(block_input, value_weight) + value_bias))
    depthwise = jnp.zeros((total_rows, D), jnp.float32)
    for tap_index in range(KERNEL):
        depthwise = depthwise + depth_kernel[tap_index] * shifted(block_input, segment, tap_index - reach)
    depthwise = reduced_precision_backward(reduced_precision(depthwise))
    keyconv = reduced_precision_backward(product(depthwise, point_weight) + point_bias)
    span_in = reduced_precision_backward(reduced_precision(keyconv * query))
    span_logits = reduced_precision_backward(product(span_in, span_weight) + span_bias).reshape(total_rows, HEADS, KERNEL)
    taps = jax.nn.softmax(span_logits, axis=-1)
    conv_source = reduced_precision_backward(product(block_input, conv_out_weight) + conv_out_bias).reshape(total_rows, HEADS, HEAD_DIM)
    convolved = jnp.zeros((total_rows, HEADS, HEAD_DIM), jnp.float32)
    for tap_index in range(KERNEL):
        convolved = convolved + taps[:, :, tap_index:tap_index + 1] * shifted(conv_source, segment, tap_index - reach)
    query_heads = query.reshape(total_rows, HEADS, HEAD_DIM)
    key_heads = keys.reshape(total_rows, HEADS, HEAD_DIM)
    value_heads = values.reshape(total_rows, HEADS, HEAD_DIM)
    scores = jnp.einsum('qhd,khd->hqk', query_heads, key_heads, precision=FULL_PRECISION) * (1.0 / math.sqrt(HEAD_DIM))
    scores = reduced_precision_backward(scores)
    allowed = segment[:, None] == segment[None, :]
    scores = jnp.where(allowed[None], scores, NEGATIVE)
    probs = reduced_precision(jax.nn.softmax(scores, axis=-1))
    attended = jnp.einsum('hqk,khd->qhd', probs, value_heads, precision=FULL_PRECISION).reshape(total_rows, ATT)
    context = reduced_precision_backward(reduced_precision(jnp.concatenate([attended, convolved.reshape(total_rows, ATT)], 1)))
    mixed = reduced_precision_backward(product(context, dense_weight) + dense_bias)
    normed1 = reduced_precision(layer_norm(mixed + block_input, first_gain, first_shift))
    grouped = reduced_precision_backward(normed1).reshape(total_rows, GROUPS, D // GROUPS)
    inner = reduced_precision_backward(jnp.einsum('ngc,gcf->ngf', grouped, inter_weight, precision=FULL_PRECISION) + inter_bias[None])
    activated_rows = reduced_precision(jax.nn.gelu(inner, approximate=False))
    partial_output_rows = reduced_precision_backward(reduced_precision(jnp.einsum('iao,aoj->iaj', activated_rows, grouped_down_weight, precision=FULL_PRECISION)))
    partial_output_rows = partial_output_rows.reshape(total_rows, D)
    result = layer_norm(partial_output_rows + output_bias + normed1, second_gain, second_shift)
    return result * alive[:, None].astype(jnp.float32)

def reference(layer_input, lengths, query_weight, query_bias, key_weight, value_weight, value_bias, depth_kernel, point_weight, point_bias, span_weight, span_bias, conv_out_weight, conv_out_bias, dense_weight, dense_bias, first_gain, first_shift, inter_weight, inter_bias, grouped_down_weight, output_bias, second_gain, second_shift, upstream_grad):
    params = tuple((item.astype(jnp.float32) for item in (query_weight, query_bias, key_weight, value_weight, value_bias, depth_kernel, point_weight, point_bias, span_weight, span_bias, conv_out_weight, conv_out_bias, dense_weight, dense_bias, first_gain, first_shift, inter_weight, inter_bias, grouped_down_weight, output_bias, second_gain, second_shift)))
    inputs = layer_input.astype(jnp.float32).reshape(BUFFERS, TOK_DEV, D)

    def forward(blocks_in, weights):

        def one_buffer(block_input, length_row):
            return buffer_forward(block_input, length_row, weights)
        checked = jax.checkpoint(one_buffer)
        return lax.map(lambda pair: checked(pair[0], pair[1]), (blocks_in, lengths))
    outputs, pullback = jax.vjp(forward, inputs, params)
    grad_inputs, grads = pullback(upstream_grad.astype(jnp.float32).reshape(BUFFERS, TOK_DEV, D))
    return (outputs.reshape(TOKENS, D).astype(jnp.bfloat16), grad_inputs.reshape(TOKENS, D).astype(jnp.bfloat16), grads[0], grads[1], grads[2], grads[3], grads[4], grads[5], grads[6], grads[7], grads[8], grads[9], grads[10], grads[11], grads[12], grads[13], grads[14], grads[15], grads[16], grads[17], grads[18], grads[19], grads[20], grads[21])
```

```python
import functools

import jax
import jax.numpy as jnp
from jax import lax
from jax.experimental import pallas as pl
from jax.experimental.pallas import tpu as pltpu
from jax.sharding import PartitionSpec as P

HEADS = 6
HEAD_DIM = 64
KERNEL = 9
REACH = KERNEL // 2
SLOT = 512
HALO = 8
LANES = 128
TAP_STRIDE = 8
CHUNK_ROWS = 768
EXTRA = 128
SPAN_ROW = 16
OWN_ROW = 152
SMALL_ROWS = 160
BIAS_ROWS = 8
RADIX = 4
NEGATIVE = -1e30
NORM_EPS = 1e-12
ROOT_HALF = 0.7071067811865476
DENSITY = 0.3989422804014327
BF16 = jnp.bfloat16
F32 = jnp.float32


def product(left, right):
    return jnp.dot(left, right, preferred_element_type=F32)


def right_product(left, right):
    return lax.dot_general(left, right, (((1,), (1,)), ((), ())), preferred_element_type=F32)


def transposed(block):
    return jnp.transpose(block, (1, 0))


def column_sum(block):
    return jnp.sum(block, axis=0, keepdims=True)


def row_mean(block):
    return jnp.mean(block, axis=-1, keepdims=True)


def tap_groups(block, combine):
    step = TAP_STRIDE
    while step < LANES:
        block = combine(block, pltpu.roll(block, step, 1))
        step *= 2
    return block


def high_low(block):
    high = block.astype(BF16)
    low = (block - high.astype(F32)).astype(BF16)
    return high, low


def slot_bounds(info_ref, index):
    start = jnp.int32(0)
    for other in range(info_ref.shape[0] - 3):
        start = start + jnp.where(index > other, info_ref[other], 0)
    return start, info_ref[index]


def my_place(info_ref):
    return info_ref[info_ref.shape[0] - 2], info_ref[info_ref.shape[0] - 1]


def rows_to_slot(source_ref, start, length, write):
    total = source_ref.shape[0]
    step, window = 128, 256
    for piece in range(SLOT // step):
        first = start + piece * step
        base = jnp.minimum(first // 16 * 16, total - window)
        base = pl.multiple_of(base, 16)
        row = lax.broadcasted_iota(jnp.int32, (step, window), 0)
        col = lax.broadcasted_iota(jnp.int32, (step, window), 1)
        pick = (col + base == row + first) & (row + piece * step < length)
        pick = jnp.where(pick, 1.0, 0.0).astype(BF16)
        write(piece * step, step, product(pick, source_ref[pl.ds(base, window), :]))


def pair_mask(half):
    lane = lax.broadcasted_iota(jnp.int32, (1, LANES), 1)
    return (lane // HEAD_DIM) == half


def digits_of(count):
    digits, stride = [], 1
    while stride < count:
        radix = RADIX if (count // stride) % RADIX == 0 else 2
        digits.append((stride, radix))
        stride *= radix
    return digits


def offset_masks(count):
    masks = [0]
    for stride, radix in reversed(digits_of(count)):
        masks = [digit * stride ^ mask for digit in range(radix) for mask in masks]
    return masks


def vector_row(ref):
    return ref[...].reshape(1, ref.shape[0])


def tap_order():
    row = lax.broadcasted_iota(jnp.int32, (HEADS * KERNEL, LANES), 0)
    lane = lax.broadcasted_iota(jnp.int32, (HEADS * KERNEL, LANES), 1)
    tap, head = lane // TAP_STRIDE, lane % TAP_STRIDE
    return (row == head * KERNEL + tap) & (head < HEADS) & (tap < KERNEL)


def ordered_span(ws_ref):
    return product(ws_ref[...], jnp.where(tap_order(), 1.0, 0.0).astype(BF16)).astype(BF16)


def spread_table(half):
    lane = lax.broadcasted_iota(jnp.int32, (2 * LANES, half), 0) % LANES
    head = lax.broadcasted_iota(jnp.int32, (2 * LANES, half), 1) // HEAD_DIM
    return jnp.where(lane == head, 1.0, 0.0).astype(BF16)


def gather_table(half):
    head = lax.broadcasted_iota(jnp.int32, (half, LANES), 0) // HEAD_DIM
    lane = lax.broadcasted_iota(jnp.int32, (half, LANES), 1)
    return jnp.where(lane == head, 1.0, 0.0).astype(BF16)


def tap_terms(taps, j):
    moved = taps if j == 0 else pltpu.roll(taps, LANES - j * TAP_STRIDE, 1)
    return jnp.concatenate(high_low(moved), 1)


def project_kernel(
    info_ref, x_ref, wq_ref, wk_ref, wv_ref, wc_ref, bq_ref, bv_ref, bc_ref, xs_ref, qkv_ref, cs_ref
):
    half = wq_ref.shape[1]
    start, length = slot_bounds(info_ref, pl.program_id(0))

    def put_rows(at, count, rows):
        xs_ref[at : at + count, :] = rows.astype(BF16)

    rows_to_slot(x_ref, start, length, put_rows)
    inside = lax.broadcasted_iota(jnp.int32, (SLOT, 1), 0) < length
    rows = xs_ref[...]
    qkv_ref[:, :half] = (product(rows, wq_ref[...]) + vector_row(bq_ref)).astype(BF16)
    qkv_ref[:, half : 2 * half] = product(rows, wk_ref[...]).astype(BF16)
    qkv_ref[:, 2 * half :] = (product(rows, wv_ref[...]) + vector_row(bv_ref)).astype(BF16)
    cs_ref[...] = jnp.where(inside, product(rows, wc_ref[...]) + vector_row(bc_ref), 0.0)


def convolve_kernel(
    info_ref, xs_ref, query_ref, cs_ref, dk_ref, wp_ref, bp_ref, ws_ref, bs_ref,
    dw_ref, kc_ref, taps_ref, conv_ref,
    xh, ch,
):
    width = xs_ref.shape[1]
    half = width // 2
    for halo in (xh, ch):
        halo[0:HALO, :] = jnp.zeros((HALO, halo.shape[1]), F32)
        halo[HALO + SLOT :, :] = jnp.zeros((HALO, halo.shape[1]), F32)
    xh[HALO : HALO + SLOT, :] = xs_ref[...].astype(F32)
    ch[HALO : HALO + SLOT, :] = cs_ref[...]

    def depth_chunk(c, carry):
        lanes = pl.ds(pl.multiple_of(c * LANES, LANES), LANES)
        for part in range(2):
            rows = SLOT // 2
            base = HALO - REACH + part * rows
            total = jnp.zeros((rows, LANES), F32)
            for j in range(KERNEL):
                total = total + dk_ref[j : j + 1, lanes] * xh[base + j : base + j + rows, lanes]
            dw_ref[part * rows : (part + 1) * rows, lanes] = total.astype(BF16)
        return carry

    lax.fori_loop(0, width // LANES, depth_chunk, 0)
    keyconv = product(dw_ref[...], wp_ref[...]) + vector_row(bp_ref)
    kc_ref[...] = keyconv
    span_in = (keyconv * query_ref[...].astype(F32)).astype(BF16)
    wide = jnp.broadcast_to(vector_row(bs_ref), (8, HEADS * KERNEL))
    order = jnp.where(tap_order(), 1.0, 0.0)
    shift = jnp.dot(wide, order, precision=lax.Precision.HIGHEST, preferred_element_type=F32)[0:1]
    lane = lax.broadcasted_iota(jnp.int32, (1, LANES), 1)
    used = (lane // TAP_STRIDE < KERNEL) & (lane % TAP_STRIDE < HEADS)
    shift = jnp.where(used, shift, NEGATIVE)
    logits = product(span_in, ordered_span(ws_ref)) + shift
    weights = jnp.exp(logits - tap_groups(logits, jnp.maximum))
    taps = weights / tap_groups(weights, jnp.add)
    taps_ref[...] = taps
    table = spread_table(half)
    total = jnp.zeros((SLOT, half), F32)
    for j in range(KERNEL):
        spread = product(tap_terms(taps, j), table)
        total = total + spread * ch[HALO - REACH + j : HALO - REACH + j + SLOT, :]
    conv_ref[...] = total.astype(BF16)


def attend_kernel(info_ref, qkv_ref, conv_ref, ctx_ref, lse_ref, att):
    half = conv_ref.shape[1]
    length = info_ref[pl.program_id(0)]
    inside = lax.broadcasted_iota(jnp.int32, (SLOT, 1), 0) < length
    for pair in range(HEADS // 2):
        at = pair * LANES
        query = qkv_ref[:, at : at + LANES]
        keys = qkv_ref[:, half + at : half + at + LANES]
        values = transposed(qkv_ref[:, 2 * half + at : 2 * half + at + LANES])
        for side in range(2):
            mine = jnp.where(pair_mask(side), keys, jnp.zeros_like(keys)) * BF16(0.125)
            scores = right_product(mine, query)
            scores = jnp.where(inside, scores, NEGATIVE)
            highest = jnp.max(scores, axis=0, keepdims=True)
            weights = jnp.exp(scores - highest)
            summed = column_sum(weights)
            probs = (weights * (1.0 / summed)).astype(BF16)
            head = 2 * pair + side
            att[head * HEAD_DIM : (head + 1) * HEAD_DIM, :] = product(
                values[side * HEAD_DIM : (side + 1) * HEAD_DIM, :], probs
            )
            lse_ref[head : head + 1, :] = highest + jnp.log(summed)
    ctx_ref[:, :half] = transposed(att[...]).astype(BF16)
    ctx_ref[:, half:] = conv_ref[...]


def emit_chunks(sources, masks, place, keep_ref, send_ref):
    group, own = place
    count, columns = len(masks), keep_ref.shape[2]
    for position, mask in enumerate(masks):
        for ref, side in ((keep_ref, group), (send_ref, 1 - group)):
            pieces = []
            for source, rows, blocks in sources:
                first = jnp.minimum((side * count + (own ^ mask)) * rows, source.shape[0] - rows)
                piece = source[pl.ds(pl.multiple_of(first, 8), rows), :]
                pieces += [piece[:, b * columns : (b + 1) * columns] for b in range(blocks)]
            ref[position] = jnp.concatenate(pieces, 0).astype(BF16)


def middle_kernel(
    info_ref, ctx_ref, xs_ref, up_ref, wd_ref, bd_ref, g1_ref, b1_ref,
    ob_ref, g2_ref, b2_ref, *rest, pieces,
):
    weight_refs, rest = rest[: 2 * pieces], rest[2 * pieces :]
    (
        out_ref, gm_ref, gctx_ref, keep_ref, send_ref, grad_dense_ref, small_ref,
        w1, w2, bias, act, slope, low1, low2, first_t, grad_t, back, acc1, acc2, sems,
    ) = rest
    step = pl.program_id(0)
    last = pl.num_programs(0) - 1
    start, length = slot_bounds(info_ref, step)
    group = my_place(info_ref)[0]
    count, shard, part = w2.shape[1:]
    blocks = count // pieces
    span = count
    while span * shard > CHUNK_ROWS:
        span //= 2
    per = count // span
    wide = span * shard
    half = part
    width = 2 * half

    def copies():
        made = []
        for side in range(2):
            for piece in range(pieces):
                source = weight_refs[side * pieces + piece]
                at = pl.ds(piece * blocks, blocks)
                made.append((source.at[:, pl.ds(0, shard), :], w1.at[side, at, :, pl.ds(0, part)]))
                made.append((source.at[:, pl.ds(shard, shard), :], w2.at[side, at]))
                made.append(
                    (source.at[:, pl.ds(2 * shard, BIAS_ROWS), pl.ds(0, LANES)], bias.at[side, at])
                )
        return [pltpu.make_async_copy(a, b, sems.at[i]) for i, (a, b) in enumerate(made)]

    @pl.when(step == 0)
    def _():
        for copy in copies():
            copy.start()
        acc1[...] = jnp.zeros_like(acc1)
        acc2[...] = jnp.zeros_like(acc2)
        grad_dense_ref[...] = jnp.zeros_like(grad_dense_ref)
        small_ref[...] = jnp.zeros_like(small_ref)

    g1_row, g2_row = vector_row(g1_ref), vector_row(g2_ref)
    summed = product(ctx_ref[...], wd_ref[...]) + vector_row(bd_ref) + xs_ref[...].astype(F32)
    centred = summed - row_mean(summed)
    scale1 = lax.rsqrt(row_mean(centred * centred) + NORM_EPS)
    hat1 = centred * scale1
    normed1 = (hat1 * g1_row + vector_row(b1_ref)).astype(BF16)
    lane = lax.broadcasted_iota(jnp.int32, (SLOT, EXTRA), 1)
    ones = jnp.where(lane < 3, 1.0, 0.0).astype(BF16)
    for g in range(2):
        low1[g, :, :part] = normed1[:, g * part : (g + 1) * part]
        low1[g, :, part:] = ones
        first_t[g] = transposed(low1[g])[: first_t.shape[1], :]
        back[g] = jnp.zeros_like(back[g])

    @pl.when(step == 0)
    def _():
        for copy in copies():
            copy.wait()
        for side in range(2):
            for position in range(count):
                column = transposed(bias[side, position].astype(F32))
                column = jnp.concatenate(
                    [column, jnp.zeros((LANES, EXTRA - BIAS_ROWS), F32)], 1
                )
                w1[side, position, :, part:] = column[:shard].astype(BF16)

    for r in range(2):
        owner = group ^ r

        def up_chunk(c, carry, r=r, owner=owner):
            lanes = pl.ds(pl.multiple_of(c * wide, wide), wide)
            some = pl.ds(c * span, span)
            first = w1[r, some].reshape(wide, part + EXTRA)
            inner = right_product(low1[owner], first)
            cdf = 0.5 * (1.0 + lax.erf(inner * ROOT_HALF))
            pdf = jnp.exp(-0.5 * inner * inner) * DENSITY
            active = (inner * cdf).astype(BF16)
            act[r, :, lanes] = active
            slope[r, :, lanes] = (cdf + inner * pdf).astype(BF16)
            back[owner] += product(active, w2[r, some].reshape(wide, part))
            return carry

        lax.fori_loop(0, per, up_chunk, 0)

    partial = jnp.concatenate([back[g] for g in range(2)], 1).astype(BF16).astype(F32)
    summed2 = partial + vector_row(ob_ref) + normed1.astype(F32)
    centred2 = summed2 - row_mean(summed2)
    scale2 = lax.rsqrt(row_mean(centred2 * centred2) + NORM_EPS)
    hat2 = centred2 * scale2
    out_ref[...] = (hat2 * g2_row + vector_row(b2_ref)).astype(BF16)

    def put_rows(at, count, rows):
        for g in range(2):
            back[g, at : at + count, :] = rows[:, g * part : (g + 1) * part]

    rows_to_slot(up_ref, start, length, put_rows)
    upper = jnp.concatenate([back[g] for g in range(2)], 1)

    def add_small(index, block):
        total = column_sum(block)
        for g in range(2):
            row = 2 * index + g
            small_ref[row : row + 1, :] += total[:, g * half : (g + 1) * half]

    add_small(0, upper * hat2)
    add_small(1, upper)
    lifted = upper * g2_row
    total2 = scale2 * (lifted - row_mean(lifted) - hat2 * row_mean(lifted * hat2))
    add_small(2, total2)
    grad_low = total2.astype(BF16)
    for g in range(2):
        low2[g] = grad_low[:, g * part : (g + 1) * part]
        grad_t[g] = transposed(low2[g])
        back[g] = jnp.zeros_like(back[g])

    for r in range(2):
        owner = group ^ r

        def down_chunk(c, carry, r=r, owner=owner):
            lanes = pl.ds(pl.multiple_of(c * wide, wide), wide)
            some = pl.ds(c * span, span)
            grad_active = right_product(low2[owner], w2[r, some].reshape(wide, part))
            grad_inner = (grad_active * slope[r, :, lanes].astype(F32)).astype(BF16)
            acc2[r, :, lanes] += product(grad_t[owner], act[r, :, lanes])
            acc1[r, :, lanes] += product(first_t[owner], grad_inner)
            back[owner] += product(grad_inner, w1[r, some].reshape(wide, part + EXTRA)[:, :part])
            return carry

        lax.fori_loop(0, per, down_chunk, 0)

    grouped = jnp.concatenate([back[g] for g in range(2)], 1).astype(BF16).astype(F32)
    grad1 = grouped + total2
    add_small(3, grad1 * hat1)
    add_small(4, grad1)
    lifted = grad1 * g1_row
    mixed = scale1 * (lifted - row_mean(lifted) - hat1 * row_mean(lifted * hat1))
    gm_ref[...] = mixed
    mixed_low = mixed.astype(BF16)
    add_small(5, mixed_low.astype(F32))
    grad_dense_ref[...] += product(transposed(ctx_ref[...]), mixed_low)
    gctx_ref[...] = right_product(mixed_low, wd_ref[...]).astype(BF16)

    @pl.when(step == last)
    def _():
        for r, ref in enumerate((keep_ref, send_ref)):
            for c in range(per):
                lanes = slice(c * wide, (c + 1) * wide)
                some = slice(c * span, (c + 1) * span)
                turned = transposed(acc1[r, :part, lanes]).astype(BF16)
                ref[some, 0:shard, :] = turned.reshape(span, shard, part)
                turned = transposed(acc2[r, :, lanes]).astype(BF16)
                ref[some, shard : 2 * shard, :] = turned.reshape(span, shard, part)
            row = acc1[r, part : part + 8, :]
            row = jnp.concatenate([row, jnp.zeros((8, -row.shape[1] % LANES), F32)], 1) if row.shape[1] % LANES else row
            total = row.shape[1]
            for position in range(count):
                turned = pltpu.roll(row, (total - position * shard) % total, 1)
                ref[position, 2 * shard :, :] = turned[:, :part].astype(BF16)


def span_backward_kernel(
    info_ref, gctx_ref, xs_ref, query_ref, cs_ref, dw_ref, kc_ref, taps_ref, ws_ref, dense_ref,
    gs_ref, extra_ref, gk_ref, keep_ref, send_ref, small_ref,
    ch, th, acc, *, masks, chunk_rows,
):
    step = pl.program_id(0)
    last = pl.num_programs(0) - 1
    length = info_ref[step]
    width = xs_ref.shape[1]
    half = width // 2

    @pl.when(step == 0)
    def _():
        acc[...] = jnp.zeros_like(acc)
        small_ref[...] = jnp.zeros_like(small_ref)

    for halo in (ch, th):
        halo[0:HALO, :] = jnp.zeros((HALO, halo.shape[1]), F32)
        halo[HALO + SLOT :, :] = jnp.zeros((HALO, halo.shape[1]), F32)
    inside = lax.broadcasted_iota(jnp.int32, (SLOT, 1), 0) < length

    ch[HALO : HALO + SLOT, :] = cs_ref[...]
    grad_conv = gctx_ref[...].astype(F32)
    taps = taps_ref[...]
    table, picker = spread_table(half), gather_table(half)
    grad_taps = jnp.zeros((SLOT, LANES), F32)
    grad_source = jnp.zeros((SLOT, half), F32)
    for j in range(KERNEL):
        moved = grad_conv * ch[HALO - REACH + j : HALO - REACH + j + SLOT, :]
        high, low = high_low(moved)
        here = product(high, picker) + product(low, picker)
        grad_taps = grad_taps + (here if j == 0 else pltpu.roll(here, j * TAP_STRIDE, 1))
        th[HALO : HALO + SLOT, :] = product(tap_terms(taps, j), table) * grad_conv
        grad_source = grad_source + th[HALO + REACH - j : HALO + REACH - j + SLOT, :]
    grad_source = jnp.where(inside, grad_source, 0.0).astype(BF16)
    gs_ref[...] = grad_source
    small_ref[130:131, :] += column_sum(grad_source.astype(F32))

    query = query_ref[...].astype(F32)
    keyconv = kc_ref[...]
    grad_logits = taps * (grad_taps - tap_groups(taps * grad_taps, jnp.add))
    grad_logits = grad_logits.astype(BF16)
    small_ref[129:130, :LANES] += column_sum(grad_logits.astype(F32))
    span_in = (keyconv * query).astype(BF16)
    small_ref[0:LANES, :] += product(transposed(grad_logits), span_in)
    grad_span = right_product(grad_logits, ordered_span(ws_ref)).astype(BF16).astype(F32)
    extra_ref[...] = grad_span * keyconv
    grad_key = (grad_span * query).astype(BF16)
    gk_ref[...] = grad_key
    small_ref[128:129, :] += column_sum(grad_key.astype(F32))
    acc[:, 0:half] += product(transposed(dw_ref[...]), grad_key)
    acc[:, half:] += product(transposed(xs_ref[...]), grad_source)

    @pl.when(step == last)
    def _():
        sources = ((acc, chunk_rows, 2), (dense_ref, chunk_rows, 2))
        emit_chunks(sources, masks, my_place(info_ref), keep_ref, send_ref)


def depth_backward_kernel(info_ref, gk_ref, base_ref, xs_ref, dk_ref, wp_ref, in_ref, small_ref, gh):
    @pl.when(pl.program_id(0) == 0)
    def _():
        small_ref[...] = jnp.zeros_like(small_ref)

    half = xs_ref.shape[1]
    gh[0:HALO, :] = jnp.zeros((HALO, half), F32)
    gh[HALO + SLOT :, :] = jnp.zeros((HALO, half), F32)
    gh[HALO : HALO + SLOT, :] = right_product(gk_ref[...], wp_ref[...]).astype(BF16).astype(F32)
    for c in range(half // LANES):
        lanes = slice(c * LANES, (c + 1) * LANES)
        for part in range(2):
            rows = SLOT // 2
            base = HALO + REACH + part * rows
            inner = slice(part * rows, (part + 1) * rows)
            total = base_ref[inner, lanes]
            own = xs_ref[inner, lanes].astype(F32)
            for j in range(KERNEL):
                moved = gh[base - j : base - j + rows, lanes]
                total = total + dk_ref[j : j + 1, lanes] * moved
                small_ref[j : j + 1, lanes] += column_sum(moved * own)
            in_ref[inner, lanes] = total.astype(BF16)


def attend_backward_kernel(
    info_ref, gctx_ref, ctx_ref, xs_ref, qkv_ref, lse_ref, extra_ref, smallm_ref, smallc_ref,
    flat_ref, keep_ref, send_ref,
    gqt, acc, small_ref, *, masks, chunk_rows, small_rows,
):
    step = pl.program_id(0)
    last = pl.num_programs(0) - 1
    length = info_ref[step]
    width = xs_ref.shape[1]
    half = width // 2

    @pl.when(step == 0)
    def _():
        acc[...] = jnp.zeros_like(acc)
        small_ref[...] = jnp.zeros_like(small_ref)

    inside = lax.broadcasted_iota(jnp.int32, (SLOT, 1), 0) < length
    for pair in range(HEADS // 2):
        at = pair * LANES
        query_pair = qkv_ref[:, at : at + LANES]
        keys = qkv_ref[:, half + at : half + at + LANES]
        values = qkv_ref[:, 2 * half + at : 2 * half + at + LANES]
        keys_t = transposed(keys)
        grad_pair = gctx_ref[:, at : at + LANES]
        dots = transposed(grad_pair.astype(F32) * ctx_ref[:, at : at + LANES].astype(F32))
        grad_keys, grad_values = [], []
        for side in range(2):
            head = 2 * pair + side
            mask = pair_mask(side)
            rows = slice(side * HEAD_DIM, (side + 1) * HEAD_DIM)
            scores = right_product(
                jnp.where(mask, keys, jnp.zeros_like(keys)) * BF16(0.125), query_pair
            )
            scores = jnp.where(inside, scores, NEGATIVE)
            probs = jnp.exp(scores - lse_ref[head : head + 1, :])
            grad_probs = right_product(jnp.where(mask, values, jnp.zeros_like(values)), grad_pair)
            weighted = column_sum(dots[rows, :])
            grad_scores = (probs * (grad_probs - weighted)).astype(BF16)
            grad_keys.append(product(grad_scores, query_pair))
            grad_values.append(product(probs.astype(BF16), grad_pair))
            gqt[head * HEAD_DIM : (head + 1) * HEAD_DIM, :] = product(keys_t[rows, :], grad_scores)
        first = pair_mask(0)
        flat_ref[:, half + at : half + at + LANES] = (
            jnp.where(first, grad_keys[0], grad_keys[1]) * 0.125
        ).astype(BF16)
        flat_ref[:, 2 * half + at : 2 * half + at + LANES] = jnp.where(
            first, grad_values[0], grad_values[1]
        ).astype(BF16)
    flat_ref[:, :half] = (transposed(gqt[...]) * 0.125 + extra_ref[...]).astype(BF16)
    acc[...] += product(transposed(xs_ref[...]), flat_ref[...])
    for third in range(3):
        small_ref[OWN_ROW + third : OWN_ROW + third + 1, :] += column_sum(
            flat_ref[:, third * half : (third + 1) * half].astype(F32)
        )

    @pl.when(step == last)
    def _():
        small_ref[: smallm_ref.shape[0], :] = smallm_ref[...]
        small_ref[SPAN_ROW : SPAN_ROW + smallc_ref.shape[0], :] = smallc_ref[...]
        sources = ((acc, chunk_rows, 3), (small_ref, small_rows, 1))
        emit_chunks(sources, masks, my_place(info_ref), keep_ref, send_ref)


def input_kernel(info_ref, gm_ref, flat_ref, gs_ref, wq_ref, wk_ref, wv_ref, wc_ref, out_ref):
    half = gs_ref.shape[1]
    total = gm_ref[...] + right_product(gs_ref[...], wc_ref[...])
    for third, ref in enumerate((wq_ref, wk_ref, wv_ref)):
        total = total + right_product(flat_ref[:, third * half : (third + 1) * half], ref[...])
    out_ref[...] = total


def restore_kernel(info_ref, *refs, first_tile):
    out_ref = refs[-1]
    sources = refs[:-1] if first_tile == 0 else refs[:-2]
    tile = pl.program_id(0) + first_tile
    step, window = out_ref.shape[0], 256
    out_ref[...] = jnp.zeros_like(out_ref)
    for slot in range(sources[0].shape[0]):
        start, length = slot_bounds(info_ref, slot)
        first = tile * step - start

        @pl.when((first + step > 0) & (first < length))
        def _(slot=slot, first=first, length=length):
            base = jnp.clip(first // 16 * 16, 0, SLOT - window)
            base = pl.multiple_of(base, 16)
            row = lax.broadcasted_iota(jnp.int32, (step, window), 0)
            col = lax.broadcasted_iota(jnp.int32, (step, window), 1)
            pick = (col + base == row + first) & (row + first >= 0) & (row + first < length)
            pick = jnp.where(pick, 1.0, 0.0).astype(BF16)
            at = 0
            for ref in sources:
                wide = ref.shape[2]
                rows = product(pick, ref[slot, pl.ds(base, window), :])
                out_ref[:, at : at + wide] += rows.astype(BF16)
                at += wide


def assemble_kernel(info_ref, *refs, pieces, masks, layout):
    sources, outs = refs[: 2 * pieces], refs[2 * pieces :]
    group, own = my_place(info_ref)
    count = len(masks)
    blocks = count // pieces
    columns = sources[0].shape[2]
    for core in range(2):
        for position, mask in enumerate(masks):
            source = sources[core * pieces + position // blocks]
            index = (group ^ core) * count + (own ^ mask)
            chunk = source[position % blocks].astype(F32)
            at = 0
            for out, (rows, wide) in zip(outs, layout):
                for block in range(wide):
                    out[index, :, block * columns : (block + 1) * columns] = chunk[at : at + rows]
                    at += rows


def resident(shape):
    zeros = (0,) * len(shape)
    return pl.BlockSpec(tuple(shape), lambda *_: zeros, pipeline_mode=pl.Buffered(1))


def slot_block(columns, rows=SLOT, column=0):
    return pl.BlockSpec((None, rows, columns), lambda i: (i, 0, column))


SCALARS = pl.BlockSpec(memory_space=pltpu.SMEM)
ANYWHERE = pl.BlockSpec(memory_space=pl.ANY)
LIMIT = 60 * 1024 * 1024


def shape_of(*dims, dtype=F32):
    return jax.ShapeDtypeStruct(dims, dtype)


def cost(flops, nbytes):
    return pl.CostEstimate(flops=int(flops), bytes_accessed=int(nbytes), transcendentals=0)


PARAMS = pltpu.CompilerParams(vmem_limit_bytes=LIMIT)
LARGE = pltpu.CompilerParams(vmem_limit_bytes=LIMIT + 3 * 1024 * 1024)
RATE = 600e6


def busy(us):
    return cost(us * RATE, us * 1e6)


def run_project(info, slots, x, *rest):
    total, width = x.shape
    half = width // 2
    return pl.pallas_call(
        project_kernel,
        grid=(slots,),
        in_specs=[SCALARS] + [resident(a.shape) for a in (x,) + rest],
        out_specs=[slot_block(width), slot_block(3 * half), slot_block(half)],
        out_shape=[
            shape_of(slots, SLOT, width, dtype=BF16),
            shape_of(slots, SLOT, 3 * half, dtype=BF16),
            shape_of(slots, SLOT, half),
        ],
        compiler_params=PARAMS,
        cost_estimate=busy(10),
        name="project",
    )(info, x, *rest)


def run_convolve(info, xs, qkv, cs, *rest):
    slots, _, width = xs.shape
    half = width // 2
    return pl.pallas_call(
        convolve_kernel,
        grid=(slots,),
        in_specs=[SCALARS, slot_block(width), slot_block(half), slot_block(half)]
        + [resident(a.shape) for a in rest],
        out_specs=[slot_block(width), slot_block(half), slot_block(LANES), slot_block(half)],
        out_shape=[
            shape_of(slots, SLOT, width, dtype=BF16),
            shape_of(slots, SLOT, half),
            shape_of(slots, SLOT, LANES),
            shape_of(slots, SLOT, half, dtype=BF16),
        ],
        scratch_shapes=[
            pltpu.VMEM((SLOT + 2 * HALO, width), F32),
            pltpu.VMEM((SLOT + 2 * HALO, half), F32),
        ],
        compiler_params=PARAMS,
        cost_estimate=busy(15),
        name="convolve",
    )(info, xs, qkv, cs, *rest)


def run_attend(info, qkv, conv):
    slots, _, half = conv.shape
    return pl.pallas_call(
        attend_kernel,
        grid=(slots,),
        in_specs=[SCALARS, slot_block(3 * half), slot_block(half)],
        out_specs=[slot_block(2 * half), slot_block(SLOT, 8)],
        out_shape=[shape_of(slots, SLOT, 2 * half, dtype=BF16), shape_of(slots, 8, SLOT)],
        scratch_shapes=[pltpu.VMEM((half, SLOT), F32)],
        compiler_params=PARAMS,
        cost_estimate=busy(16),
        name="attend",
    )(info, qkv, conv)


def run_middle(info, ctx, xs, upstream, vectors, wd, weights, shard, count):
    slots, _, width = xs.shape
    half = width // 2
    hidden = count * shard
    pieces = len(weights) // 2
    bd, g1, b1, ob, g2, b2 = vectors
    rows = 2 * shard + BIAS_ROWS
    return pl.pallas_call(
        functools.partial(middle_kernel, pieces=pieces),
        grid=(slots,),
        in_specs=[SCALARS, slot_block(width), slot_block(width)]
        + [resident(a.shape) for a in (upstream, wd, bd, g1, b1, ob, g2, b2)]
        + [ANYWHERE] * len(weights),
        out_specs=[slot_block(width), slot_block(width), slot_block(width)]
        + [resident((count, rows, half))] * 2
        + [resident((width, width)), resident((16, half))],
        out_shape=[
            shape_of(slots, SLOT, width, dtype=BF16),
            shape_of(slots, SLOT, width),
            shape_of(slots, SLOT, width, dtype=BF16),
        ]
        + [shape_of(count, rows, half, dtype=BF16)] * 2
        + [shape_of(width, width), shape_of(16, half)],
        scratch_shapes=[
            pltpu.VMEM((2, count, shard, half + EXTRA), BF16),
            pltpu.VMEM((2, count, shard, half), BF16),
            pltpu.VMEM((2, count, BIAS_ROWS, LANES), BF16),
            pltpu.VMEM((2, SLOT, hidden), BF16),
            pltpu.VMEM((2, SLOT, hidden), BF16),
            pltpu.VMEM((2, SLOT, half + EXTRA), BF16),
            pltpu.VMEM((2, SLOT, half), BF16),
            pltpu.VMEM((2, half + 16, SLOT), BF16),
            pltpu.VMEM((2, half, SLOT), BF16),
            pltpu.VMEM((2, SLOT, half), F32),
            pltpu.VMEM((2, half + 16, hidden), F32),
            pltpu.VMEM((2, half, hidden), F32),
            pltpu.SemaphoreType.DMA((6 * pieces,)),
        ],
        compiler_params=LARGE,
        cost_estimate=busy(64),
        name="feed_forward",
    )(info, ctx, xs, upstream, wd, bd, g1, b1, ob, g2, b2, *weights)


def run_span_backward(info, gctx, xs, qkv, cs, dw, kc, taps, ws, dense, masks, chunk_rows):
    slots, _, width = xs.shape
    half = width // 2
    count = len(masks)
    return pl.pallas_call(
        functools.partial(span_backward_kernel, masks=masks, chunk_rows=chunk_rows),
        grid=(slots,),
        in_specs=[
            SCALARS, slot_block(half, column=1), slot_block(width), slot_block(half),
            slot_block(half), slot_block(width), slot_block(half), slot_block(LANES),
            resident(ws.shape), resident(dense.shape),
        ],
        out_specs=[slot_block(half)] * 3
        + [resident((count, 4 * chunk_rows, half))] * 2
        + [resident((136, half))],
        out_shape=[
            shape_of(slots, SLOT, half, dtype=BF16),
            shape_of(slots, SLOT, half),
            shape_of(slots, SLOT, half, dtype=BF16),
        ]
        + [shape_of(count, 4 * chunk_rows, half, dtype=BF16)] * 2
        + [shape_of(136, half)],
        scratch_shapes=[
            pltpu.VMEM((SLOT + 2 * HALO, half), F32),
            pltpu.VMEM((SLOT + 2 * HALO, half), F32),
            pltpu.VMEM((width, width), F32),
        ],
        compiler_params=PARAMS,
        cost_estimate=busy(23),
        name="span_backward",
    )(info, gctx, xs, qkv, cs, dw, kc, taps, ws, dense)


def run_depth_backward(info, gk, base, xs, dk, wp, side):
    slots, _, width = xs.shape
    half = width // 2
    return pl.pallas_call(
        depth_backward_kernel,
        grid=(slots,),
        in_specs=[
            SCALARS, slot_block(half), slot_block(half, column=side), slot_block(half, column=side),
            pl.BlockSpec((KERNEL, half), lambda i: (0, side)),
            pl.BlockSpec((half, half), lambda i: (side, 0)),
        ],
        out_specs=[slot_block(half), resident((16, half))],
        out_shape=[shape_of(slots, SLOT, half, dtype=BF16), shape_of(16, half)],
        scratch_shapes=[pltpu.VMEM((SLOT + 2 * HALO, half), F32)],
        compiler_params=PARAMS,
        cost_estimate=busy(10),
        name="depth_backward",
    )(info, gk, base, xs, dk, wp)


def run_attend_backward(info, gctx, ctx, xs, qkv, lse, extra, smalls, masks, chunk_rows):
    slots, _, width = xs.shape
    half = width // 2
    count = len(masks)
    small_rows = small_chunk(count)
    rows = 3 * chunk_rows + small_rows
    return pl.pallas_call(
        functools.partial(
            attend_backward_kernel, masks=masks, chunk_rows=chunk_rows, small_rows=small_rows
        ),
        grid=(slots,),
        in_specs=[
            SCALARS, slot_block(half), slot_block(half), slot_block(width), slot_block(3 * half),
            slot_block(SLOT, 8), slot_block(half),
        ]
        + [resident(a.shape) for a in smalls],
        out_specs=[slot_block(3 * half)] + [resident((count, rows, half))] * 2,
        out_shape=[shape_of(slots, SLOT, 3 * half, dtype=BF16)]
        + [shape_of(count, rows, half, dtype=BF16)] * 2,
        scratch_shapes=[
            pltpu.VMEM((half, SLOT), F32),
            pltpu.VMEM((width, 3 * half), F32),
            pltpu.VMEM((SMALL_ROWS, half), F32),
        ],
        compiler_params=PARAMS,
        cost_estimate=busy(21),
        name="attend_backward",
    )(info, gctx, ctx, xs, qkv, lse, extra, *smalls)


def run_input(info, gm, flat, gs, *weights):
    slots, _, width = gm.shape
    return pl.pallas_call(
        input_kernel,
        grid=(slots,),
        in_specs=[SCALARS, slot_block(width), slot_block(flat.shape[2]), slot_block(gs.shape[2])]
        + [resident(w.shape) for w in weights],
        out_specs=slot_block(width),
        out_shape=shape_of(slots, SLOT, width),
        compiler_params=PARAMS,
        cost_estimate=busy(9),
        name="input_gradient",
    )(info, gm, flat, gs, *weights)


def run_restore(info, sources, total, before=None):
    width = sum(s.shape[2] for s in sources)
    tile = 128
    tiles = total // tile // 2
    first_tile = 0 if before is None else tiles
    more = [] if before is None else [before]
    return pl.pallas_call(
        functools.partial(restore_kernel, first_tile=first_tile),
        grid=(tiles,),
        in_specs=[SCALARS] + [resident(s.shape) for s in sources] + [ANYWHERE] * len(more),
        out_specs=pl.BlockSpec((tile, width), lambda i: (i + first_tile, 0)),
        out_shape=shape_of(total, width, dtype=BF16),
        input_output_aliases={1 + len(sources): 0} if more else {},
        compiler_params=PARAMS,
        cost_estimate=busy(4),
        name="restore_rows",
    )(info, *sources, *more)


def run_assemble(info, sources, masks, layout):
    pieces = len(sources) // 2
    half = sources[0].shape[2]
    chunks = 2 * len(masks)
    shapes = [(chunks, rows, wide * half) for rows, wide in layout]
    outs = pl.pallas_call(
        functools.partial(assemble_kernel, pieces=pieces, masks=masks, layout=layout),
        in_specs=[SCALARS] + [pl.BlockSpec(memory_space=pltpu.VMEM)] * len(sources),
        out_specs=[pl.BlockSpec(memory_space=pltpu.VMEM)] * len(shapes),
        out_shape=[shape_of(*s) for s in shapes],
        compiler_params=PARAMS,
        cost_estimate=busy(3),
        name="assemble",
    )(info, *sources)
    return [o.reshape(chunks * o.shape[1], -1) for o in outs]


def small_chunk(count):
    return round_up(-(-SMALL_ROWS // (2 * count)), 8)


def swap_groups(block):
    return lax.ppermute(block, "grp", [(0, 1), (1, 0)])


def send_across(block, count, offset):
    return lax.ppermute(block, "dp", [(i, i ^ offset) for i in range(count)])


def tree_sum(parts):
    parts = [p.astype(F32) for p in parts]
    while len(parts) > 1:
        parts = [parts[i] + parts[i + 1] for i in range(0, len(parts), 2)]
    return parts[0].astype(BF16)


def tie(value, *others):
    return lax.optimization_barrier((value, others))[0]


def advance(done, *sums):
    held = lax.optimization_barrier((done, [s.current for s in sums]))[1]
    sent = []
    for one, current in zip(sums, held):
        one.current = current
        sent += one.step()
    return sent


class ChunkSum:
    def __init__(self, keep, send, count, gather):
        self.count, self.digits, self.gather = count, digits_of(count), gather
        self.current, self.stage = [keep, swap_groups(send)], 0
        self.result = None

    def offsets(self, stage):
        stride, radix = self.digits[stage]
        return [s * stride for s in range(1, radix)]

    def step(self):
        last = len(self.digits)
        if self.stage < last:
            radix = self.digits[self.stage][1]
            size = self.current[0].shape[0] // radix
            parts = [
                tree_sum([p[s * size : (s + 1) * size] for p in self.current]) for s in range(radix)
            ]
            offsets = self.offsets(self.stage)
            self.current = [parts[0]] + [
                send_across(p, self.count, o) for p, o in zip(parts[1:], offsets)
            ]
            sent = parts
        elif self.stage == last:
            own = tree_sum(self.current)
            self.result = own
            sent = [own]
            if self.gather:
                self.spread(own, last - 1)
        elif self.stage < 2 * last:
            own = jnp.concatenate(self.current, 0)
            sent = [own]
            self.spread(own, 2 * last - 1 - self.stage)
        else:
            own = jnp.concatenate(self.current, 0)
            sent = [own]
            self.result = [own, swap_groups(own)]
        self.stage += 1
        return sent

    def spread(self, own, stage):
        self.current = [own] + [send_across(own, self.count, o) for o in self.offsets(stage)]

    def finish(self):
        while self.stage <= (2 if self.gather else 1) * len(self.digits):
            self.step()
        return self.result


class SmallSum:
    def __init__(self, block, count):
        self.count, self.digits, self.stage = count, digits_of(count), 0
        self.current = [block, swap_groups(block)]

    def step(self):
        block = tree_sum(self.current)
        stride, radix = self.digits[self.stage]
        self.current = [block] + [
            send_across(block, self.count, s * stride) for s in range(1, radix)
        ]
        self.stage += 1
        return [block]

    def finish(self):
        while self.stage < len(self.digits):
            self.step()
        return tree_sum(self.current)


def round_up(value, unit):
    return -(-value // unit) * unit


def weight_shard(inter_weight, inter_bias, down_weight):
    columns = inter_weight.shape[2]
    shard = round_up(columns, 16)
    half = down_weight.shape[2]
    pad = ((0, shard - columns), (0, 0))
    first = jnp.pad(jnp.transpose(inter_weight[0]), pad)
    second = jnp.pad(down_weight[0], pad)
    rest, terms = inter_bias, []
    for _ in range(3):
        term = lax.reduce_precision(rest, 8, 7)
        terms.append(term)
        rest = rest - term
    terms = jnp.concatenate(terms, 0).astype(BF16)
    terms = jnp.pad(terms, ((0, BIAS_ROWS - 3), (0, half - columns)))
    return jnp.concatenate([first, second, terms], 0)[None], shard


def from_tap_rows(block):
    shaped = block.reshape(LANES // TAP_STRIDE, TAP_STRIDE, -1)[:KERNEL, :HEADS]
    return jnp.swapaxes(shaped, 0, 1).reshape(HEADS * KERNEL, -1)


def on_device(
    count, layer_input, lengths, query_weight, query_bias, key_weight, value_weight, value_bias,
    depth_kernel, point_weight, point_bias, span_weight, span_bias, conv_out_weight,
    conv_out_bias, dense_weight, dense_bias, first_gain, first_shift, inter_weight, inter_bias,
    grouped_down_weight, output_bias, second_gain, second_shift, upstream_grad,
):
    total, width = layer_input.shape
    half = width // 2
    slots = lengths.shape[1]
    masks = offset_masks(count)
    chunk_rows = round_up(-(-width // (2 * count)), 8)
    info = jnp.concatenate(
        [
            lengths[0],
            jnp.zeros((1,), jnp.int32),
            lax.axis_index("grp").astype(jnp.int32).reshape(1),
            lax.axis_index("dp").astype(jnp.int32).reshape(1),
        ]
    )
    own_weights, shard = weight_shard(inter_weight, inter_bias, grouped_down_weight)
    digits = digits_of(count)
    block = own_weights
    for stride, radix in reversed(digits[1:]):
        block = [block] + [send_across(block, count, s * stride) for s in range(1, radix)]
        if stride == digits[1][0]:
            break
        block = jnp.concatenate(block, 0)

    xs, qkv, cs = run_project(
        info, slots, tie(layer_input, own_weights), query_weight, key_weight, value_weight,
        conv_out_weight, query_bias, value_bias, conv_out_bias,
    )
    block = jnp.concatenate(tie(block, xs), 0)
    stride, radix = digits[0]
    block = [block] + [send_across(block, count, s * stride) for s in range(1, radix)]
    dw, kc, taps, conv = run_convolve(
        info, tie(xs, block[0]), qkv, cs, depth_kernel, point_weight, point_bias, span_weight, span_bias
    )
    ctx, lse = run_attend(info, qkv, conv)
    block = tie(block, ctx)
    weights = block + [swap_groups(b) for b in block]
    vectors = (dense_bias, first_gain, first_shift, output_bias, second_gain, second_shift)
    out_slots, gm, gctx, keep, send, dense, small_m = run_middle(
        info, ctx, xs, upstream_grad, vectors, dense_weight, weights, shard, count
    )
    ffn_sum = ChunkSum(keep, send, count, False)
    first_rows = run_restore(info, [tie(out_slots, send)], total)
    sent = advance(first_rows, ffn_sum)
    gs, extra, gk, keep_c, send_c, small_c = run_span_backward(
        info, tie(gctx, sent), xs, qkv, cs, dw, kc, taps, span_weight, dense, masks, chunk_rows
    )
    span_sum = ChunkSum(keep_c, send_c, count, True)
    layer_out = run_restore(info, [tie(out_slots, send_c)], total, first_rows)
    sent = advance(layer_out, span_sum)
    flat, keep_a, send_a = run_attend_backward(
        info, tie(gctx, sent), ctx, xs, qkv, lse, extra, [small_m, small_c], masks, chunk_rows
    )
    mixer_sum = ChunkSum(keep_a, send_a, count, True)
    sent = advance(flat, ffn_sum, span_sum)
    base = run_input(
        info, tie(gm, sent, send_a), flat, gs, query_weight, key_weight, value_weight, conv_out_weight
    )
    sent = advance(base, mixer_sum, span_sum)
    in_first, small_first = run_depth_backward(
        info, gk, tie(base, sent), xs, depth_kernel, point_weight, 0
    )
    sent = advance(in_first, mixer_sum, span_sum)
    in_second, small_second = run_depth_backward(
        info, gk, tie(base, sent), xs, depth_kernel, point_weight, 1
    )
    taps_sum = SmallSum(jnp.concatenate([small_first, small_second], 0).astype(BF16), count)
    sent = advance(in_second, mixer_sum, ffn_sum)
    in_rows = run_restore(info, [in_first, tie(in_second, sent)], total)
    sent = advance(in_rows, mixer_sum, span_sum, taps_sum)
    in_grad = run_restore(info, [in_first, tie(in_second, sent)], total, in_rows)
    sent = advance(in_grad, mixer_sum, taps_sum)

    rows = chunk_rows
    grad_point_conv, grad_dense = run_assemble(
        info, tie(span_sum.finish(), sent), masks, ((rows, 2), (rows, 2))
    )
    grad_query, grad_key, grad_value, small = run_assemble(
        info, mixer_sum.finish(), masks, ((rows, 1),) * 3 + ((small_chunk(count), 1),)
    )
    grad_query, grad_key, grad_value = [g[:width] for g in (grad_query, grad_key, grad_value)]
    grad_point_conv, grad_dense = grad_point_conv[:width], grad_dense[:width]
    grad_point, grad_conv = grad_point_conv[:, :half], grad_point_conv[:, half:]
    small_d = taps_sum.finish().astype(F32)
    ffn = ffn_sum.finish().astype(F32)
    pair = lambda i: small[2 * i : 2 * i + 2].reshape(width)
    small_c, small_a = small[SPAN_ROW:], small[OWN_ROW:]
    columns = inter_weight.shape[2]
    return (
        layer_out,
        in_grad,
        grad_query,
        small_a[0],
        grad_key,
        grad_value,
        small_a[2],
        jnp.concatenate([small_d[:KERNEL], small_d[16 : 16 + KERNEL]], 1),
        grad_point,
        small_c[128],
        jnp.transpose(from_tap_rows(small_c[:LANES])),
        from_tap_rows(small_c[129, :LANES][:, None])[:, 0],
        grad_conv,
        small_c[130],
        grad_dense,
        pair(5),
        pair(3),
        pair(4),
        jnp.transpose(ffn[:, :columns], (0, 2, 1)),
        ffn[:, 2 * shard, :columns],
        ffn[:, shard : shard + columns],
        pair(2),
        pair(0),
        pair(1),
    )


def solution(mesh):
    rows = P(("grp", "dp"), None)
    one = P()
    return jax.shard_map(
        functools.partial(on_device, mesh.shape["dp"]),
        mesh=mesh,
        in_specs=(rows, rows) + (one,) * 16
        + (P("grp", None, "dp"), P("grp", "dp"), P("grp", "dp", None)) + (one,) * 3 + (rows,),
        out_specs=(rows, rows) + (one,) * 16
        + (P("grp", None, "dp"), P("grp", "dp"), P("grp", "dp", None)) + (one,) * 3,
        check_vma=False,
    )
```

```python
import functools

import jax
import jax.numpy as jnp
from jax import lax
from jax.experimental import pallas as pl
from jax.experimental.pallas import tpu as pltpu
from jax.sharding import PartitionSpec as P

HEADS = 6
HEAD_DIM = 64
KERNEL = 9
REACH = KERNEL // 2
SLOT = 512
SLOTS = 3
GROUP = 8
SPAN = SLOT // GROUP
EDGE = REACH * GROUP
LANES = 128
TAP_STRIDE = 8
CHUNK_ROWS = 1536
EXTRA = 128
ROWS = 128
SPAN_ROW = 16
TAPS_ROW = 80
OWN_ROW = 152
SMALL_ROWS = 160
BIAS_ROWS = 8
RADIX = 4
NEGATIVE = -1e30
NORM_EPS = 1e-12
ROOT_HALF = 0.7071067811865476
DENSITY = 0.3989422804014327
BF16 = jnp.bfloat16
F32 = jnp.float32


def product(left, right):
    return jnp.dot(left, right, preferred_element_type=F32)


def right_product(left, right):
    return lax.dot_general(left, right, (((1,), (1,)), ((), ())), preferred_element_type=F32)


def transposed(block):
    return jnp.transpose(block, (1, 0))


def column_sum(block):
    return jnp.sum(block, axis=0, keepdims=True)


def row_mean(block):
    return jnp.mean(block, axis=-1, keepdims=True)


def tap_groups(block, combine):
    step = TAP_STRIDE
    while step < LANES:
        block = combine(block, pltpu.roll(block, step, 1))
        step *= 2
    return block


def high_low(block):
    high = block.astype(BF16)
    low = (block - high.astype(F32)).astype(BF16)
    return high, low


HEAD = 2


def slot_bounds(info_ref, index):
    start = jnp.int32(0)
    for other in range(SLOTS - 1):
        start = start + jnp.where(index > other, info_ref[HEAD + other], 0)
    return start, info_ref[HEAD + index]


def my_place(info_ref):
    return info_ref[0], info_ref[1]


def mask_at(info_ref, position):
    return info_ref[HEAD + SLOTS + position]


def slot_times(first, count):
    row = lax.broadcasted_iota(jnp.int32, (count, 1), 0) + first
    return (row & (GROUP - 1)) * SPAN + row // GROUP


def rows_to_slot(source_ref, start, length):
    total = source_ref.shape[0]
    window = SLOT + 16
    base = pl.multiple_of(jnp.minimum(start // 16 * 16, total - window), 16)
    source = source_ref[pl.ds(base, window), :]
    col = lax.broadcasted_iota(jnp.int32, (1, window), 1) + (base - start)
    time = slot_times(0, SLOT)
    time = jnp.where(time < length, time, -SLOT * SLOT)
    pick = jnp.where(col == time, 1.0, 0.0).astype(BF16)
    return product(pick, source)


def slot_to_rows(target_ref, start, length, block):
    total = target_ref.shape[0]
    window = SLOT + 16
    base = pl.multiple_of(jnp.minimum(start // 16 * 16, total - window), 16)
    col = lax.broadcasted_iota(jnp.int32, (1, SLOT), 1)
    time = lax.broadcasted_iota(jnp.int32, (window, 1), 0) + (base - start)
    row = (time & (SPAN - 1)) * GROUP + (time // SPAN)
    row = jnp.where((time >= 0) & (time < length), row, -1)
    pick = jnp.where(col == row, 1.0, 0.0).astype(BF16)
    target_ref[pl.ds(base, window), :] += product(pick, block).astype(BF16)


def put_with_edges(ref, block):
    ref[EDGE : EDGE + SLOT, :] = block
    sub = lax.broadcasted_iota(jnp.int32, (GROUP, 1), 0)
    for k in range(REACH):
        before = block[SLOT - EDGE + k * GROUP : SLOT - EDGE + (k + 1) * GROUP, :]
        before = jnp.where(sub == 0, 0.0, pltpu.roll(before, 1, 0))
        ref[k * GROUP : (k + 1) * GROUP, :] = before
        after = block[k * GROUP : (k + 1) * GROUP, :]
        after = jnp.where(sub == GROUP - 1, 0.0, pltpu.roll(after, GROUP - 1, 0))
        ref[EDGE + SLOT + k * GROUP : EDGE + SLOT + (k + 1) * GROUP, :] = after


def shifted_rows(offset, first=0, count=SLOT):
    at = EDGE + offset * GROUP + first
    return slice(at, at + count)


def pair_mask(half):
    lane = lax.broadcasted_iota(jnp.int32, (1, LANES), 1)
    return (lane // HEAD_DIM) == half


def digits_of(count, wide=64):
    digits, stride = [], 1
    while stride < count:
        radix = RADIX if (count // stride) % RADIX == 0 and stride < wide else 2
        digits.append((stride, radix))
        stride *= radix
    return digits


def offset_masks(digits):
    masks = [0]
    for stride, radix in reversed(digits):
        masks = [digit * stride ^ mask for digit in range(radix) for mask in masks]
    return masks


def vector_row(ref):
    return ref[...].reshape(1, ref.shape[0])


def tap_order():
    row = lax.broadcasted_iota(jnp.int32, (HEADS * KERNEL, LANES), 0)
    lane = lax.broadcasted_iota(jnp.int32, (HEADS * KERNEL, LANES), 1)
    tap, head = lane // TAP_STRIDE, lane % TAP_STRIDE
    return (row == head * KERNEL + tap) & (head < HEADS) & (tap < KERNEL)


def ordered_span(ws_ref):
    return product(ws_ref[...], jnp.where(tap_order(), 1.0, 0.0).astype(BF16)).astype(BF16)


def spread_table(half):
    lane = lax.broadcasted_iota(jnp.int32, (2 * LANES, half), 0) % LANES
    head = lax.broadcasted_iota(jnp.int32, (2 * LANES, half), 1) // HEAD_DIM
    return jnp.where(lane == head, 1.0, 0.0).astype(BF16)


def gather_table(half):
    head = lax.broadcasted_iota(jnp.int32, (half, LANES), 0) // HEAD_DIM
    lane = lax.broadcasted_iota(jnp.int32, (half, LANES), 1)
    return jnp.where(lane == head, 1.0, 0.0).astype(BF16)


def tap_terms(taps, j):
    moved = taps if j == 0 else pltpu.roll(taps, LANES - j * TAP_STRIDE, 1)
    return jnp.concatenate(high_low(moved), 1)


def project_kernel(
    info_ref, x_ref, wq_ref, wk_ref, wv_ref, wc_ref, bq_ref, bv_ref, bc_ref, xs_ref, qkv_ref, cs_ref
):
    half = wq_ref.shape[1]
    start, length = slot_bounds(info_ref, pl.program_id(0))
    xs_ref[...] = rows_to_slot(x_ref, start, length).astype(BF16)
    inside = slot_times(0, SLOT) < length
    rows = xs_ref[...]
    qkv_ref[:, :half] = (product(rows, wq_ref[...]) + vector_row(bq_ref)).astype(BF16)
    qkv_ref[:, half : 2 * half] = product(rows, wk_ref[...]).astype(BF16)
    qkv_ref[:, 2 * half :] = (product(rows, wv_ref[...]) + vector_row(bv_ref)).astype(BF16)
    source = product(rows, wc_ref[...]) + vector_row(bc_ref)
    cs_ref[...] = jnp.where(inside, source, 0.0).astype(BF16)


def convolve_kernel(
    info_ref, xs_ref, query_ref, cs_ref, dk_ref, wp_ref, bp_ref, ws_ref, bs_ref,
    dw_ref, kc_ref, taps_ref, conv_ref,
    xh, ch,
):
    width = xs_ref.shape[1]
    half = width // 2
    put_with_edges(xh, xs_ref[...].astype(F32))
    put_with_edges(ch, cs_ref[...].astype(F32))

    def depth_chunk(c, carry):
        lanes = pl.ds(pl.multiple_of(c * LANES, LANES), LANES)
        for first in range(0, SLOT, ROWS):
            total = jnp.zeros((ROWS, LANES), F32)
            for j in range(KERNEL):
                total = total + dk_ref[j : j + 1, lanes] * xh[shifted_rows(j - REACH, first, ROWS), lanes]
            dw_ref[first : first + ROWS, lanes] = total.astype(BF16)
        return carry

    lax.fori_loop(0, width // LANES, depth_chunk, 0)
    keyconv = product(dw_ref[...], wp_ref[...]) + vector_row(bp_ref)
    kc_ref[...] = keyconv.astype(BF16)
    span_in = (keyconv * query_ref[...].astype(F32)).astype(BF16)
    wide = jnp.broadcast_to(vector_row(bs_ref), (8, HEADS * KERNEL))
    order = jnp.where(tap_order(), 1.0, 0.0)
    shift = jnp.dot(wide, order, precision=lax.Precision.HIGHEST, preferred_element_type=F32)[0:1]
    lane = lax.broadcasted_iota(jnp.int32, (1, LANES), 1)
    used = (lane // TAP_STRIDE < KERNEL) & (lane % TAP_STRIDE < HEADS)
    shift = jnp.where(used, shift, NEGATIVE)
    logits = product(span_in, ordered_span(ws_ref)) + shift
    weights = jnp.exp(logits - tap_groups(logits, jnp.maximum))
    taps = weights / tap_groups(weights, jnp.add)
    taps_ref[...] = taps
    table = spread_table(half)
    total = jnp.zeros((SLOT, half), F32)
    for j in range(KERNEL):
        spread = product(tap_terms(taps, j), table)
        total = total + spread * ch[shifted_rows(j - REACH), :]
    conv_ref[...] = total.astype(BF16)


def head_scores(keys, query, side, outside):
    lane = lax.broadcasted_iota(jnp.int32, (1, LANES), 1)
    spare = lane == (1 - side) * HEAD_DIM
    rest = jnp.where(spare, outside, jnp.zeros_like(keys))
    keys = jnp.where(pair_mask(side), keys * BF16(0.125), rest)
    query = jnp.where(spare, jnp.ones_like(query), query)
    return right_product(keys, query)


def dead_rows(length):
    return jnp.where(slot_times(0, SLOT) < length, 0.0, NEGATIVE).astype(BF16)


def attend_kernel(info_ref, qkv_ref, conv_ref, ctx_ref, lse_ref, att):
    half = conv_ref.shape[1]
    outside = dead_rows(info_ref[HEAD + pl.program_id(0)])
    ones = jnp.ones((16, SLOT), BF16)

    def one_pair(pair, carry):
        at = pl.multiple_of(pair * LANES, LANES)
        query = qkv_ref[:, pl.ds(at, LANES)]
        keys = qkv_ref[:, pl.ds(half + at, LANES)]
        values = transposed(qkv_ref[:, pl.ds(2 * half + at, LANES)])
        for side in range(2):
            scores = head_scores(keys, query, side, outside)
            highest = jnp.max(scores, axis=0, keepdims=True)
            weights = jnp.exp(scores - highest).astype(BF16)
            mine = jnp.concatenate([values[side * HEAD_DIM : (side + 1) * HEAD_DIM, :], ones], 0)
            both = product(mine, weights)
            summed = both[HEAD_DIM : HEAD_DIM + 1, :]
            att[pl.ds(pl.multiple_of(at + side * HEAD_DIM, HEAD_DIM), HEAD_DIM), :] = (
                both[:HEAD_DIM, :] * (1.0 / summed)
            )
            lse_ref[pl.ds(2 * pair + side, 1), :] = highest + jnp.log(summed)
        return carry

    lax.fori_loop(0, HEADS // 2, one_pair, 0)
    ctx_ref[:, :half] = transposed(att[...]).astype(BF16)
    ctx_ref[:, half:] = conv_ref[...]


def emit_chunks(sources, info_ref, keep_ref, send_ref):
    group, own = my_place(info_ref)
    count, columns = keep_ref.shape[0], keep_ref.shape[2]

    def one(position, carry):
        other = own ^ mask_at(info_ref, position)
        for ref, side in ((keep_ref, group), (send_ref, 1 - group)):
            pieces = []
            for source, rows, blocks in sources:
                first = jnp.minimum((side * count + other) * rows, source.shape[0] - rows)
                piece = source[pl.ds(pl.multiple_of(first, 8), rows), :]
                pieces += [piece[:, b * columns : (b + 1) * columns] for b in range(blocks)]
            ref[position] = jnp.concatenate(pieces, 0).astype(BF16)
        return carry

    lax.fori_loop(0, count, one, 0)


def middle_kernel(
    info_ref, ctx_ref, xs_ref, up_ref, wd_ref, bd_ref, g1_ref, b1_ref,
    ob_ref, g2_ref, b2_ref, *rest, pieces, order,
):
    weight_refs, rest = rest[: 2 * pieces], rest[2 * pieces :]
    (
        out_ref, gm_ref, gctx_ref, keep_ref, send_ref, grad_dense_ref, small_ref,
        w1, w2, bias, act, slope, low1, low2, first_t, grad_t, back, acc1, acc2, sems,
    ) = rest
    step = pl.program_id(0)
    last = pl.num_programs(0) - 1
    start, length = slot_bounds(info_ref, step)
    group = my_place(info_ref)[0]
    count, shard, part = w2.shape[1:]
    blocks = count // pieces
    span = count
    while span * shard > CHUNK_ROWS:
        span //= 2
    per = count // span
    wide = span * shard
    half = part
    width = 2 * half

    def copies():
        made = []
        for side in range(2):
            for piece in range(pieces):
                source = weight_refs[side * pieces + piece]
                at = pl.ds(piece * blocks, blocks)
                made.append((source.at[:, pl.ds(0, shard), :], w1.at[side, at, :, pl.ds(0, part)]))
                made.append((source.at[:, pl.ds(shard, shard), :], w2.at[side, at]))
                made.append(
                    (source.at[:, pl.ds(2 * shard, BIAS_ROWS), pl.ds(0, LANES)], bias.at[side, at])
                )
        return [pltpu.make_async_copy(a, b, sems.at[i]) for i, (a, b) in enumerate(made)]

    @pl.when(step == 0)
    def _():
        for copy in copies():
            copy.start()
        acc1[...] = jnp.zeros_like(acc1)
        acc2[...] = jnp.zeros_like(acc2)
        grad_dense_ref[...] = jnp.zeros_like(grad_dense_ref)
        small_ref[...] = jnp.zeros_like(small_ref)

    g1_row, g2_row = vector_row(g1_ref), vector_row(g2_ref)
    summed = product(ctx_ref[...], wd_ref[...]) + vector_row(bd_ref) + xs_ref[...].astype(F32)
    centred = summed - row_mean(summed)
    scale1 = lax.rsqrt(row_mean(centred * centred) + NORM_EPS)
    hat1 = centred * scale1
    normed1 = (hat1 * g1_row + vector_row(b1_ref)).astype(BF16)
    lane = lax.broadcasted_iota(jnp.int32, (SLOT, EXTRA), 1)
    ones = jnp.where(lane < 3, 1.0, 0.0).astype(BF16)
    for g in range(2):
        low1[g, :, :part] = normed1[:, g * part : (g + 1) * part]
        low1[g, :, part:] = ones
        first_t[g] = transposed(low1[g])[: first_t.shape[1], :]
        back[g] = jnp.zeros_like(back[g])

    @pl.when(step == 0)
    def _():
        for copy in copies():
            copy.wait()
        for side in range(2):
            for position in range(count):
                column = transposed(bias[side, position].astype(F32))
                column = jnp.concatenate(
                    [column, jnp.zeros((LANES, EXTRA - BIAS_ROWS), F32)], 1
                )
                w1[side, position, :, part:] = column[:shard].astype(BF16)

    def up_chunk(item, carry):
        r, c = item // per, item % per
        owner = group ^ r
        lanes = pl.ds(pl.multiple_of(c * wide, LANES), wide)
        some = pl.ds(c * span, span)
        first = w1[r, some].reshape(wide, part + EXTRA)
        inner = right_product(low1[owner], first)
        cdf = 0.5 * (1.0 + lax.erf(inner * ROOT_HALF))
        pdf = jnp.exp(-0.5 * inner * inner) * DENSITY
        active = (inner * cdf).astype(BF16)
        act[r, :, lanes] = active
        slope[r, :, lanes] = (cdf + inner * pdf).astype(BF16)
        back[owner] += product(active, w2[r, some].reshape(wide, part))
        return carry

    lax.fori_loop(0, 2 * per, up_chunk, 0)

    partial = jnp.concatenate([back[g] for g in range(2)], 1).astype(BF16).astype(F32)
    summed2 = partial + vector_row(ob_ref) + normed1.astype(F32)
    centred2 = summed2 - row_mean(summed2)
    scale2 = lax.rsqrt(row_mean(centred2 * centred2) + NORM_EPS)
    hat2 = centred2 * scale2
    out_ref[...] = (hat2 * g2_row + vector_row(b2_ref)).astype(BF16)

    upper = rows_to_slot(up_ref, start, length)

    def add_small(index, block):
        total = column_sum(block)
        for g in range(2):
            row = 2 * index + g
            small_ref[row : row + 1, :] += total[:, g * half : (g + 1) * half]

    add_small(0, upper * hat2)
    add_small(1, upper)
    lifted = upper * g2_row
    total2 = scale2 * (lifted - row_mean(lifted) - hat2 * row_mean(lifted * hat2))
    add_small(2, total2)
    grad_low = total2.astype(BF16)
    for g in range(2):
        low2[g] = grad_low[:, g * part : (g + 1) * part]
        grad_t[g] = transposed(low2[g])
        back[g] = jnp.zeros_like(back[g])

    def down_chunk(item, carry):
        r, c = item // per, item % per
        owner = group ^ r
        lanes = pl.ds(pl.multiple_of(c * wide, LANES), wide)
        some = pl.ds(c * span, span)
        grad_active = right_product(low2[owner], w2[r, some].reshape(wide, part))
        grad_inner = (grad_active * slope[r, :, lanes].astype(F32)).astype(BF16)
        acc2[r, :, lanes] += product(grad_t[owner], act[r, :, lanes])
        acc1[r, :, lanes] += product(first_t[owner], grad_inner)
        back[owner] += product(grad_inner, w1[r, some].reshape(wide, part + EXTRA)[:, :part])
        return carry

    lax.fori_loop(0, 2 * per, down_chunk, 0)

    grouped = jnp.concatenate([back[g] for g in range(2)], 1).astype(BF16).astype(F32)
    grad1 = grouped + total2
    add_small(3, grad1 * hat1)
    add_small(4, grad1)
    lifted = grad1 * g1_row
    mixed = scale1 * (lifted - row_mean(lifted) - hat1 * row_mean(lifted * hat1))
    mixed_low = mixed.astype(BF16)
    gm_ref[...] = mixed_low
    add_small(5, mixed_low.astype(F32))
    grad_dense_ref[...] += product(transposed(ctx_ref[...]), mixed_low)
    gctx_ref[...] = right_product(mixed_low, wd_ref[...]).astype(BF16)

    @pl.when(step == last)
    def _():
        for r, ref in enumerate((keep_ref, send_ref)):
            for c in range(per):
                lanes = slice(c * wide, (c + 1) * wide)
                first = transposed(acc1[r, :part, lanes]).astype(BF16)
                second = transposed(acc2[r, :, lanes]).astype(BF16)
                for p in range(span):
                    rows = slice(p * shard, (p + 1) * shard)
                    ref[order[c * span + p], 0:shard, :] = first[rows]
                    ref[order[c * span + p], shard : 2 * shard, :] = second[rows]
            row = acc1[r, part : part + 8, :]
            total = row.shape[1]
            for p in range(count):
                turned = pltpu.roll(row, (total - p * shard) % total, 1)
                ref[order[p], 2 * shard :, :] = turned[:, :part].astype(BF16)


def span_backward_kernel(
    info_ref, gctx_ref, xs_ref, query_ref, cs_ref, dw_ref, kc_ref, taps_ref, ws_ref, wp_ref, dense_ref,
    gs_ref, extra_ref, gk_ref, keep_ref, send_ref, small_ref,
    ch, gh, th, xh, sums, acc, *, chunk_rows,
):
    step = pl.program_id(0)
    last = pl.num_programs(0) - 1
    length = info_ref[HEAD + step]
    width = xs_ref.shape[1]
    half = width // 2

    @pl.when(step == 0)
    def _():
        acc[...] = jnp.zeros_like(acc)
        sums[...] = jnp.zeros_like(sums)
        small_ref[...] = jnp.zeros_like(small_ref)

    inside = slot_times(0, SLOT) < length
    put_with_edges(ch, cs_ref[...].astype(F32))
    grad_conv = gctx_ref[...].astype(F32)
    put_with_edges(gh, grad_conv)
    taps = taps_ref[...]
    put_with_edges(th, taps)
    table, picker = spread_table(half), gather_table(half)
    grad_taps = jnp.zeros((SLOT, LANES), F32)
    grad_source = jnp.zeros((SLOT, half), F32)
    for j in range(KERNEL):
        moved = grad_conv * ch[shifted_rows(j - REACH), :]
        here = product(moved.astype(BF16), picker)
        grad_taps = grad_taps + (here if j == 0 else pltpu.roll(here, j * TAP_STRIDE, 1))
        back = shifted_rows(REACH - j)
        grad_source = grad_source + product(tap_terms(th[back, :], j), table) * gh[back, :]
    grad_source = jnp.where(inside, grad_source, 0.0).astype(BF16)
    gs_ref[...] = grad_source
    small_ref[130:131, :] += column_sum(grad_source.astype(F32))

    query = query_ref[...].astype(F32)
    keyconv = kc_ref[...].astype(F32)
    grad_logits = taps * (grad_taps - tap_groups(taps * grad_taps, jnp.add))
    grad_logits = grad_logits.astype(BF16)
    small_ref[129:130, :LANES] += column_sum(grad_logits.astype(F32))
    span_in = (keyconv * query).astype(BF16)
    small_ref[0:TAPS_ROW, :] += product(transposed(grad_logits)[0:TAPS_ROW, :], span_in)
    grad_span = right_product(grad_logits, ordered_span(ws_ref)).astype(BF16).astype(F32)
    extra_ref[...] = (grad_span * keyconv).astype(BF16)
    grad_key = (grad_span * query).astype(BF16)
    gk_ref[...] = grad_key
    small_ref[128:129, :] += column_sum(grad_key.astype(F32))
    acc[:, 0:half] += product(transposed(dw_ref[...]), grad_key)
    acc[:, half:] += product(transposed(xs_ref[...]), grad_source)
    put_with_edges(xh, right_product(grad_key, wp_ref[...]).astype(BF16).astype(F32))

    def depth_chunk(c, carry):
        lanes = pl.ds(pl.multiple_of(c * LANES, LANES), LANES)
        for j in range(KERNEL):
            total = jnp.zeros((GROUP, LANES), F32)
            for first in range(0, SLOT, ROWS):
                own = xs_ref[first : first + ROWS, lanes].astype(F32)
                moved = xh[shifted_rows(REACH - j, first, ROWS), lanes] * own
                total = total + jnp.sum(moved.reshape(ROWS // GROUP, GROUP, LANES), axis=0)
            sums[j, :, lanes] += total
        return carry

    lax.fori_loop(0, width // LANES, depth_chunk, 0)

    @pl.when(step == last)
    def _():
        for j in range(KERNEL):
            total = column_sum(sums[j])
            for side in range(2):
                row = TAPS_ROW + side * KERNEL + j
                small_ref[row : row + 1, :] = total[:, side * half : (side + 1) * half]
        sources = ((acc, chunk_rows, 2), (dense_ref, chunk_rows, 2))
        emit_chunks(sources, info_ref, keep_ref, send_ref)


def input_kernel(
    info_ref, gm_ref, flat_ref, gs_ref, gk_ref, wq_ref, wk_ref, wv_ref, wc_ref, wp_ref, dk_ref,
    *rest,
):
    rows_ref, base, gh, block = rest[-4:]
    step = pl.program_id(0)
    start, length = slot_bounds(info_ref, step)
    half = gs_ref.shape[1]

    @pl.when(step == 0)
    def _():
        rows_ref[...] = jnp.zeros_like(rows_ref)

    put_with_edges(gh, right_product(gk_ref[...], wp_ref[...]).astype(BF16).astype(F32))
    total = gm_ref[...].astype(F32) + right_product(gs_ref[...], wc_ref[...])
    for third, ref in enumerate((wq_ref, wk_ref, wv_ref)):
        total = total + right_product(flat_ref[:, third * half : (third + 1) * half], ref[...])
    base[...] = total

    def depth_chunk(c, carry):
        lanes = pl.ds(pl.multiple_of(c * LANES, LANES), LANES)
        for first in range(0, SLOT, ROWS):
            inner = slice(first, first + ROWS)
            total = base[inner, lanes]
            for j in range(KERNEL):
                total = total + dk_ref[j : j + 1, lanes] * gh[shifted_rows(REACH - j, first, ROWS), lanes]
            block[inner, lanes] = total.astype(BF16)
        return carry

    lax.fori_loop(0, half // LANES, depth_chunk, 0)
    slot_to_rows(rows_ref, start, length, block[...])


def attend_backward_kernel(
    info_ref, gctx_ref, ctx_ref, xs_ref, qkv_ref, lse_ref, extra_ref, *rest, first_slot, small, chunks
):
    if chunks is None:
        flat_ref, sum_ref, own_ref, gqt = rest
    else:
        smallm_ref, smallc_ref, _, before_ref, own_before_ref = rest[:5]
        flat_ref, keep_ref, send_ref, gqt, sum_ref, own_ref, small_ref = rest[5:]
    step = pl.program_id(0)
    half = gctx_ref.shape[1]

    @pl.when(step == 0)
    def _():
        if chunks is None:
            sum_ref[...] = jnp.zeros_like(sum_ref)
            own_ref[...] = jnp.zeros_like(own_ref)
        else:
            sum_ref[...] = before_ref[...]
            own_ref[...] = own_before_ref[...]

    outside = dead_rows(info_ref[HEAD + step + first_slot])

    def one_pair(pair, carry):
        at = pl.multiple_of(pair * LANES, LANES)
        here, there, third = (pl.ds(k * half + at, LANES) for k in range(3))
        query_pair = qkv_ref[:, here]
        keys = qkv_ref[:, there]
        values = qkv_ref[:, third]
        keys_t = transposed(keys)
        grad_pair = gctx_ref[:, here]
        dots = transposed(grad_pair.astype(F32) * ctx_ref[:, here].astype(F32))
        grad_keys, grad_values = [], []
        for side in range(2):
            mask = pair_mask(side)
            rows = slice(side * HEAD_DIM, (side + 1) * HEAD_DIM)
            scores = head_scores(keys, query_pair, side, outside)
            probs = jnp.exp(scores - lse_ref[pl.ds(2 * pair + side, 1), :])
            grad_probs = right_product(jnp.where(mask, values, jnp.zeros_like(values)), grad_pair)
            weighted = column_sum(dots[rows, :])
            grad_scores = (probs * (grad_probs - weighted)).astype(BF16)
            grad_keys.append(product(grad_scores, query_pair))
            grad_values.append(product(probs.astype(BF16), grad_pair))
            gqt[pl.ds(pl.multiple_of(at + side * HEAD_DIM, HEAD_DIM), HEAD_DIM), :] = product(
                keys_t[rows, :], grad_scores
            )
        first = pair_mask(0)
        flat_ref[:, there] = (jnp.where(first, grad_keys[0], grad_keys[1]) * 0.125).astype(BF16)
        flat_ref[:, third] = jnp.where(first, grad_values[0], grad_values[1]).astype(BF16)
        return carry

    lax.fori_loop(0, HEADS // 2, one_pair, 0)
    flat_ref[:, :half] = (transposed(gqt[...]) * 0.125 + extra_ref[...].astype(F32)).astype(BF16)
    sum_ref[...] += product(transposed(xs_ref[...]), flat_ref[...])
    for third in range(3):
        own_ref[third : third + 1, :] += column_sum(
            flat_ref[:, third * half : (third + 1) * half].astype(F32)
        )
    if chunks is None:
        return

    @pl.when(step == pl.num_programs(0) - 1)
    def _():
        small_ref[: smallm_ref.shape[0], :] = smallm_ref[...]
        small_ref[SPAN_ROW : SPAN_ROW + smallc_ref.shape[0], :] = smallc_ref[...]
        small_ref[OWN_ROW : OWN_ROW + own_ref.shape[0], :] = own_ref[...]
        sources = ((sum_ref, chunks, 3), (small_ref, small, 1))
        emit_chunks(sources, info_ref, keep_ref, send_ref)


def restore_kernel(info_ref, slot_ref, rows_ref):
    step = pl.program_id(0)
    start, length = slot_bounds(info_ref, step)

    @pl.when(step == 0)
    def _():
        rows_ref[...] = jnp.zeros_like(rows_ref)

    slot_to_rows(rows_ref, start, length, slot_ref[...])


def assemble_kernel(info_ref, *refs, layout):
    sources, outs, small_ref = refs[:2], refs[2:-1], refs[-1]
    group, own = my_place(info_ref)
    count, _, columns = sources[0].shape

    def one(position, carry):
        for core, source in enumerate(sources):
            index = (group ^ core) * count + (own ^ mask_at(info_ref, position))
            chunk = source[position].astype(F32)
            at, place = 0, 0
            for rows, wide in layout:
                if wide == 0:
                    small_ref[pl.ds(pl.multiple_of(index * rows, 8), rows), :] = chunk[at : at + rows]
                    at += rows
                    continue
                for block in range(wide):
                    outs[place][index, :, block * columns : (block + 1) * columns] = chunk[at : at + rows]
                    at += rows
                place += 1
        return carry

    lax.fori_loop(0, count, one, 0)
    place = sum(1 for _, wide in layout if wide)
    vectors, (depth_ref, span_ref, bias_ref) = outs[place : place + 10], outs[place + 10 :]
    for i in range(6):
        pair = [small_ref[2 * i + g : 2 * i + g + 1, :] for g in range(2)]
        vectors[i][...] = jnp.concatenate(pair, 1).reshape(2 * columns)
    for i, row in enumerate((OWN_ROW, OWN_ROW + 2, SPAN_ROW + 128, SPAN_ROW + 130)):
        vectors[6 + i][...] = small_ref[row : row + 1, :].reshape(columns)
    first = SPAN_ROW + TAPS_ROW
    for g in range(2):
        rows = small_ref[first + g * KERNEL : first + (g + 1) * KERNEL, :]
        depth_ref[:, g * columns : (g + 1) * columns] = rows
    order = jnp.where(tap_order(), 1.0, 0.0).astype(BF16)
    span = transposed(small_ref[SPAN_ROW : SPAN_ROW + LANES, :]).astype(BF16)
    span_ref[...] = right_product(span, order)
    bias = small_ref[SPAN_ROW + 129 : SPAN_ROW + 130, :LANES]
    bias = jnp.broadcast_to(bias, (16, LANES)).astype(BF16)
    bias_ref[...] = right_product(bias, order)[0:1].reshape(HEADS * KERNEL)


def resident(shape):
    zeros = (0,) * len(shape)
    return pl.BlockSpec(tuple(shape), lambda *_: zeros, pipeline_mode=pl.Buffered(1))


def slot_block(columns, rows=SLOT, column=0):
    return pl.BlockSpec((None, rows, columns), lambda i: (i, 0, column))


SCALARS = pl.BlockSpec(memory_space=pltpu.SMEM)
ANYWHERE = pl.BlockSpec(memory_space=pl.ANY)
LIMIT = 60 * 1024 * 1024


def shape_of(*dims, dtype=F32):
    return jax.ShapeDtypeStruct(dims, dtype)


def cost(flops, nbytes):
    return pl.CostEstimate(flops=int(flops), bytes_accessed=int(nbytes), transcendentals=0)


PARAMS = pltpu.CompilerParams(vmem_limit_bytes=LIMIT)
LARGE = pltpu.CompilerParams(vmem_limit_bytes=LIMIT + 3 * 1024 * 1024)
RATE = 1.15e9


def busy(us):
    return cost(us * RATE, us * 1e6)


def run_project(info, slots, x, *rest):
    total, width = x.shape
    half = width // 2
    return pl.pallas_call(
        project_kernel,
        grid=(slots,),
        in_specs=[SCALARS] + [resident(a.shape) for a in (x,) + rest],
        out_specs=[slot_block(width), slot_block(3 * half), slot_block(half)],
        out_shape=[
            shape_of(slots, SLOT, width, dtype=BF16),
            shape_of(slots, SLOT, 3 * half, dtype=BF16),
            shape_of(slots, SLOT, half, dtype=BF16),
        ],
        compiler_params=PARAMS,
        cost_estimate=busy(10),
        name="project",
    )(info, x, *rest)


def run_convolve(info, xs, qkv, cs, *rest):
    slots, _, width = xs.shape
    half = width // 2
    return pl.pallas_call(
        convolve_kernel,
        grid=(slots,),
        in_specs=[SCALARS, slot_block(width), slot_block(half), slot_block(half)]
        + [resident(a.shape) for a in rest],
        out_specs=[slot_block(width), slot_block(half), slot_block(LANES), slot_block(half)],
        out_shape=[
            shape_of(slots, SLOT, width, dtype=BF16),
            shape_of(slots, SLOT, half, dtype=BF16),
            shape_of(slots, SLOT, LANES),
            shape_of(slots, SLOT, half, dtype=BF16),
        ],
        scratch_shapes=[
            pltpu.VMEM((SLOT + 2 * EDGE, width), F32),
            pltpu.VMEM((SLOT + 2 * EDGE, half), F32),
        ],
        compiler_params=PARAMS,
        cost_estimate=busy(15),
        name="convolve",
    )(info, xs, qkv, cs, *rest)


def run_attend(info, qkv, conv):
    slots, _, half = conv.shape
    return pl.pallas_call(
        attend_kernel,
        grid=(slots,),
        in_specs=[SCALARS, slot_block(3 * half), slot_block(half)],
        out_specs=[slot_block(2 * half), slot_block(SLOT, 8)],
        out_shape=[shape_of(slots, SLOT, 2 * half, dtype=BF16), shape_of(slots, 8, SLOT)],
        scratch_shapes=[pltpu.VMEM((half, SLOT), F32)],
        compiler_params=PARAMS,
        cost_estimate=busy(16),
        name="attend",
    )(info, qkv, conv)


def run_middle(info, ctx, xs, upstream, vectors, wd, weights, shard, count):
    bits = offset_masks(digits_of(count, RADIX))
    order = [bits.index(mask) for mask in offset_masks(digits_of(count))]
    slots, _, width = xs.shape
    half = width // 2
    hidden = count * shard
    pieces = len(weights) // 2
    bd, g1, b1, ob, g2, b2 = vectors
    rows = 2 * shard + BIAS_ROWS
    return pl.pallas_call(
        functools.partial(middle_kernel, pieces=pieces, order=order),
        grid=(slots,),
        in_specs=[SCALARS, slot_block(width), slot_block(width)]
        + [resident(a.shape) for a in (upstream, wd, bd, g1, b1, ob, g2, b2)]
        + [ANYWHERE] * len(weights),
        out_specs=[slot_block(width), slot_block(width), slot_block(width)]
        + [resident((count, rows, half))] * 2
        + [resident((width, width)), resident((16, half))],
        out_shape=[
            shape_of(slots, SLOT, width, dtype=BF16),
            shape_of(slots, SLOT, width, dtype=BF16),
            shape_of(slots, SLOT, width, dtype=BF16),
        ]
        + [shape_of(count, rows, half, dtype=BF16)] * 2
        + [shape_of(width, width), shape_of(16, half)],
        scratch_shapes=[
            pltpu.VMEM((2, count, shard, half + EXTRA), BF16),
            pltpu.VMEM((2, count, shard, half), BF16),
            pltpu.VMEM((2, count, BIAS_ROWS, LANES), BF16),
            pltpu.VMEM((2, SLOT, hidden), BF16),
            pltpu.VMEM((2, SLOT, hidden), BF16),
            pltpu.VMEM((2, SLOT, half + EXTRA), BF16),
            pltpu.VMEM((2, SLOT, half), BF16),
            pltpu.VMEM((2, half + 16, SLOT), BF16),
            pltpu.VMEM((2, half, SLOT), BF16),
            pltpu.VMEM((2, SLOT, half), F32),
            pltpu.VMEM((2, half + 16, hidden), F32),
            pltpu.VMEM((2, half, hidden), F32),
            pltpu.SemaphoreType.DMA((6 * pieces,)),
        ],
        compiler_params=LARGE,
        cost_estimate=busy(64),
        name="feed_forward",
    )(info, ctx, xs, upstream, wd, bd, g1, b1, ob, g2, b2, *weights)


def run_span_backward(info, gctx, xs, qkv, cs, dw, kc, taps, ws, wp, dense, count, chunk_rows):
    slots, _, width = xs.shape
    half = width // 2
    return pl.pallas_call(
        functools.partial(span_backward_kernel, chunk_rows=chunk_rows),
        grid=(slots,),
        in_specs=[
            SCALARS, slot_block(half, column=1), slot_block(width), slot_block(half),
            slot_block(half), slot_block(width), slot_block(half), slot_block(LANES),
            resident(ws.shape), resident(wp.shape), resident(dense.shape),
        ],
        out_specs=[slot_block(half)] * 3
        + [resident((count, 4 * chunk_rows, half))] * 2
        + [resident((136, half))],
        out_shape=[
            shape_of(slots, SLOT, half, dtype=BF16),
            shape_of(slots, SLOT, half, dtype=BF16),
            shape_of(slots, SLOT, half, dtype=BF16),
        ]
        + [shape_of(count, 4 * chunk_rows, half, dtype=BF16)] * 2
        + [shape_of(136, half)],
        scratch_shapes=[
            pltpu.VMEM((SLOT + 2 * EDGE, half), F32),
            pltpu.VMEM((SLOT + 2 * EDGE, half), F32),
            pltpu.VMEM((SLOT + 2 * EDGE, LANES), F32),
            pltpu.VMEM((SLOT + 2 * EDGE, width), F32),
            pltpu.VMEM((KERNEL, GROUP, width), F32),
            pltpu.VMEM((width, width), F32),
        ],
        compiler_params=PARAMS,
        cost_estimate=busy(23),
        name="span_backward",
    )(info, gctx, xs, qkv, cs, dw, kc, taps, ws, wp, dense)


def run_attend_backward(info, gctx, ctx, xs, qkv, lse, extra, count, chunk_rows, before=None, smalls=()):
    slots, _, width = xs.shape
    half = width // 2
    ending = before is not None
    first = 1 if ending else 0
    small_rows = small_chunk(count)
    rows = 3 * chunk_rows + small_rows

    def block(columns, rows=SLOT):
        return pl.BlockSpec((None, rows, columns), lambda i: (i + first, 0, 0))

    more = list(smalls) + list(before) if ending else []
    more_specs = [resident(a.shape) for a in more]
    if ending:
        more_specs[len(smalls)] = ANYWHERE
    sums = [(width, 3 * half), (8, half)]
    return pl.pallas_call(
        functools.partial(
            attend_backward_kernel, first_slot=first, small=small_rows, chunks=chunk_rows if ending else None
        ),
        grid=(slots - 1 if ending else 1,),
        in_specs=[SCALARS, block(half), block(half), block(width), block(3 * half), block(SLOT, 8), block(half)]
        + more_specs,
        out_specs=[block(3 * half)]
        + ([resident((count, rows, half))] * 2 if ending else [resident(d) for d in sums]),
        out_shape=[shape_of(slots, SLOT, 3 * half, dtype=BF16)]
        + ([shape_of(count, rows, half, dtype=BF16)] * 2 if ending else [shape_of(*d) for d in sums]),
        scratch_shapes=[pltpu.VMEM((half, SLOT), F32)]
        + ([pltpu.VMEM(d, F32) for d in sums + [(SMALL_ROWS, half)]] if ending else []),
        input_output_aliases={7 + len(smalls): 0} if ending else {},
        compiler_params=PARAMS,
        cost_estimate=busy(14 if ending else 7),
        name="attend_backward",
    )(info, gctx, ctx, xs, qkv, lse, extra, *more)


def run_input(info, gm, flat, gs, gk, weights, dk, total, before=None):
    slots, _, width = gm.shape
    half = width // 2
    side = 0 if before is None else 1
    more = [] if before is None else [before]
    rows = pl.BlockSpec((half, half), lambda i: (side, 0))
    return pl.pallas_call(
        input_kernel,
        grid=(slots,),
        in_specs=[
            SCALARS, slot_block(half, column=side), slot_block(3 * half), slot_block(half),
            slot_block(half),
        ]
        + [rows] * len(weights)
        + [pl.BlockSpec((KERNEL, half), lambda i: (0, side))]
        + [ANYWHERE] * len(more),
        out_specs=pl.BlockSpec((total, half), lambda i: (0, side)),
        out_shape=shape_of(total, width, dtype=BF16),
        scratch_shapes=[
            pltpu.VMEM((SLOT, half), F32),
            pltpu.VMEM((SLOT + 2 * EDGE, half), F32),
            pltpu.VMEM((SLOT, half), BF16),
        ],
        input_output_aliases={6 + len(weights): 0} if more else {},
        compiler_params=PARAMS,
        cost_estimate=busy(8),
        name="input_gradient",
    )(info, gm, flat, gs, gk, *weights, dk, *more)


def run_restore(info, block, total):
    slots, _, width = block.shape
    return pl.pallas_call(
        restore_kernel,
        grid=(slots,),
        in_specs=[SCALARS, slot_block(width)],
        out_specs=resident((total, width)),
        out_shape=shape_of(total, width, dtype=BF16),
        compiler_params=PARAMS,
        cost_estimate=busy(4),
        name="restore_rows",
    )(info, block)


def run_assemble(info, sources, layout):
    count, _, half = sources[0].shape
    width, taps = 2 * half, HEADS * KERNEL
    shapes = [(2 * count, rows, wide * half) for rows, wide in layout if wide]
    whole = len(shapes)
    shapes += [(width,)] * 6 + [(half,)] * 4 + [(KERNEL, width), (half, taps), (taps,)]
    outs = pl.pallas_call(
        functools.partial(assemble_kernel, layout=layout),
        in_specs=[SCALARS] + [pl.BlockSpec(memory_space=pltpu.VMEM)] * len(sources),
        out_specs=[pl.BlockSpec(memory_space=pltpu.VMEM)] * len(shapes),
        out_shape=[shape_of(*s) for s in shapes],
        scratch_shapes=[pltpu.VMEM((2 * count * small_chunk(count), half), F32)],
        compiler_params=PARAMS,
        cost_estimate=busy(3),
        name="assemble",
    )(info, *sources)
    return [o.reshape(2 * count * o.shape[1], -1) for o in outs[:whole]] + list(outs[whole:])


def small_chunk(count):
    return round_up(-(-SMALL_ROWS // (2 * count)), 8)


def swap_groups(block):
    return lax.ppermute(block, "grp", [(0, 1), (1, 0)])


def send_across(block, count, offset):
    return lax.ppermute(block, "dp", [(i, i ^ offset) for i in range(count)])


def tree_sum(parts):
    parts = [p.astype(F32) for p in parts]
    while len(parts) > 1:
        parts = [parts[i] + parts[i + 1] for i in range(0, len(parts), 2)]
    return parts[0].astype(BF16)


def tie(value, *others):
    return lax.optimization_barrier((value, others))[0]


def advance(done, *sums, held=()):
    both = sums + tuple(held)
    arrived = lax.optimization_barrier((done, [s.current for s in both]))[1]
    for one, current in zip(both, arrived):
        one.current = current
    sent = []
    for one in sums:
        sent += one.step()
    return sent


class ChunkSum:
    def __init__(self, keep, send, count, digits=None):
        self.count, self.digits = count, digits or digits_of(count)
        self.current, self.stage = [keep, swap_groups(send)], 0

    def step(self):
        if self.stage == len(self.digits):
            return []
        stride, radix = self.digits[self.stage]
        size = self.current[0].shape[0] // radix
        parts = [
            tree_sum([p[s * size : (s + 1) * size] for p in self.current]) for s in range(radix)
        ]
        self.current = [parts[0]] + [
            send_across(parts[s], self.count, s * stride) for s in range(1, radix)
        ]
        self.stage += 1
        return parts

    def finish(self):
        while self.stage < len(self.digits):
            self.step()
        return tree_sum(self.current)


class Gather:
    def __init__(self, own, count, digits):
        self.count, self.digits, self.stage, self.current = count, digits, 0, [own]

    def step(self):
        own = jnp.concatenate(self.current, 0)
        if self.stage == len(self.digits):
            self.current = [own]
            return [own]
        stride, radix = self.digits[self.stage]
        self.current = [own] + [send_across(own, self.count, s * stride) for s in range(1, radix)]
        self.stage += 1
        return [own]

    def finish(self):
        while self.stage < len(self.digits):
            self.step()
        return jnp.concatenate(self.current, 0)


def round_up(value, unit):
    return -(-value // unit) * unit


def weight_shard(inter_weight, inter_bias, down_weight):
    columns = inter_weight.shape[2]
    shard = round_up(columns, 16)
    half = down_weight.shape[2]
    pad = ((0, shard - columns), (0, 0))
    first = jnp.pad(jnp.transpose(inter_weight[0]), pad)
    second = jnp.pad(down_weight[0], pad)
    rest, terms = inter_bias, []
    for _ in range(3):
        term = lax.reduce_precision(rest, 8, 7)
        terms.append(term)
        rest = rest - term
    terms = jnp.concatenate(terms, 0).astype(BF16)
    terms = jnp.pad(terms, ((0, BIAS_ROWS - 3), (0, half - columns)))
    return jnp.concatenate([first, second, terms], 0)[None], shard


def on_device(
    count, layer_input, lengths, query_weight, query_bias, key_weight, value_weight, value_bias,
    depth_kernel, point_weight, point_bias, span_weight, span_bias, conv_out_weight,
    conv_out_bias, dense_weight, dense_bias, first_gain, first_shift, inter_weight, inter_bias,
    grouped_down_weight, output_bias, second_gain, second_shift, upstream_grad,
):
    total, width = layer_input.shape
    half = width // 2
    slots = lengths.shape[1]
    chunk_rows = round_up(-(-width // (2 * count)), 8)
    info = jnp.concatenate(
        [
            lax.axis_index("grp").astype(jnp.int32).reshape(1),
            lax.axis_index("dp").astype(jnp.int32).reshape(1),
            lengths[0],
            jnp.array(offset_masks(digits_of(count)), jnp.int32),
        ]
    )
    own_weights, shard = weight_shard(inter_weight, inter_bias, grouped_down_weight)
    digits = digits_of(count)
    block = own_weights
    for stride, radix in reversed(digits[1:]):
        block = [block] + [send_across(block, count, s * stride) for s in range(1, radix)]
        if stride == digits[1][0]:
            break
        block = jnp.concatenate(block, 0)

    xs, qkv, cs = run_project(
        info, slots, tie(layer_input, own_weights), query_weight, key_weight, value_weight,
        conv_out_weight, query_bias, value_bias, conv_out_bias,
    )
    block = jnp.concatenate(tie(block, xs), 0)
    stride, radix = digits[0]
    block = [block] + [send_across(block, count, s * stride) for s in range(1, radix)]
    dw, kc, taps, conv = run_convolve(
        info, tie(xs, block[0]), qkv, cs, depth_kernel, point_weight, point_bias, span_weight, span_bias
    )
    ctx, lse = run_attend(info, qkv, conv)
    block = tie(block, ctx)
    weights = block + [swap_groups(b) for b in block]
    vectors = (dense_bias, first_gain, first_shift, output_bias, second_gain, second_shift)
    out_slots, gm, gctx, keep, send, dense, small_m = run_middle(
        info, ctx, xs, upstream_grad, vectors, dense_weight, weights, shard, count
    )
    ffn_sum = ChunkSum(keep, send, count, digits_of(count, RADIX))
    layer_out = run_restore(info, tie(out_slots, send), total)
    sent = advance(layer_out, ffn_sum)
    gs, extra, gk, keep_c, send_c, small_c = run_span_backward(
        info, tie(gctx, sent), xs, qkv, cs, dw, kc, taps, span_weight, point_weight, dense, count, chunk_rows
    )
    span_sum = ChunkSum(keep_c, send_c, count)
    sent = advance(gs, ffn_sum)
    part = run_attend_backward(
        info, tie(gctx, send_c, sent), ctx, xs, qkv, lse, extra, count, chunk_rows
    )
    sent = advance(part, span_sum, ffn_sum)
    flat, keep_a, send_a = run_attend_backward(
        info, tie(gctx, sent), ctx, xs, qkv, lse, extra, count, chunk_rows, part, [small_m, small_c]
    )
    mixer_sum = ChunkSum(keep_a, send_a, count)
    sent = advance(flat, span_sum, held=[ffn_sum])
    matrices = [query_weight, key_weight, value_weight, conv_out_weight, point_weight]
    in_half = run_input(info, tie(gm, sent, send_a), flat, gs, gk, matrices, depth_kernel, total)
    digits, bits = digits_of(count), digits_of(count, RADIX)
    sent = advance(in_half, mixer_sum, held=[span_sum])
    span_all = Gather(span_sum.finish(), count, bits[1:])
    sent += span_all.step()
    in_grad = run_input(info, tie(gm, sent), flat, gs, gk, matrices, depth_kernel, total, in_half)
    sent = advance(in_grad, mixer_sum, span_all)
    mixer_all = Gather(tie(mixer_sum.finish(), sent), count, digits[:0:-1])
    sent = mixer_all.step() + advance(sent, held=[span_all])
    sent = advance(sent, mixer_all) if len(digits) > 2 else sent
    pieces = [tie(mixer_all.finish(), sent), span_all.finish()]
    pieces = Gather(jnp.concatenate(pieces, 1), count, digits[:1]).finish()
    ffn = ffn_sum.finish()
    rows = chunk_rows
    outs = run_assemble(
        info, [pieces, swap_groups(pieces)],
        ((rows, 1),) * 3 + ((small_chunk(count), 0), (rows, 1), (rows, 1), (rows, 2)),
    )
    grad_query, grad_key, grad_value, grad_point, grad_conv, grad_dense = [g[:width] for g in outs[:6]]
    vectors, (grad_depth, grad_span, grad_span_bias) = outs[6:16], outs[16:]
    ffn = ffn.astype(F32)
    columns = inter_weight.shape[2]
    return (
        layer_out,
        in_grad,
        grad_query,
        vectors[6],
        grad_key,
        grad_value,
        vectors[7],
        grad_depth,
        grad_point,
        vectors[8],
        grad_span,
        grad_span_bias,
        grad_conv,
        vectors[9],
        grad_dense,
        vectors[5],
        vectors[3],
        vectors[4],
        jnp.transpose(ffn[:, :columns], (0, 2, 1)),
        ffn[:, 2 * shard, :columns],
        ffn[:, shard : shard + columns],
        vectors[2],
        vectors[0],
        vectors[1],
    )


def solution(mesh):
    rows = P(("grp", "dp"), None)
    one = P()
    return jax.shard_map(
        functools.partial(on_device, mesh.shape["dp"]),
        mesh=mesh,
        in_specs=(rows, rows) + (one,) * 16
        + (P("grp", None, "dp"), P("grp", "dp"), P("grp", "dp", None)) + (one,) * 3 + (rows,),
        out_specs=(rows, rows) + (one,) * 16
        + (P("grp", None, "dp"), P("grp", "dp"), P("grp", "dp", None)) + (one,) * 3,
        check_vma=False,
    )
```

```python
import functools

import jax
import jax.numpy as jnp
from jax import lax
from jax.experimental import pallas as pl
from jax.experimental.pallas import tpu as pltpu
from jax.sharding import PartitionSpec as P

HEADS = 6
HEAD_DIM = 64
KERNEL = 9
REACH = KERNEL // 2
SLOT = 512
SLOTS = 3
GROUP = 8
SPAN = SLOT // GROUP
EDGE = REACH * GROUP
LANES = 128
TAP_STRIDE = 8
CHUNK_ROWS = 1536
EXTRA = 128
ROWS = 128
SPAN_ROW = 16
TAPS_ROW = 80
OWN_ROW = 152
SMALL_ROWS = 160
BIAS_ROWS = 8
RADIX = 4
NEGATIVE = -1e30
NORM_EPS = 1e-12
ROOT_HALF = 0.7071067811865476
DENSITY = 0.3989422804014327
BF16 = jnp.bfloat16
F32 = jnp.float32


def product(left, right):
    return jnp.dot(left, right, preferred_element_type=F32)


def right_product(left, right):
    return lax.dot_general(left, right, (((1,), (1,)), ((), ())), preferred_element_type=F32)


def transposed(block):
    return jnp.transpose(block, (1, 0))


def column_sum(block):
    return jnp.sum(block, axis=0, keepdims=True)


def row_mean(block):
    return jnp.mean(block, axis=-1, keepdims=True)


def tap_groups(block, combine):
    step = TAP_STRIDE
    while step < LANES:
        block = combine(block, pltpu.roll(block, step, 1))
        step *= 2
    return block


def high_low(block):
    high = block.astype(BF16)
    low = (block - high.astype(F32)).astype(BF16)
    return high, low


HEAD = 2


def slot_bounds(info_ref, index):
    start = jnp.int32(0)
    for other in range(SLOTS - 1):
        start = start + jnp.where(index > other, info_ref[HEAD + other], 0)
    return start, info_ref[HEAD + index]


def my_place(info_ref):
    return info_ref[0], info_ref[1]


def mask_at(info_ref, position):
    return info_ref[HEAD + SLOTS + position]


def slot_times(first, count):
    row = lax.broadcasted_iota(jnp.int32, (count, 1), 0) + first
    return (row & (GROUP - 1)) * SPAN + row // GROUP


def rows_to_slot(source_ref, start, length):
    total = source_ref.shape[0]
    window = SLOT + 16
    base = pl.multiple_of(jnp.minimum(start // 16 * 16, total - window), 16)
    source = source_ref[pl.ds(base, window), :]
    col = lax.broadcasted_iota(jnp.int32, (1, window), 1) + (base - start)
    time = slot_times(0, SLOT)
    time = jnp.where(time < length, time, -SLOT * SLOT)
    pick = jnp.where(col == time, 1.0, 0.0).astype(BF16)
    return product(pick, source)


def slot_to_rows(target_ref, start, length, block):
    total = target_ref.shape[0]
    window = SLOT + 16
    base = pl.multiple_of(jnp.minimum(start // 16 * 16, total - window), 16)
    col = lax.broadcasted_iota(jnp.int32, (1, SLOT), 1)
    time = lax.broadcasted_iota(jnp.int32, (window, 1), 0) + (base - start)
    row = (time & (SPAN - 1)) * GROUP + (time // SPAN)
    row = jnp.where((time >= 0) & (time < length), row, -1)
    pick = jnp.where(col == row, 1.0, 0.0).astype(BF16)
    target_ref[pl.ds(base, window), :] += product(pick, block).astype(BF16)


def put_with_edges(ref, block):
    ref[EDGE : EDGE + SLOT, :] = block
    sub = lax.broadcasted_iota(jnp.int32, (GROUP, 1), 0)
    for k in range(REACH):
        before = block[SLOT - EDGE + k * GROUP : SLOT - EDGE + (k + 1) * GROUP, :]
        before = jnp.where(sub == 0, 0.0, pltpu.roll(before, 1, 0))
        ref[k * GROUP : (k + 1) * GROUP, :] = before
        after = block[k * GROUP : (k + 1) * GROUP, :]
        after = jnp.where(sub == GROUP - 1, 0.0, pltpu.roll(after, GROUP - 1, 0))
        ref[EDGE + SLOT + k * GROUP : EDGE + SLOT + (k + 1) * GROUP, :] = after


def shifted_rows(offset, first=0, count=SLOT):
    at = EDGE + offset * GROUP + first
    return slice(at, at + count)


def pair_mask(half):
    lane = lax.broadcasted_iota(jnp.int32, (1, LANES), 1)
    return (lane // HEAD_DIM) == half


def digits_of(count, wide=64):
    digits, stride = [], 1
    while stride < count:
        radix = RADIX if (count // stride) % RADIX == 0 and stride < wide else 2
        digits.append((stride, radix))
        stride *= radix
    return digits


def offset_masks(digits):
    masks = [0]
    for stride, radix in reversed(digits):
        masks = [digit * stride ^ mask for digit in range(radix) for mask in masks]
    return masks


def vector_row(ref):
    return ref[...].reshape(1, ref.shape[0])


def tap_order():
    row = lax.broadcasted_iota(jnp.int32, (HEADS * KERNEL, LANES), 0)
    lane = lax.broadcasted_iota(jnp.int32, (HEADS * KERNEL, LANES), 1)
    tap, head = lane // TAP_STRIDE, lane % TAP_STRIDE
    return (row == head * KERNEL + tap) & (head < HEADS) & (tap < KERNEL)


def ordered_span(ws_ref):
    return product(ws_ref[...], jnp.where(tap_order(), 1.0, 0.0).astype(BF16)).astype(BF16)


def spread_table(half):
    lane = lax.broadcasted_iota(jnp.int32, (2 * LANES, half), 0) % LANES
    head = lax.broadcasted_iota(jnp.int32, (2 * LANES, half), 1) // HEAD_DIM
    return jnp.where(lane == head, 1.0, 0.0).astype(BF16)


def gather_table(half):
    head = lax.broadcasted_iota(jnp.int32, (half, LANES), 0) // HEAD_DIM
    lane = lax.broadcasted_iota(jnp.int32, (half, LANES), 1)
    return jnp.where(lane == head, 1.0, 0.0).astype(BF16)


def tap_terms(taps, j):
    moved = taps if j == 0 else pltpu.roll(taps, LANES - j * TAP_STRIDE, 1)
    return jnp.concatenate(high_low(moved), 1)


def project_kernel(
    info_ref, x_ref, wq_ref, wk_ref, wv_ref, wc_ref, bq_ref, bv_ref, bc_ref, xs_ref, qkv_ref, cs_ref
):
    half = wq_ref.shape[1]
    start, length = slot_bounds(info_ref, pl.program_id(0))
    xs_ref[...] = rows_to_slot(x_ref, start, length).astype(BF16)
    inside = slot_times(0, SLOT) < length
    rows = xs_ref[...]
    qkv_ref[:, :half] = (product(rows, wq_ref[...]) + vector_row(bq_ref)).astype(BF16)
    qkv_ref[:, half : 2 * half] = product(rows, wk_ref[...]).astype(BF16)
    qkv_ref[:, 2 * half :] = (product(rows, wv_ref[...]) + vector_row(bv_ref)).astype(BF16)
    source = product(rows, wc_ref[...]) + vector_row(bc_ref)
    cs_ref[...] = jnp.where(inside, source, 0.0).astype(BF16)


def convolve_kernel(
    info_ref, xs_ref, query_ref, cs_ref, dk_ref, wp_ref, bp_ref, ws_ref, bs_ref,
    dw_ref, kc_ref, taps_ref, conv_ref,
    xh, ch,
):
    width = xs_ref.shape[1]
    half = width // 2
    put_with_edges(xh, xs_ref[...].astype(F32))
    put_with_edges(ch, cs_ref[...].astype(F32))

    def depth_chunk(c, carry):
        lanes = pl.ds(pl.multiple_of(c * LANES, LANES), LANES)
        for first in range(0, SLOT, ROWS):
            total = jnp.zeros((ROWS, LANES), F32)
            for j in range(KERNEL):
                total = total + dk_ref[j : j + 1, lanes] * xh[shifted_rows(j - REACH, first, ROWS), lanes]
            dw_ref[first : first + ROWS, lanes] = total.astype(BF16)
        return carry

    lax.fori_loop(0, width // LANES, depth_chunk, 0)
    keyconv = product(dw_ref[...], wp_ref[...]) + vector_row(bp_ref)
    kc_ref[...] = keyconv.astype(BF16)
    span_in = (keyconv * query_ref[...].astype(F32)).astype(BF16)
    wide = jnp.broadcast_to(vector_row(bs_ref), (8, HEADS * KERNEL))
    order = jnp.where(tap_order(), 1.0, 0.0)
    shift = jnp.dot(wide, order, precision=lax.Precision.HIGHEST, preferred_element_type=F32)[0:1]
    lane = lax.broadcasted_iota(jnp.int32, (1, LANES), 1)
    used = (lane // TAP_STRIDE < KERNEL) & (lane % TAP_STRIDE < HEADS)
    shift = jnp.where(used, shift, NEGATIVE)
    logits = product(span_in, ordered_span(ws_ref)) + shift
    weights = jnp.exp(logits - tap_groups(logits, jnp.maximum))
    taps = weights / tap_groups(weights, jnp.add)
    taps_ref[...] = taps
    table = spread_table(half)
    total = jnp.zeros((SLOT, half), F32)
    for j in range(KERNEL):
        spread = product(tap_terms(taps, j), table)
        total = total + spread * ch[shifted_rows(j - REACH), :]
    conv_ref[...] = total.astype(BF16)


def head_scores(keys, query, side, outside):
    lane = lax.broadcasted_iota(jnp.int32, (1, LANES), 1)
    spare = lane == (1 - side) * HEAD_DIM
    rest = jnp.where(spare, outside, jnp.zeros_like(keys))
    keys = jnp.where(pair_mask(side), keys * BF16(0.125), rest)
    query = jnp.where(spare, jnp.ones_like(query), query)
    return right_product(keys, query)


def dead_rows(length):
    return jnp.where(slot_times(0, SLOT) < length, 0.0, NEGATIVE).astype(BF16)


def attend_kernel(info_ref, qkv_ref, conv_ref, ctx_ref, lse_ref, att):
    half = conv_ref.shape[1]
    outside = dead_rows(info_ref[HEAD + pl.program_id(0)])
    ones = jnp.ones((16, SLOT), BF16)

    def one_pair(pair):
        at = pair * LANES
        query = qkv_ref[:, pl.ds(at, LANES)]
        keys = qkv_ref[:, pl.ds(half + at, LANES)]
        values = transposed(qkv_ref[:, pl.ds(2 * half + at, LANES)])
        for side in range(2):
            scores = head_scores(keys, query, side, outside)
            highest = jnp.max(scores, axis=0, keepdims=True)
            weights = jnp.exp(scores - highest).astype(BF16)
            mine = jnp.concatenate([values[side * HEAD_DIM : (side + 1) * HEAD_DIM, :], ones], 0)
            both = product(mine, weights)
            summed = both[HEAD_DIM : HEAD_DIM + 1, :]
            att[pl.ds(at + side * HEAD_DIM, HEAD_DIM), :] = (
                both[:HEAD_DIM, :] * (1.0 / summed)
            )
            lse_ref[pl.ds(2 * pair + side, 1), :] = highest + jnp.log(summed)

    for pair in range(HEADS // 2):
        one_pair(pair)
    ctx_ref[:, :half] = transposed(att[...]).astype(BF16)
    ctx_ref[:, half:] = conv_ref[...]


def emit_chunks(sources, info_ref, keep_ref, send_ref):
    group, own = my_place(info_ref)
    count, columns = keep_ref.shape[0], keep_ref.shape[2]

    def one(position, carry):
        other = own ^ mask_at(info_ref, position)
        for ref, side in ((keep_ref, group), (send_ref, 1 - group)):
            pieces = []
            for source, rows, blocks in sources:
                first = jnp.minimum((side * count + other) * rows, source.shape[0] - rows)
                piece = source[pl.ds(pl.multiple_of(first, 8), rows), :]
                pieces += [piece[:, b * columns : (b + 1) * columns] for b in range(blocks)]
            ref[position] = jnp.concatenate(pieces, 0).astype(BF16)
        return carry

    lax.fori_loop(0, count, one, 0)


def middle_kernel(
    info_ref, ctx_ref, xs_ref, up_ref, wd_ref, bd_ref, g1_ref, b1_ref,
    ob_ref, g2_ref, b2_ref, *rest, pieces, order,
):
    weight_refs, rest = rest[: 2 * pieces], rest[2 * pieces :]
    (
        out_ref, gm_ref, gctx_ref, keep_ref, send_ref, grad_dense_ref, small_ref,
        w1, w2, bias, act, slope, low1, low2, first_t, grad_t, back, acc1, acc2, sems,
    ) = rest
    step = pl.program_id(0)
    last = pl.num_programs(0) - 1
    start, length = slot_bounds(info_ref, step)
    group = my_place(info_ref)[0]
    count, shard, part = w2.shape[1:]
    blocks = count // pieces
    span = count
    while span * shard > CHUNK_ROWS:
        span //= 2
    per = count // span
    wide = span * shard
    half = part
    width = 2 * half

    def copies():
        made = []
        for side in range(2):
            for piece in range(pieces):
                source = weight_refs[side * pieces + piece]
                at = pl.ds(piece * blocks, blocks)
                made.append((source.at[:, pl.ds(0, shard), :], w1.at[side, at, :, pl.ds(0, part)]))
                made.append((source.at[:, pl.ds(shard, shard), :], w2.at[side, at]))
                made.append(
                    (source.at[:, pl.ds(2 * shard, BIAS_ROWS), pl.ds(0, LANES)], bias.at[side, at])
                )
        return [pltpu.make_async_copy(a, b, sems.at[i]) for i, (a, b) in enumerate(made)]

    @pl.when(step == 0)
    def _():
        for copy in copies():
            copy.start()
        acc1[...] = jnp.zeros_like(acc1)
        acc2[...] = jnp.zeros_like(acc2)
        grad_dense_ref[...] = jnp.zeros_like(grad_dense_ref)
        small_ref[...] = jnp.zeros_like(small_ref)

    g1_row, g2_row = vector_row(g1_ref), vector_row(g2_ref)
    summed = product(ctx_ref[...], wd_ref[...]) + vector_row(bd_ref) + xs_ref[...].astype(F32)
    centred = summed - row_mean(summed)
    scale1 = lax.rsqrt(row_mean(centred * centred) + NORM_EPS)
    hat1 = centred * scale1
    normed1 = (hat1 * g1_row + vector_row(b1_ref)).astype(BF16)
    lane = lax.broadcasted_iota(jnp.int32, (SLOT, EXTRA), 1)
    ones = jnp.where(lane < 3, 1.0, 0.0).astype(BF16)
    for g in range(2):
        low1[g, :, :part] = normed1[:, g * part : (g + 1) * part]
        low1[g, :, part:] = ones
        first_t[g] = transposed(low1[g])[: first_t.shape[1], :]
        back[g] = jnp.zeros_like(back[g])

    @pl.when(step == 0)
    def _():
        for copy in copies():
            copy.wait()
        for side in range(2):
            for position in range(count):
                column = transposed(bias[side, position].astype(F32))
                column = jnp.concatenate(
                    [column, jnp.zeros((LANES, EXTRA - BIAS_ROWS), F32)], 1
                )
                w1[side, position, :, part:] = column[:shard].astype(BF16)

    def up_chunk(item, carry):
        r, c = item // per, item % per
        owner = group ^ r
        lanes = pl.ds(pl.multiple_of(c * wide, LANES), wide)
        some = pl.ds(c * span, span)
        first = w1[r, some].reshape(wide, part + EXTRA)
        inner = right_product(low1[owner], first)
        cdf = 0.5 * (1.0 + lax.erf(inner * ROOT_HALF))
        pdf = jnp.exp(-0.5 * inner * inner) * DENSITY
        active = (inner * cdf).astype(BF16)
        act[r, :, lanes] = active
        slope[r, :, lanes] = (cdf + inner * pdf).astype(BF16)
        back[owner] += product(active, w2[r, some].reshape(wide, part))
        return carry

    lax.fori_loop(0, 2 * per, up_chunk, 0)

    partial = jnp.concatenate([back[g] for g in range(2)], 1).astype(BF16).astype(F32)
    summed2 = partial + vector_row(ob_ref) + normed1.astype(F32)
    centred2 = summed2 - row_mean(summed2)
    scale2 = lax.rsqrt(row_mean(centred2 * centred2) + NORM_EPS)
    hat2 = centred2 * scale2
    out_ref[...] = (hat2 * g2_row + vector_row(b2_ref)).astype(BF16)

    upper = rows_to_slot(up_ref, start, length)

    def add_small(index, block):
        total = column_sum(block)
        for g in range(2):
            row = 2 * index + g
            small_ref[row : row + 1, :] += total[:, g * half : (g + 1) * half]

    add_small(0, upper * hat2)
    add_small(1, upper)
    lifted = upper * g2_row
    total2 = scale2 * (lifted - row_mean(lifted) - hat2 * row_mean(lifted * hat2))
    add_small(2, total2)
    grad_low = total2.astype(BF16)
    for g in range(2):
        low2[g] = grad_low[:, g * part : (g + 1) * part]
        grad_t[g] = transposed(low2[g])
        back[g] = jnp.zeros_like(back[g])

    def down_chunk(item, carry):
        r, c = item // per, item % per
        owner = group ^ r
        lanes = pl.ds(pl.multiple_of(c * wide, LANES), wide)
        some = pl.ds(c * span, span)
        grad_active = right_product(low2[owner], w2[r, some].reshape(wide, part))
        grad_inner = (grad_active * slope[r, :, lanes].astype(F32)).astype(BF16)
        acc2[r, :, lanes] += product(grad_t[owner], act[r, :, lanes])
        acc1[r, :, lanes] += product(first_t[owner], grad_inner)
        back[owner] += product(grad_inner, w1[r, some].reshape(wide, part + EXTRA)[:, :part])
        return carry

    lax.fori_loop(0, 2 * per, down_chunk, 0)

    grouped = jnp.concatenate([back[g] for g in range(2)], 1).astype(BF16).astype(F32)
    grad1 = grouped + total2
    add_small(3, grad1 * hat1)
    add_small(4, grad1)
    lifted = grad1 * g1_row
    mixed = scale1 * (lifted - row_mean(lifted) - hat1 * row_mean(lifted * hat1))
    mixed_low = mixed.astype(BF16)
    gm_ref[...] = mixed_low
    add_small(5, mixed_low.astype(F32))
    grad_dense_ref[...] += product(transposed(ctx_ref[...]), mixed_low)
    gctx_ref[...] = right_product(mixed_low, wd_ref[...]).astype(BF16)

    @pl.when(step == last)
    def _():
        for r, ref in enumerate((keep_ref, send_ref)):
            for c in range(per):
                lanes = slice(c * wide, (c + 1) * wide)
                first = transposed(acc1[r, :part, lanes]).astype(BF16)
                second = transposed(acc2[r, :, lanes]).astype(BF16)
                for p in range(span):
                    rows = slice(p * shard, (p + 1) * shard)
                    ref[order[c * span + p], 0:shard, :] = first[rows]
                    ref[order[c * span + p], shard : 2 * shard, :] = second[rows]
            row = acc1[r, part : part + 8, :]
            total = row.shape[1]
            for p in range(count):
                turned = pltpu.roll(row, (total - p * shard) % total, 1)
                ref[order[p], 2 * shard :, :] = turned[:, :part].astype(BF16)


def span_backward_kernel(
    info_ref, gctx_ref, xs_ref, query_ref, cs_ref, dw_ref, kc_ref, taps_ref, ws_ref, wp_ref, dense_ref,
    gs_ref, extra_ref, gk_ref, keep_ref, send_ref, small_ref,
    ch, gh, th, xh, sums, acc, *, chunk_rows,
):
    step = pl.program_id(0)
    last = pl.num_programs(0) - 1
    length = info_ref[HEAD + step]
    width = xs_ref.shape[1]
    half = width // 2

    @pl.when(step == 0)
    def _():
        acc[...] = jnp.zeros_like(acc)
        sums[...] = jnp.zeros_like(sums)
        small_ref[...] = jnp.zeros_like(small_ref)

    inside = slot_times(0, SLOT) < length
    put_with_edges(ch, cs_ref[...].astype(F32))
    grad_conv = gctx_ref[...].astype(F32)
    put_with_edges(gh, grad_conv)
    taps = taps_ref[...]
    put_with_edges(th, taps)
    table, picker = spread_table(half), gather_table(half)
    grad_taps = jnp.zeros((SLOT, LANES), F32)
    grad_source = jnp.zeros((SLOT, half), F32)
    for j in range(KERNEL):
        moved = grad_conv * ch[shifted_rows(j - REACH), :]
        here = product(moved.astype(BF16), picker)
        grad_taps = grad_taps + (here if j == 0 else pltpu.roll(here, j * TAP_STRIDE, 1))
        back = shifted_rows(REACH - j)
        grad_source = grad_source + product(tap_terms(th[back, :], j), table) * gh[back, :]
    grad_source = jnp.where(inside, grad_source, 0.0).astype(BF16)
    gs_ref[...] = grad_source
    small_ref[130:131, :] += column_sum(grad_source.astype(F32))

    query = query_ref[...].astype(F32)
    keyconv = kc_ref[...].astype(F32)
    grad_logits = taps * (grad_taps - tap_groups(taps * grad_taps, jnp.add))
    grad_logits = grad_logits.astype(BF16)
    small_ref[129:130, :LANES] += column_sum(grad_logits.astype(F32))
    span_in = (keyconv * query).astype(BF16)
    small_ref[0:TAPS_ROW, :] += product(transposed(grad_logits)[0:TAPS_ROW, :], span_in)
    grad_span = right_product(grad_logits, ordered_span(ws_ref)).astype(BF16).astype(F32)
    extra_ref[...] = (grad_span * keyconv).astype(BF16)
    grad_key = (grad_span * query).astype(BF16)
    gk_ref[...] = grad_key
    small_ref[128:129, :] += column_sum(grad_key.astype(F32))
    acc[:, 0:half] += product(transposed(dw_ref[...]), grad_key)
    acc[:, half:] += product(transposed(xs_ref[...]), grad_source)
    put_with_edges(xh, right_product(grad_key, wp_ref[...]).astype(BF16).astype(F32))

    def depth_chunk(c, carry):
        lanes = pl.ds(pl.multiple_of(c * LANES, LANES), LANES)
        for j in range(KERNEL):
            total = jnp.zeros((GROUP, LANES), F32)
            for first in range(0, SLOT, ROWS):
                own = xs_ref[first : first + ROWS, lanes].astype(F32)
                moved = xh[shifted_rows(REACH - j, first, ROWS), lanes] * own
                total = total + jnp.sum(moved.reshape(ROWS // GROUP, GROUP, LANES), axis=0)
            sums[j, :, lanes] += total
        return carry

    lax.fori_loop(0, width // LANES, depth_chunk, 0)

    @pl.when(step == last)
    def _():
        for j in range(KERNEL):
            total = column_sum(sums[j])
            for side in range(2):
                row = TAPS_ROW + side * KERNEL + j
                small_ref[row : row + 1, :] = total[:, side * half : (side + 1) * half]
        sources = ((acc, chunk_rows, 2), (dense_ref, chunk_rows, 2))
        emit_chunks(sources, info_ref, keep_ref, send_ref)


def input_kernel(
    info_ref, gm_ref, flat_ref, gs_ref, gk_ref, wq_ref, wk_ref, wv_ref, wc_ref, wp_ref, dk_ref,
    *rest,
):
    rows_ref, base, gh, block = rest[-4:]
    step = pl.program_id(0)
    start, length = slot_bounds(info_ref, step)
    half = gs_ref.shape[1]

    @pl.when(step == 0)
    def _():
        rows_ref[...] = jnp.zeros_like(rows_ref)

    put_with_edges(gh, right_product(gk_ref[...], wp_ref[...]).astype(BF16).astype(F32))
    total = gm_ref[...].astype(F32) + right_product(gs_ref[...], wc_ref[...])
    for third, ref in enumerate((wq_ref, wk_ref, wv_ref)):
        total = total + right_product(flat_ref[:, third * half : (third + 1) * half], ref[...])
    base[...] = total

    def depth_chunk(c, carry):
        lanes = pl.ds(pl.multiple_of(c * LANES, LANES), LANES)
        for first in range(0, SLOT, ROWS):
            inner = slice(first, first + ROWS)
            total = base[inner, lanes]
            for j in range(KERNEL):
                total = total + dk_ref[j : j + 1, lanes] * gh[shifted_rows(REACH - j, first, ROWS), lanes]
            block[inner, lanes] = total.astype(BF16)
        return carry

    lax.fori_loop(0, half // LANES, depth_chunk, 0)
    slot_to_rows(rows_ref, start, length, block[...])


def attend_backward_kernel(
    info_ref, gctx_ref, ctx_ref, xs_ref, qkv_ref, lse_ref, extra_ref, *rest, first_slot, small, chunks
):
    if chunks is None:
        flat_ref, sum_ref, own_ref, gqt = rest
    else:
        smallm_ref, smallc_ref, _, before_ref, own_before_ref = rest[:5]
        flat_ref, keep_ref, send_ref, gqt, sum_ref, own_ref, small_ref = rest[5:]
    step = pl.program_id(0)
    half = gctx_ref.shape[1]

    @pl.when(step == 0)
    def _():
        if chunks is None:
            sum_ref[...] = jnp.zeros_like(sum_ref)
            own_ref[...] = jnp.zeros_like(own_ref)
        else:
            sum_ref[...] = before_ref[...]
            own_ref[...] = own_before_ref[...]

    outside = dead_rows(info_ref[HEAD + step + first_slot])

    def one_pair(pair):
        at = pair * LANES
        here, there, third = (pl.ds(k * half + at, LANES) for k in range(3))
        query_pair = qkv_ref[:, here]
        keys = qkv_ref[:, there]
        values = qkv_ref[:, third]
        keys_t = transposed(keys)
        grad_pair = gctx_ref[:, here]
        dots = transposed(grad_pair.astype(F32) * ctx_ref[:, here].astype(F32))
        grad_keys, grad_values = [], []
        for side in range(2):
            mask = pair_mask(side)
            rows = slice(side * HEAD_DIM, (side + 1) * HEAD_DIM)
            scores = head_scores(keys, query_pair, side, outside)
            probs = jnp.exp(scores - lse_ref[pl.ds(2 * pair + side, 1), :])
            grad_probs = right_product(jnp.where(mask, values, jnp.zeros_like(values)), grad_pair)
            weighted = column_sum(dots[rows, :])
            grad_scores = (probs * (grad_probs - weighted)).astype(BF16)
            grad_keys.append(product(grad_scores, query_pair))
            grad_values.append(product(probs.astype(BF16), grad_pair))
            gqt[pl.ds(at + side * HEAD_DIM, HEAD_DIM), :] = product(
                keys_t[rows, :], grad_scores
            )
        first = pair_mask(0)
        flat_ref[:, there] = (jnp.where(first, grad_keys[0], grad_keys[1]) * 0.125).astype(BF16)
        flat_ref[:, third] = jnp.where(first, grad_values[0], grad_values[1]).astype(BF16)

    for pair in range(HEADS // 2):
        one_pair(pair)
    flat_ref[:, :half] = (transposed(gqt[...]) * 0.125 + extra_ref[...].astype(F32)).astype(BF16)
    sum_ref[...] += product(transposed(xs_ref[...]), flat_ref[...])
    for third in range(3):
        own_ref[third : third + 1, :] += column_sum(
            flat_ref[:, third * half : (third + 1) * half].astype(F32)
        )
    if chunks is None:
        return

    @pl.when(step == pl.num_programs(0) - 1)
    def _():
        small_ref[: smallm_ref.shape[0], :] = smallm_ref[...]
        small_ref[SPAN_ROW : SPAN_ROW + smallc_ref.shape[0], :] = smallc_ref[...]
        small_ref[OWN_ROW : OWN_ROW + own_ref.shape[0], :] = own_ref[...]
        sources = ((sum_ref, chunks, 3), (small_ref, small, 1))
        emit_chunks(sources, info_ref, keep_ref, send_ref)


def restore_kernel(info_ref, slot_ref, rows_ref):
    step = pl.program_id(0)
    start, length = slot_bounds(info_ref, step)

    @pl.when(step == 0)
    def _():
        rows_ref[...] = jnp.zeros_like(rows_ref)

    slot_to_rows(rows_ref, start, length, slot_ref[...])


def assemble_kernel(info_ref, *refs, layout):
    sources, outs, small_ref = refs[:2], refs[2:-1], refs[-1]
    group, own = my_place(info_ref)
    count, _, columns = sources[0].shape

    def one(position, carry):
        for core, source in enumerate(sources):
            index = (group ^ core) * count + (own ^ mask_at(info_ref, position))
            chunk = source[position].astype(F32)
            at, place = 0, 0
            for rows, wide in layout:
                if wide == 0:
                    small_ref[pl.ds(pl.multiple_of(index * rows, 8), rows), :] = chunk[at : at + rows]
                    at += rows
                    continue
                for block in range(wide):
                    outs[place][index, :, block * columns : (block + 1) * columns] = chunk[at : at + rows]
                    at += rows
                place += 1
        return carry

    lax.fori_loop(0, count, one, 0)
    place = sum(1 for _, wide in layout if wide)
    if place == len(layout):
        return
    vectors, (depth_ref, span_ref, bias_ref) = outs[place : place + 10], outs[place + 10 :]
    for i in range(6):
        pair = [small_ref[2 * i + g : 2 * i + g + 1, :] for g in range(2)]
        vectors[i][...] = jnp.concatenate(pair, 1).reshape(2 * columns)
    for i, row in enumerate((OWN_ROW, OWN_ROW + 2, SPAN_ROW + 128, SPAN_ROW + 130)):
        vectors[6 + i][...] = small_ref[row : row + 1, :].reshape(columns)
    first = SPAN_ROW + TAPS_ROW
    for g in range(2):
        rows = small_ref[first + g * KERNEL : first + (g + 1) * KERNEL, :]
        depth_ref[:, g * columns : (g + 1) * columns] = rows
    order = jnp.where(tap_order(), 1.0, 0.0).astype(BF16)
    span_ref[...] = product(order, small_ref[SPAN_ROW : SPAN_ROW + LANES, :].astype(BF16))
    bias = small_ref[SPAN_ROW + 129 : SPAN_ROW + 130, :LANES]
    bias = jnp.broadcast_to(bias, (16, LANES)).astype(BF16)
    bias_ref[...] = right_product(bias, order)[0:1].reshape(HEADS * KERNEL)


def resident(shape):
    zeros = (0,) * len(shape)
    return pl.BlockSpec(tuple(shape), lambda *_: zeros, pipeline_mode=pl.Buffered(1))


def slot_block(columns, rows=SLOT, column=0):
    return pl.BlockSpec((None, rows, columns), lambda i: (i, 0, column))


SCALARS = pl.BlockSpec(memory_space=pltpu.SMEM)
ANYWHERE = pl.BlockSpec(memory_space=pl.ANY)
LIMIT = 60 * 1024 * 1024


def shape_of(*dims, dtype=F32):
    return jax.ShapeDtypeStruct(dims, dtype)


def cost(flops, nbytes):
    return pl.CostEstimate(flops=int(flops), bytes_accessed=int(nbytes), transcendentals=0)


PARAMS = pltpu.CompilerParams(vmem_limit_bytes=LIMIT)
LARGE = pltpu.CompilerParams(vmem_limit_bytes=LIMIT + 3 * 1024 * 1024)
RATE = 1.15e9


def busy(us):
    return cost(us * RATE, us * 1e6)


def run_project(info, slots, x, *rest):
    total, width = x.shape
    half = width // 2
    return pl.pallas_call(
        project_kernel,
        grid=(slots,),
        in_specs=[SCALARS] + [resident(a.shape) for a in (x,) + rest],
        out_specs=[slot_block(width), slot_block(3 * half), slot_block(half)],
        out_shape=[
            shape_of(slots, SLOT, width, dtype=BF16),
            shape_of(slots, SLOT, 3 * half, dtype=BF16),
            shape_of(slots, SLOT, half, dtype=BF16),
        ],
        compiler_params=PARAMS,
        cost_estimate=busy(10),
        name="project",
    )(info, x, *rest)


def run_convolve(info, xs, qkv, cs, *rest):
    slots, _, width = xs.shape
    half = width // 2
    return pl.pallas_call(
        convolve_kernel,
        grid=(slots,),
        in_specs=[SCALARS, slot_block(width), slot_block(half), slot_block(half)]
        + [resident(a.shape) for a in rest],
        out_specs=[slot_block(width), slot_block(half), slot_block(LANES), slot_block(half)],
        out_shape=[
            shape_of(slots, SLOT, width, dtype=BF16),
            shape_of(slots, SLOT, half, dtype=BF16),
            shape_of(slots, SLOT, LANES),
            shape_of(slots, SLOT, half, dtype=BF16),
        ],
        scratch_shapes=[
            pltpu.VMEM((SLOT + 2 * EDGE, width), F32),
            pltpu.VMEM((SLOT + 2 * EDGE, half), F32),
        ],
        compiler_params=PARAMS,
        cost_estimate=busy(15),
        name="convolve",
    )(info, xs, qkv, cs, *rest)


def run_attend(info, qkv, conv):
    slots, _, half = conv.shape
    return pl.pallas_call(
        attend_kernel,
        grid=(slots,),
        in_specs=[SCALARS, slot_block(3 * half), slot_block(half)],
        out_specs=[slot_block(2 * half), slot_block(SLOT, 8)],
        out_shape=[shape_of(slots, SLOT, 2 * half, dtype=BF16), shape_of(slots, 8, SLOT)],
        scratch_shapes=[pltpu.VMEM((half, SLOT), F32)],
        compiler_params=PARAMS,
        cost_estimate=busy(16),
        name="attend",
    )(info, qkv, conv)


def run_middle(info, ctx, xs, upstream, vectors, wd, weights, shard, count):
    bits = offset_masks(digits_of(count, RADIX))
    order = [bits.index(mask) for mask in offset_masks(digits_of(count))]
    slots, _, width = xs.shape
    half = width // 2
    hidden = count * shard
    pieces = len(weights) // 2
    bd, g1, b1, ob, g2, b2 = vectors
    rows = 2 * shard + BIAS_ROWS
    return pl.pallas_call(
        functools.partial(middle_kernel, pieces=pieces, order=order),
        grid=(slots,),
        in_specs=[SCALARS, slot_block(width), slot_block(width)]
        + [resident(a.shape) for a in (upstream, wd, bd, g1, b1, ob, g2, b2)]
        + [ANYWHERE] * len(weights),
        out_specs=[slot_block(width), slot_block(width), slot_block(width)]
        + [resident((count, rows, half))] * 2
        + [resident((width, width)), resident((16, half))],
        out_shape=[
            shape_of(slots, SLOT, width, dtype=BF16),
            shape_of(slots, SLOT, width, dtype=BF16),
            shape_of(slots, SLOT, width, dtype=BF16),
        ]
        + [shape_of(count, rows, half, dtype=BF16)] * 2
        + [shape_of(width, width), shape_of(16, half)],
        scratch_shapes=[
            pltpu.VMEM((2, count, shard, half + EXTRA), BF16),
            pltpu.VMEM((2, count, shard, half), BF16),
            pltpu.VMEM((2, count, BIAS_ROWS, LANES), BF16),
            pltpu.VMEM((2, SLOT, hidden), BF16),
            pltpu.VMEM((2, SLOT, hidden), BF16),
            pltpu.VMEM((2, SLOT, half + EXTRA), BF16),
            pltpu.VMEM((2, SLOT, half), BF16),
            pltpu.VMEM((2, half + 16, SLOT), BF16),
            pltpu.VMEM((2, half, SLOT), BF16),
            pltpu.VMEM((2, SLOT, half), F32),
            pltpu.VMEM((2, half + 16, hidden), F32),
            pltpu.VMEM((2, half, hidden), F32),
            pltpu.SemaphoreType.DMA((6 * pieces,)),
        ],
        compiler_params=LARGE,
        cost_estimate=busy(64),
        name="feed_forward",
    )(info, ctx, xs, upstream, wd, bd, g1, b1, ob, g2, b2, *weights)


def run_span_backward(info, gctx, xs, qkv, cs, dw, kc, taps, ws, wp, dense, count, chunk_rows):
    slots, _, width = xs.shape
    half = width // 2
    return pl.pallas_call(
        functools.partial(span_backward_kernel, chunk_rows=chunk_rows),
        grid=(slots,),
        in_specs=[
            SCALARS, slot_block(half, column=1), slot_block(width), slot_block(half),
            slot_block(half), slot_block(width), slot_block(half), slot_block(LANES),
            resident(ws.shape), resident(wp.shape), resident(dense.shape),
        ],
        out_specs=[slot_block(half)] * 3
        + [resident((count, 4 * chunk_rows, half))] * 2
        + [resident((136, half))],
        out_shape=[
            shape_of(slots, SLOT, half, dtype=BF16),
            shape_of(slots, SLOT, half, dtype=BF16),
            shape_of(slots, SLOT, half, dtype=BF16),
        ]
        + [shape_of(count, 4 * chunk_rows, half, dtype=BF16)] * 2
        + [shape_of(136, half)],
        scratch_shapes=[
            pltpu.VMEM((SLOT + 2 * EDGE, half), F32),
            pltpu.VMEM((SLOT + 2 * EDGE, half), F32),
            pltpu.VMEM((SLOT + 2 * EDGE, LANES), F32),
            pltpu.VMEM((SLOT + 2 * EDGE, width), F32),
            pltpu.VMEM((KERNEL, GROUP, width), F32),
            pltpu.VMEM((width, width), F32),
        ],
        compiler_params=PARAMS,
        cost_estimate=busy(23),
        name="span_backward",
    )(info, gctx, xs, qkv, cs, dw, kc, taps, ws, wp, dense)


def run_attend_backward(info, gctx, ctx, xs, qkv, lse, extra, count, chunk_rows, before=None, smalls=()):
    slots, _, width = xs.shape
    half = width // 2
    ending = before is not None
    first = 1 if ending else 0
    small_rows = small_chunk(count)
    rows = 3 * chunk_rows + small_rows

    def block(columns, rows=SLOT):
        return pl.BlockSpec((None, rows, columns), lambda i: (i + first, 0, 0))

    more = list(smalls) + list(before) if ending else []
    more_specs = [resident(a.shape) for a in more]
    if ending:
        more_specs[len(smalls)] = ANYWHERE
    sums = [(width, 3 * half), (8, half)]
    return pl.pallas_call(
        functools.partial(
            attend_backward_kernel, first_slot=first, small=small_rows, chunks=chunk_rows if ending else None
        ),
        grid=(slots - 1 if ending else 1,),
        in_specs=[SCALARS, block(half), block(half), block(width), block(3 * half), block(SLOT, 8), block(half)]
        + more_specs,
        out_specs=[block(3 * half)]
        + ([resident((count, rows, half))] * 2 if ending else [resident(d) for d in sums]),
        out_shape=[shape_of(slots, SLOT, 3 * half, dtype=BF16)]
        + ([shape_of(count, rows, half, dtype=BF16)] * 2 if ending else [shape_of(*d) for d in sums]),
        scratch_shapes=[pltpu.VMEM((half, SLOT), F32)]
        + ([pltpu.VMEM(d, F32) for d in sums + [(SMALL_ROWS, half)]] if ending else []),
        input_output_aliases={7 + len(smalls): 0} if ending else {},
        compiler_params=PARAMS,
        cost_estimate=busy(14 if ending else 7),
        name="attend_backward",
    )(info, gctx, ctx, xs, qkv, lse, extra, *more)


def run_input(info, gm, flat, gs, gk, weights, dk, total, before=None):
    slots, _, width = gm.shape
    half = width // 2
    side = 0 if before is None else 1
    more = [] if before is None else [before]
    rows = pl.BlockSpec((half, half), lambda i: (side, 0))
    return pl.pallas_call(
        input_kernel,
        grid=(slots,),
        in_specs=[
            SCALARS, slot_block(half, column=side), slot_block(3 * half), slot_block(half),
            slot_block(half),
        ]
        + [rows] * len(weights)
        + [pl.BlockSpec((KERNEL, half), lambda i: (0, side))]
        + [ANYWHERE] * len(more),
        out_specs=pl.BlockSpec((total, half), lambda i: (0, side)),
        out_shape=shape_of(total, width, dtype=BF16),
        scratch_shapes=[
            pltpu.VMEM((SLOT, half), F32),
            pltpu.VMEM((SLOT + 2 * EDGE, half), F32),
            pltpu.VMEM((SLOT, half), BF16),
        ],
        input_output_aliases={6 + len(weights): 0} if more else {},
        compiler_params=PARAMS,
        cost_estimate=busy(8),
        name="input_gradient",
    )(info, gm, flat, gs, gk, *weights, dk, *more)


def run_restore(info, block, total):
    slots, _, width = block.shape
    return pl.pallas_call(
        restore_kernel,
        grid=(slots,),
        in_specs=[SCALARS, slot_block(width)],
        out_specs=resident((total, width)),
        out_shape=shape_of(total, width, dtype=BF16),
        compiler_params=PARAMS,
        cost_estimate=busy(4),
        name="restore_rows",
    )(info, block)


def run_assemble(info, sources, layout):
    count, _, half = sources[0].shape
    width, taps = 2 * half, HEADS * KERNEL
    shapes = [(2 * count, rows, wide * half) for rows, wide in layout if wide]
    whole = len(shapes)
    if whole < len(layout):
        shapes += [(width,)] * 6 + [(half,)] * 4 + [(KERNEL, width), (taps, half), (taps,)]
    outs = pl.pallas_call(
        functools.partial(assemble_kernel, layout=layout),
        in_specs=[SCALARS] + [pl.BlockSpec(memory_space=pltpu.VMEM)] * len(sources),
        out_specs=[pl.BlockSpec(memory_space=pltpu.VMEM)] * len(shapes),
        out_shape=[shape_of(*s) for s in shapes],
        scratch_shapes=[pltpu.VMEM((2 * count * small_chunk(count), half), F32)],
        compiler_params=PARAMS,
        cost_estimate=busy(3),
        name="assemble",
    )(info, *sources)
    return [o.reshape(2 * count * o.shape[1], -1) for o in outs[:whole]] + list(outs[whole:])


def small_chunk(count):
    return round_up(-(-SMALL_ROWS // (2 * count)), 8)


def swap_groups(block):
    return lax.ppermute(block, "grp", [(0, 1), (1, 0)])


def send_across(block, count, offset):
    return lax.ppermute(block, "dp", [(i, i ^ offset) for i in range(count)])


def tree_sum(parts):
    parts = [p.astype(F32) for p in parts]
    while len(parts) > 1:
        parts = [parts[i] + parts[i + 1] for i in range(0, len(parts), 2)]
    return parts[0].astype(BF16)


def tie(value, *others):
    return lax.optimization_barrier((value, others))[0]


def advance(done, *sums, held=()):
    both = sums + tuple(held)
    arrived = lax.optimization_barrier((done, [s.current for s in both]))[1]
    for one, current in zip(both, arrived):
        one.current = current
    sent = []
    for one in sums:
        sent += one.step()
    return sent


class ChunkSum:
    def __init__(self, keep, send, count, digits=None):
        self.count, self.digits = count, digits or digits_of(count)
        self.current, self.stage = [keep, swap_groups(send)], 0

    def step(self):
        if self.stage == len(self.digits):
            return []
        stride, radix = self.digits[self.stage]
        size = self.current[0].shape[0] // radix
        parts = [
            tree_sum([p[s * size : (s + 1) * size] for p in self.current]) for s in range(radix)
        ]
        self.current = [parts[0]] + [
            send_across(parts[s], self.count, s * stride) for s in range(1, radix)
        ]
        self.stage += 1
        return parts

    def finish(self):
        while self.stage < len(self.digits):
            self.step()
        return tree_sum(self.current)


class Gather:
    def __init__(self, own, count, digits):
        self.count, self.digits, self.stage, self.current = count, digits, 0, [own]

    def step(self):
        own = jnp.concatenate(self.current, 0)
        if self.stage == len(self.digits):
            self.current = [own]
            return [own]
        stride, radix = self.digits[self.stage]
        self.current = [own] + [send_across(own, self.count, s * stride) for s in range(1, radix)]
        self.stage += 1
        return [own]

    def finish(self, wanted=None):
        while self.stage < len(self.digits):
            self.step()
        whole = jnp.concatenate(self.current, 0)
        if wanted is None:
            return whole
        masks = [0]
        for stride, radix in self.digits:
            masks = [digit * stride ^ mask for digit in range(radix) for mask in masks]
        places = [masks.index(mask) for mask in wanted]
        return jnp.concatenate([whole[p : p + 1] for p in places], 0)


def round_up(value, unit):
    return -(-value // unit) * unit


def weight_shard(inter_weight, inter_bias, down_weight):
    columns = inter_weight.shape[2]
    shard = round_up(columns, 16)
    half = down_weight.shape[2]
    pad = ((0, shard - columns), (0, 0))
    first = jnp.pad(jnp.transpose(inter_weight[0]), pad)
    second = jnp.pad(down_weight[0], pad)
    rest, terms = inter_bias, []
    for _ in range(3):
        term = lax.reduce_precision(rest, 8, 7)
        terms.append(term)
        rest = rest - term
    terms = jnp.concatenate(terms, 0).astype(BF16)
    terms = jnp.pad(terms, ((0, BIAS_ROWS - 3), (0, half - columns)))
    return jnp.concatenate([first, second, terms], 0)[None], shard


def on_device(
    count, layer_input, lengths, query_weight, query_bias, key_weight, value_weight, value_bias,
    depth_kernel, point_weight, point_bias, span_weight, span_bias, conv_out_weight,
    conv_out_bias, dense_weight, dense_bias, first_gain, first_shift, inter_weight, inter_bias,
    grouped_down_weight, output_bias, second_gain, second_shift, upstream_grad,
):
    total, width = layer_input.shape
    half = width // 2
    slots = lengths.shape[1]
    chunk_rows = round_up(-(-width // (2 * count)), 8)
    info = jnp.concatenate(
        [
            lax.axis_index("grp").astype(jnp.int32).reshape(1),
            lax.axis_index("dp").astype(jnp.int32).reshape(1),
            lengths[0],
            jnp.array(offset_masks(digits_of(count)), jnp.int32),
        ]
    )
    own_weights, shard = weight_shard(inter_weight, inter_bias, grouped_down_weight)
    digits = digits_of(count)
    block = own_weights
    for stride, radix in reversed(digits[1:]):
        block = [block] + [send_across(block, count, s * stride) for s in range(1, radix)]
        if stride == digits[1][0]:
            break
        block = jnp.concatenate(block, 0)

    xs, qkv, cs = run_project(
        info, slots, tie(layer_input, own_weights), query_weight, key_weight, value_weight,
        conv_out_weight, query_bias, value_bias, conv_out_bias,
    )
    block = jnp.concatenate(tie(block, xs), 0)
    stride, radix = digits[0]
    block = [block] + [send_across(block, count, s * stride) for s in range(1, radix)]
    dw, kc, taps, conv = run_convolve(
        info, tie(xs, block[0]), qkv, cs, depth_kernel, point_weight, point_bias, span_weight, span_bias
    )
    ctx, lse = run_attend(info, qkv, conv)
    early = swap_groups(block[0])
    block = block[:1] + tie(block[1:], ctx)
    weights = block + [early] + [swap_groups(b) for b in block[1:]]
    vectors = (dense_bias, first_gain, first_shift, output_bias, second_gain, second_shift)
    out_slots, gm, gctx, keep, send, dense, small_m = run_middle(
        info, ctx, xs, upstream_grad, vectors, dense_weight, weights, shard, count
    )
    ffn_sum = ChunkSum(keep, send, count, digits_of(count, RADIX))
    layer_out = run_restore(info, tie(out_slots, send), total)
    sent = advance(layer_out, ffn_sum)
    gs, extra, gk, keep_c, send_c, small_c = run_span_backward(
        info, tie(gctx, sent), xs, qkv, cs, dw, kc, taps, span_weight, point_weight, dense, count, chunk_rows
    )
    span_sum = ChunkSum(keep_c, send_c, count)
    sent = advance(gs, ffn_sum)
    part = run_attend_backward(
        info, tie(gctx, send_c, sent), ctx, xs, qkv, lse, extra, count, chunk_rows
    )
    sent = advance(part, span_sum, ffn_sum)
    flat, keep_a, send_a = run_attend_backward(
        info, tie(gctx, sent), ctx, xs, qkv, lse, extra, count, chunk_rows, part, [small_m, small_c]
    )
    mixer_sum = ChunkSum(keep_a, send_a, count)
    sent = advance(flat, span_sum, held=[ffn_sum])
    matrices = [query_weight, key_weight, value_weight, conv_out_weight, point_weight]
    in_half = run_input(info, tie(gm, sent, send_a), flat, gs, gk, matrices, depth_kernel, total)
    digits, bits = digits_of(count), digits_of(count, RADIX)
    sent = advance(in_half, mixer_sum, held=[span_sum])
    wanted = offset_masks(digits[1:])
    span_all = Gather(span_sum.finish(), count, bits[:0:-1])
    sent += span_all.step()
    in_grad = run_input(info, tie(gm, sent), flat, gs, gk, matrices, depth_kernel, total, in_half)
    sent = advance(in_grad, mixer_sum, span_all)
    mixer_own = tie(mixer_sum.finish(), sent)
    span_plane = Gather(span_all.finish(wanted), count, digits[:1])
    mixer_all = Gather(mixer_own, count, bits[:0:-1])
    sent = mixer_all.step() + span_plane.step()
    for _ in bits[2:]:
        sent = advance(sent, mixer_all)
    advance(sent, held=[mixer_all, span_plane])
    mixer_plane = Gather(mixer_all.finish(wanted), count, digits[:1])
    sent = mixer_plane.step()
    span_all = tie(span_plane.finish(), sent)
    span_other = swap_groups(span_all)
    ffn = ffn_sum.finish()
    rows = chunk_rows
    span_outs = run_assemble(info, [span_all, span_other], ((rows, 1), (rows, 1), (rows, 2)))
    mixer_all = mixer_plane.finish()
    mixer_outs = run_assemble(
        info, [mixer_all, swap_groups(mixer_all)], ((rows, 1),) * 3 + ((small_chunk(count), 0),)
    )
    outs = mixer_outs[:3] + span_outs + mixer_outs[3:]
    grad_query, grad_key, grad_value, grad_point, grad_conv, grad_dense = [g[:width] for g in outs[:6]]
    vectors, (grad_depth, grad_span, grad_span_bias) = outs[6:16], outs[16:]
    ffn = ffn.astype(F32)
    columns = inter_weight.shape[2]
    return (
        layer_out,
        in_grad,
        grad_query,
        vectors[6],
        grad_key,
        grad_value,
        vectors[7],
        grad_depth,
        grad_point,
        vectors[8],
        jnp.transpose(grad_span),
        grad_span_bias,
        grad_conv,
        vectors[9],
        grad_dense,
        vectors[5],
        vectors[3],
        vectors[4],
        jnp.transpose(ffn[:, :columns], (0, 2, 1)),
        ffn[:, 2 * shard, :columns],
        ffn[:, shard : shard + columns],
        vectors[2],
        vectors[0],
        vectors[1],
    )


def solution(mesh):
    rows = P(("grp", "dp"), None)
    one = P()
    return jax.shard_map(
        functools.partial(on_device, mesh.shape["dp"]),
        mesh=mesh,
        in_specs=(rows, rows) + (one,) * 16
        + (P("grp", None, "dp"), P("grp", "dp"), P("grp", "dp", None)) + (one,) * 3 + (rows,),
        out_specs=(rows, rows) + (one,) * 16
        + (P("grp", None, "dp"), P("grp", "dp"), P("grp", "dp", None)) + (one,) * 3,
        check_vma=False,
    )
```

```python
import functools

import jax
import jax.numpy as jnp
from jax import lax
from jax.experimental import pallas as pl
from jax.experimental.pallas import tpu as pltpu
from jax.sharding import PartitionSpec as P

HEADS = 6
HEAD_DIM = 64
KERNEL = 9
REACH = KERNEL // 2
SLOT = 512
SLOTS = 3
GROUP = 8
SPAN = SLOT // GROUP
EDGE = REACH * GROUP
LANES = 128
TAP_STRIDE = 8
CHUNK_ROWS = 1536
EXTRA = 128
ROWS = 128
SPAN_ROW = 16
TAPS_ROW = 80
OWN_ROW = 152
SMALL_ROWS = 160
BIAS_ROWS = 8
RADIX = 4
NEGATIVE = -1e30
NORM_EPS = 1e-12
ROOT_HALF = 0.7071067811865476
DENSITY = 0.3989422804014327
BF16 = jnp.bfloat16
F32 = jnp.float32


def product(left, right):
    return jnp.dot(left, right, preferred_element_type=F32)


def right_product(left, right):
    return lax.dot_general(left, right, (((1,), (1,)), ((), ())), preferred_element_type=F32)


def transposed(block):
    return jnp.transpose(block, (1, 0))


def column_sum(block):
    return jnp.sum(block, axis=0, keepdims=True)


def row_mean(block):
    return jnp.mean(block, axis=-1, keepdims=True)


def tap_groups(block, combine):
    step = TAP_STRIDE
    while step < LANES:
        block = combine(block, pltpu.roll(block, step, 1))
        step *= 2
    return block


def high_low(block):
    high = block.astype(BF16)
    low = (block - high.astype(F32)).astype(BF16)
    return high, low


HEAD = 2


def slot_bounds(info_ref, index):
    start = jnp.int32(0)
    for other in range(SLOTS - 1):
        start = start + jnp.where(index > other, info_ref[HEAD + other], 0)
    return start, info_ref[HEAD + index]


def my_place(info_ref):
    return info_ref[0], info_ref[1]


def mask_at(info_ref, position):
    return info_ref[HEAD + SLOTS + position]


def slot_times(first, count):
    row = lax.broadcasted_iota(jnp.int32, (count, 1), 0) + first
    return (row & (GROUP - 1)) * SPAN + row // GROUP


def rows_to_slot(source_ref, start, length):
    total = source_ref.shape[0]
    window = SLOT + 16
    base = pl.multiple_of(jnp.minimum(start // 16 * 16, total - window), 16)
    source = source_ref[pl.ds(base, window), :]
    col = lax.broadcasted_iota(jnp.int32, (1, window), 1) + (base - start)
    time = slot_times(0, SLOT)
    time = jnp.where(time < length, time, -SLOT * SLOT)
    pick = jnp.where(col == time, 1.0, 0.0).astype(BF16)
    return product(pick, source)


def slot_to_rows(target_ref, start, length, block):
    total = target_ref.shape[0]
    window = SLOT + 16
    base = pl.multiple_of(jnp.minimum(start // 16 * 16, total - window), 16)
    col = lax.broadcasted_iota(jnp.int32, (1, SLOT), 1)
    time = lax.broadcasted_iota(jnp.int32, (window, 1), 0) + (base - start)
    row = (time & (SPAN - 1)) * GROUP + (time // SPAN)
    row = jnp.where((time >= 0) & (time < length), row, -1)
    pick = jnp.where(col == row, 1.0, 0.0).astype(BF16)
    target_ref[pl.ds(base, window), :] += product(pick, block).astype(BF16)


def put_with_edges(ref, block):
    ref[EDGE : EDGE + SLOT, :] = block
    sub = lax.broadcasted_iota(jnp.int32, (GROUP, 1), 0)
    for k in range(REACH):
        before = block[SLOT - EDGE + k * GROUP : SLOT - EDGE + (k + 1) * GROUP, :]
        before = jnp.where(sub == 0, 0.0, pltpu.roll(before, 1, 0))
        ref[k * GROUP : (k + 1) * GROUP, :] = before
        after = block[k * GROUP : (k + 1) * GROUP, :]
        after = jnp.where(sub == GROUP - 1, 0.0, pltpu.roll(after, GROUP - 1, 0))
        ref[EDGE + SLOT + k * GROUP : EDGE + SLOT + (k + 1) * GROUP, :] = after


def shifted_rows(offset, first=0, count=SLOT):
    at = EDGE + offset * GROUP + first
    return slice(at, at + count)


def pair_mask(half):
    lane = lax.broadcasted_iota(jnp.int32, (1, LANES), 1)
    return (lane // HEAD_DIM) == half


def digits_of(count, wide=64):
    digits, stride = [], 1
    while stride < count:
        radix = RADIX if (count // stride) % RADIX == 0 and stride < wide else 2
        digits.append((stride, radix))
        stride *= radix
    return digits


def offset_masks(digits):
    masks = [0]
    for stride, radix in reversed(digits):
        masks = [digit * stride ^ mask for digit in range(radix) for mask in masks]
    return masks


def vector_row(ref):
    return ref[...].reshape(1, ref.shape[0])


def tap_order():
    row = lax.broadcasted_iota(jnp.int32, (HEADS * KERNEL, LANES), 0)
    lane = lax.broadcasted_iota(jnp.int32, (HEADS * KERNEL, LANES), 1)
    tap, head = lane // TAP_STRIDE, lane % TAP_STRIDE
    return (row == head * KERNEL + tap) & (head < HEADS) & (tap < KERNEL)


def ordered_span(ws_ref):
    return product(ws_ref[...], jnp.where(tap_order(), 1.0, 0.0).astype(BF16)).astype(BF16)


def spread_table(half):
    lane = lax.broadcasted_iota(jnp.int32, (2 * LANES, half), 0) % LANES
    head = lax.broadcasted_iota(jnp.int32, (2 * LANES, half), 1) // HEAD_DIM
    return jnp.where(lane == head, 1.0, 0.0).astype(BF16)


def gather_table(half):
    head = lax.broadcasted_iota(jnp.int32, (half, LANES), 0) // HEAD_DIM
    lane = lax.broadcasted_iota(jnp.int32, (half, LANES), 1)
    return jnp.where(lane == head, 1.0, 0.0).astype(BF16)


def tap_terms(taps, j):
    moved = taps if j == 0 else pltpu.roll(taps, LANES - j * TAP_STRIDE, 1)
    return jnp.concatenate(high_low(moved), 1)


def project_kernel(
    info_ref, x_ref, wq_ref, wk_ref, wv_ref, wc_ref, bq_ref, bv_ref, bc_ref, xs_ref, qkv_ref, cs_ref
):
    half = wq_ref.shape[1]
    start, length = slot_bounds(info_ref, pl.program_id(0))
    xs_ref[...] = rows_to_slot(x_ref, start, length).astype(BF16)
    inside = slot_times(0, SLOT) < length
    rows = xs_ref[...]
    qkv_ref[:, :half] = (product(rows, wq_ref[...]) + vector_row(bq_ref)).astype(BF16)
    qkv_ref[:, half : 2 * half] = product(rows, wk_ref[...]).astype(BF16)
    qkv_ref[:, 2 * half :] = (product(rows, wv_ref[...]) + vector_row(bv_ref)).astype(BF16)
    source = product(rows, wc_ref[...]) + vector_row(bc_ref)
    cs_ref[...] = jnp.where(inside, source, 0.0).astype(BF16)


def convolve_kernel(
    info_ref, xs_ref, query_ref, cs_ref, dk_ref, wp_ref, bp_ref, ws_ref, bs_ref,
    dw_ref, kc_ref, taps_ref, conv_ref,
    xh, ch,
):
    width = xs_ref.shape[1]
    half = width // 2
    put_with_edges(xh, xs_ref[...].astype(F32))
    put_with_edges(ch, cs_ref[...].astype(F32))

    def depth_chunk(c, carry):
        lanes = pl.ds(c * LANES, LANES)
        for first in range(0, SLOT, ROWS):
            total = jnp.zeros((ROWS, LANES), F32)
            for j in range(KERNEL):
                total = total + dk_ref[j : j + 1, lanes] * xh[shifted_rows(j - REACH, first, ROWS), lanes]
            dw_ref[first : first + ROWS, lanes] = total.astype(BF16)
        return carry

    for c in range(width // LANES):
        depth_chunk(c, 0)
    keyconv = product(dw_ref[...], wp_ref[...]) + vector_row(bp_ref)
    kc_ref[...] = keyconv.astype(BF16)
    span_in = (keyconv * query_ref[...].astype(F32)).astype(BF16)
    wide = jnp.broadcast_to(vector_row(bs_ref), (8, HEADS * KERNEL))
    order = jnp.where(tap_order(), 1.0, 0.0)
    shift = jnp.dot(wide, order, precision=lax.Precision.HIGHEST, preferred_element_type=F32)[0:1]
    lane = lax.broadcasted_iota(jnp.int32, (1, LANES), 1)
    used = (lane // TAP_STRIDE < KERNEL) & (lane % TAP_STRIDE < HEADS)
    shift = jnp.where(used, shift, NEGATIVE)
    logits = product(span_in, ordered_span(ws_ref)) + shift
    weights = jnp.exp(logits - tap_groups(logits, jnp.maximum))
    taps = weights / tap_groups(weights, jnp.add)
    taps_ref[...] = taps
    table = spread_table(half)
    total = jnp.zeros((SLOT, half), F32)
    for j in range(KERNEL):
        spread = product(tap_terms(taps, j), table)
        total = total + spread * ch[shifted_rows(j - REACH), :]
    conv_ref[...] = total.astype(BF16)


def head_scores(keys, query, side, outside):
    lane = lax.broadcasted_iota(jnp.int32, (1, LANES), 1)
    spare = lane == (1 - side) * HEAD_DIM
    rest = jnp.where(spare, outside, jnp.zeros_like(keys))
    keys = jnp.where(pair_mask(side), keys * BF16(0.125), rest)
    query = jnp.where(spare, jnp.ones_like(query), query)
    return right_product(keys, query)


def dead_rows(length):
    return jnp.where(slot_times(0, SLOT) < length, 0.0, NEGATIVE).astype(BF16)


def attend_kernel(info_ref, qkv_ref, conv_ref, ctx_ref, lse_ref, att):
    half = conv_ref.shape[1]
    outside = dead_rows(info_ref[HEAD + pl.program_id(0)])
    ones = jnp.ones((16, SLOT), BF16)

    def one_pair(pair):
        at = pair * LANES
        query = qkv_ref[:, pl.ds(at, LANES)]
        keys = qkv_ref[:, pl.ds(half + at, LANES)]
        values = transposed(qkv_ref[:, pl.ds(2 * half + at, LANES)])
        for side in range(2):
            scores = head_scores(keys, query, side, outside)
            highest = jnp.max(scores, axis=0, keepdims=True)
            weights = jnp.exp(scores - highest).astype(BF16)
            mine = jnp.concatenate([values[side * HEAD_DIM : (side + 1) * HEAD_DIM, :], ones], 0)
            both = product(mine, weights)
            summed = both[HEAD_DIM : HEAD_DIM + 1, :]
            att[pl.ds(at + side * HEAD_DIM, HEAD_DIM), :] = (
                both[:HEAD_DIM, :] * (1.0 / summed)
            )
            lse_ref[pl.ds(2 * pair + side, 1), :] = highest + jnp.log(summed)

    for pair in range(HEADS // 2):
        one_pair(pair)
    ctx_ref[:, :half] = transposed(att[...]).astype(BF16)
    ctx_ref[:, half:] = conv_ref[...]


def emit_chunks(sources, info_ref, keep_ref, send_ref):
    group, own = my_place(info_ref)
    count, columns = keep_ref.shape[0], keep_ref.shape[2]

    def one(position, carry):
        other = own ^ mask_at(info_ref, position)
        for ref, side in ((keep_ref, group), (send_ref, 1 - group)):
            pieces = []
            for source, rows, blocks in sources:
                first = jnp.minimum((side * count + other) * rows, source.shape[0] - rows)
                piece = source[pl.ds(pl.multiple_of(first, 8), rows), :]
                pieces += [piece[:, b * columns : (b + 1) * columns] for b in range(blocks)]
            ref[position] = jnp.concatenate(pieces, 0).astype(BF16)
        return carry

    lax.fori_loop(0, count, one, 0)


def middle_kernel(
    info_ref, ctx_ref, xs_ref, up_ref, wd_ref, bd_ref, g1_ref, b1_ref,
    ob_ref, g2_ref, b2_ref, *rest, pieces, order,
):
    weight_refs, rest = rest[: 2 * pieces], rest[2 * pieces :]
    (
        out_ref, gm_ref, gctx_ref, keep_ref, send_ref, grad_dense_ref, small_ref,
        w1, w2, bias, act, slope, low1, low2, first_t, grad_t, back, acc1, acc2, sems,
    ) = rest
    step = pl.program_id(0)
    last = pl.num_programs(0) - 1
    start, length = slot_bounds(info_ref, step)
    group = my_place(info_ref)[0]
    count, shard, part = w2.shape[1:]
    blocks = count // pieces
    span = count
    while span * shard > CHUNK_ROWS:
        span //= 2
    per = count // span
    wide = span * shard
    half = part
    width = 2 * half

    def copies():
        made = []
        for side in range(2):
            for piece in range(pieces):
                source = weight_refs[side * pieces + piece]
                at = pl.ds(piece * blocks, blocks)
                made.append((source.at[:, pl.ds(0, shard), :], w1.at[side, at, :, pl.ds(0, part)]))
                made.append((source.at[:, pl.ds(shard, shard), :], w2.at[side, at]))
                made.append(
                    (source.at[:, pl.ds(2 * shard, BIAS_ROWS), pl.ds(0, LANES)], bias.at[side, at])
                )
        return [pltpu.make_async_copy(a, b, sems.at[i]) for i, (a, b) in enumerate(made)]

    @pl.when(step == 0)
    def _():
        for copy in copies():
            copy.start()
        acc1[...] = jnp.zeros_like(acc1)
        acc2[...] = jnp.zeros_like(acc2)
        grad_dense_ref[...] = jnp.zeros_like(grad_dense_ref)
        small_ref[...] = jnp.zeros_like(small_ref)

    g1_row, g2_row = vector_row(g1_ref), vector_row(g2_ref)
    summed = product(ctx_ref[...], wd_ref[...]) + vector_row(bd_ref) + xs_ref[...].astype(F32)
    centred = summed - row_mean(summed)
    scale1 = lax.rsqrt(row_mean(centred * centred) + NORM_EPS)
    hat1 = centred * scale1
    normed1 = (hat1 * g1_row + vector_row(b1_ref)).astype(BF16)
    lane = lax.broadcasted_iota(jnp.int32, (SLOT, EXTRA), 1)
    ones = jnp.where(lane < 3, 1.0, 0.0).astype(BF16)
    for g in range(2):
        low1[g, :, :part] = normed1[:, g * part : (g + 1) * part]
        low1[g, :, part:] = ones
        first_t[g] = transposed(low1[g])[: first_t.shape[1], :]
        back[g] = jnp.zeros_like(back[g])

    @pl.when(step == 0)
    def _():
        for copy in copies():
            copy.wait()
        for side in range(2):
            for position in range(count):
                column = transposed(bias[side, position].astype(F32))
                column = jnp.concatenate(
                    [column, jnp.zeros((LANES, EXTRA - BIAS_ROWS), F32)], 1
                )
                w1[side, position, :, part:] = column[:shard].astype(BF16)

    def up_chunk(item, carry):
        r, c = item // per, item % per
        owner = group ^ r
        lanes = pl.ds(c * wide, wide)
        some = pl.ds(c * span, span)
        first = w1[r, some].reshape(wide, part + EXTRA)
        inner = right_product(low1[owner], first)
        cdf = 0.5 * (1.0 + lax.erf(inner * ROOT_HALF))
        pdf = jnp.exp(-0.5 * inner * inner) * DENSITY
        active = (inner * cdf).astype(BF16)
        act[r, :, lanes] = active
        slope[r, :, lanes] = (cdf + inner * pdf).astype(BF16)
        back[owner] += product(active, w2[r, some].reshape(wide, part))
        return carry

    for item in range(2 * per):
        up_chunk(item, 0)

    partial = jnp.concatenate([back[g] for g in range(2)], 1).astype(BF16).astype(F32)
    summed2 = partial + vector_row(ob_ref) + normed1.astype(F32)
    centred2 = summed2 - row_mean(summed2)
    scale2 = lax.rsqrt(row_mean(centred2 * centred2) + NORM_EPS)
    hat2 = centred2 * scale2
    out_ref[...] = (hat2 * g2_row + vector_row(b2_ref)).astype(BF16)

    upper = rows_to_slot(up_ref, start, length)

    def add_small(index, block):
        total = column_sum(block)
        for g in range(2):
            row = 2 * index + g
            small_ref[row : row + 1, :] += total[:, g * half : (g + 1) * half]

    add_small(0, upper * hat2)
    add_small(1, upper)
    lifted = upper * g2_row
    total2 = scale2 * (lifted - row_mean(lifted) - hat2 * row_mean(lifted * hat2))
    add_small(2, total2)
    grad_low = total2.astype(BF16)
    for g in range(2):
        low2[g] = grad_low[:, g * part : (g + 1) * part]
        grad_t[g] = transposed(low2[g])
        back[g] = jnp.zeros_like(back[g])

    def down_chunk(item, carry):
        r, c = item // per, item % per
        owner = group ^ r
        lanes = pl.ds(c * wide, wide)
        some = pl.ds(c * span, span)
        grad_active = right_product(low2[owner], w2[r, some].reshape(wide, part))
        grad_inner = (grad_active * slope[r, :, lanes].astype(F32)).astype(BF16)
        acc2[r, :, lanes] += product(grad_t[owner], act[r, :, lanes])
        acc1[r, :, lanes] += product(first_t[owner], grad_inner)
        back[owner] += product(grad_inner, w1[r, some].reshape(wide, part + EXTRA)[:, :part])
        return carry

    for item in range(2 * per):
        down_chunk(item, 0)

    grouped = jnp.concatenate([back[g] for g in range(2)], 1).astype(BF16).astype(F32)
    grad1 = grouped + total2
    add_small(3, grad1 * hat1)
    add_small(4, grad1)
    lifted = grad1 * g1_row
    mixed = scale1 * (lifted - row_mean(lifted) - hat1 * row_mean(lifted * hat1))
    mixed_low = mixed.astype(BF16)
    gm_ref[...] = mixed_low
    add_small(5, mixed_low.astype(F32))
    grad_dense_ref[...] += product(transposed(ctx_ref[...]), mixed_low)
    gctx_ref[...] = right_product(mixed_low, wd_ref[...]).astype(BF16)

    @pl.when(step == last)
    def _():
        for r, ref in enumerate((keep_ref, send_ref)):
            for c in range(per):
                lanes = slice(c * wide, (c + 1) * wide)
                first = transposed(acc1[r, :part, lanes]).astype(BF16)
                second = transposed(acc2[r, :, lanes]).astype(BF16)
                for p in range(span):
                    rows = slice(p * shard, (p + 1) * shard)
                    ref[order[c * span + p], 0:shard, :] = first[rows]
                    ref[order[c * span + p], shard : 2 * shard, :] = second[rows]
            row = acc1[r, part : part + 8, :]
            total = row.shape[1]
            for p in range(count):
                turned = pltpu.roll(row, (total - p * shard) % total, 1)
                ref[order[p], 2 * shard :, :] = turned[:, :part].astype(BF16)


def span_backward_kernel(
    info_ref, gctx_ref, xs_ref, query_ref, cs_ref, dw_ref, kc_ref, taps_ref, ws_ref, wp_ref, dense_ref,
    gs_ref, extra_ref, gk_ref, keep_ref, send_ref, small_ref,
    ch, gh, th, xh, sums, acc, *, chunk_rows,
):
    step = pl.program_id(0)
    last = pl.num_programs(0) - 1
    length = info_ref[HEAD + step]
    width = xs_ref.shape[1]
    half = width // 2

    @pl.when(step == 0)
    def _():
        acc[...] = jnp.zeros_like(acc)
        sums[...] = jnp.zeros_like(sums)
        small_ref[...] = jnp.zeros_like(small_ref)

    inside = slot_times(0, SLOT) < length
    put_with_edges(ch, cs_ref[...].astype(F32))
    grad_conv = gctx_ref[...].astype(F32)
    put_with_edges(gh, grad_conv)
    taps = taps_ref[...]
    put_with_edges(th, taps)
    table, picker = spread_table(half), gather_table(half)
    grad_taps = jnp.zeros((SLOT, LANES), F32)
    grad_source = jnp.zeros((SLOT, half), F32)
    for j in range(KERNEL):
        moved = grad_conv * ch[shifted_rows(j - REACH), :]
        here = product(moved.astype(BF16), picker)
        grad_taps = grad_taps + (here if j == 0 else pltpu.roll(here, j * TAP_STRIDE, 1))
        back = shifted_rows(REACH - j)
        grad_source = grad_source + product(tap_terms(th[back, :], j), table) * gh[back, :]
    grad_source = jnp.where(inside, grad_source, 0.0).astype(BF16)
    gs_ref[...] = grad_source
    small_ref[130:131, :] += column_sum(grad_source.astype(F32))

    query = query_ref[...].astype(F32)
    keyconv = kc_ref[...].astype(F32)
    grad_logits = taps * (grad_taps - tap_groups(taps * grad_taps, jnp.add))
    grad_logits = grad_logits.astype(BF16)
    small_ref[129:130, :LANES] += column_sum(grad_logits.astype(F32))
    span_in = (keyconv * query).astype(BF16)
    small_ref[0:TAPS_ROW, :] += product(transposed(grad_logits)[0:TAPS_ROW, :], span_in)
    grad_span = right_product(grad_logits, ordered_span(ws_ref)).astype(BF16).astype(F32)
    extra_ref[...] = (grad_span * keyconv).astype(BF16)
    grad_key = (grad_span * query).astype(BF16)
    gk_ref[...] = grad_key
    small_ref[128:129, :] += column_sum(grad_key.astype(F32))
    acc[:, 0:half] += product(transposed(dw_ref[...]), grad_key)
    acc[:, half:] += product(transposed(xs_ref[...]), grad_source)
    put_with_edges(xh, right_product(grad_key, wp_ref[...]).astype(BF16).astype(F32))

    def depth_chunk(c, carry):
        lanes = pl.ds(c * LANES, LANES)
        totals = [jnp.zeros((GROUP, LANES), F32)] * KERNEL
        for first in range(0, SLOT, ROWS):
            own = xs_ref[first : first + ROWS, lanes].astype(F32)
            for j in range(KERNEL):
                moved = xh[shifted_rows(REACH - j, first, ROWS), lanes] * own
                moved = jnp.sum(moved.reshape(ROWS // GROUP, GROUP, LANES), axis=0)
                totals[j] = totals[j] + moved
        for j in range(KERNEL):
            sums[j, :, lanes] += totals[j]
        return carry

    for c in range(width // LANES):
        depth_chunk(c, 0)

    @pl.when(step == last)
    def _():
        for j in range(KERNEL):
            total = column_sum(sums[j])
            for side in range(2):
                row = TAPS_ROW + side * KERNEL + j
                small_ref[row : row + 1, :] = total[:, side * half : (side + 1) * half]
        sources = ((acc, chunk_rows, 2), (dense_ref, chunk_rows, 2))
        emit_chunks(sources, info_ref, keep_ref, send_ref)


def input_kernel(
    info_ref, gm_ref, flat_ref, gs_ref, gk_ref, wq_ref, wk_ref, wv_ref, wc_ref, wp_ref, dk_ref,
    *rest,
):
    rows_ref, base, gh, block = rest[-4:]
    step = pl.program_id(0)
    start, length = slot_bounds(info_ref, step)
    half = gs_ref.shape[1]

    @pl.when(step == 0)
    def _():
        rows_ref[...] = jnp.zeros_like(rows_ref)

    put_with_edges(gh, right_product(gk_ref[...], wp_ref[...]).astype(BF16).astype(F32))
    total = gm_ref[...].astype(F32) + right_product(gs_ref[...], wc_ref[...])
    for third, ref in enumerate((wq_ref, wk_ref, wv_ref)):
        total = total + right_product(flat_ref[:, third * half : (third + 1) * half], ref[...])
    base[...] = total

    def depth_chunk(c, carry):
        lanes = pl.ds(c * LANES, LANES)
        for first in range(0, SLOT, ROWS):
            inner = slice(first, first + ROWS)
            total = base[inner, lanes]
            for j in range(KERNEL):
                total = total + dk_ref[j : j + 1, lanes] * gh[shifted_rows(REACH - j, first, ROWS), lanes]
            block[inner, lanes] = total.astype(BF16)
        return carry

    for c in range(half // LANES):
        depth_chunk(c, 0)
    slot_to_rows(rows_ref, start, length, block[...])


def attend_backward_kernel(
    info_ref, gctx_ref, ctx_ref, xs_ref, qkv_ref, lse_ref, extra_ref, *rest, first_slot, small, chunks
):
    if chunks is None:
        flat_ref, sum_ref, own_ref, gqt = rest
    else:
        smallm_ref, smallc_ref, _, before_ref, own_before_ref = rest[:5]
        flat_ref, keep_ref, send_ref, gqt, sum_ref, own_ref, small_ref = rest[5:]
    step = pl.program_id(0)
    half = gctx_ref.shape[1]

    @pl.when(step == 0)
    def _():
        if chunks is None:
            sum_ref[...] = jnp.zeros_like(sum_ref)
            own_ref[...] = jnp.zeros_like(own_ref)
        else:
            sum_ref[...] = before_ref[...]
            own_ref[...] = own_before_ref[...]

    outside = dead_rows(info_ref[HEAD + step + first_slot])

    def one_pair(pair):
        at = pair * LANES
        here, there, third = (pl.ds(k * half + at, LANES) for k in range(3))
        query_pair = qkv_ref[:, here]
        keys = qkv_ref[:, there]
        values = qkv_ref[:, third]
        keys_t = transposed(keys)
        grad_pair = gctx_ref[:, here]
        dots = transposed(grad_pair.astype(F32) * ctx_ref[:, here].astype(F32))
        grad_keys, grad_values = [], []
        for side in range(2):
            mask = pair_mask(side)
            rows = slice(side * HEAD_DIM, (side + 1) * HEAD_DIM)
            scores = head_scores(keys, query_pair, side, outside)
            probs = jnp.exp(scores - lse_ref[pl.ds(2 * pair + side, 1), :])
            grad_probs = right_product(jnp.where(mask, values, jnp.zeros_like(values)), grad_pair)
            weighted = column_sum(dots[rows, :])
            grad_scores = (probs * (grad_probs - weighted)).astype(BF16)
            grad_keys.append(product(grad_scores, query_pair))
            grad_values.append(product(probs.astype(BF16), grad_pair))
            gqt[pl.ds(at + side * HEAD_DIM, HEAD_DIM), :] = product(
                keys_t[rows, :], grad_scores
            )
        first = pair_mask(0)
        flat_ref[:, there] = (jnp.where(first, grad_keys[0], grad_keys[1]) * 0.125).astype(BF16)
        flat_ref[:, third] = jnp.where(first, grad_values[0], grad_values[1]).astype(BF16)

    for pair in range(HEADS // 2):
        one_pair(pair)
    flat_ref[:, :half] = (transposed(gqt[...]) * 0.125 + extra_ref[...].astype(F32)).astype(BF16)
    sum_ref[...] += product(transposed(xs_ref[...]), flat_ref[...])
    for third in range(3):
        own_ref[third : third + 1, :] += column_sum(
            flat_ref[:, third * half : (third + 1) * half].astype(F32)
        )
    if chunks is None:
        return

    @pl.when(step == pl.num_programs(0) - 1)
    def _():
        small_ref[: smallm_ref.shape[0], :] = smallm_ref[...]
        small_ref[SPAN_ROW : SPAN_ROW + smallc_ref.shape[0], :] = smallc_ref[...]
        small_ref[OWN_ROW : OWN_ROW + own_ref.shape[0], :] = own_ref[...]
        sources = ((sum_ref, chunks, 3), (small_ref, small, 1))
        emit_chunks(sources, info_ref, keep_ref, send_ref)


def restore_kernel(info_ref, slot_ref, rows_ref):
    step = pl.program_id(0)
    start, length = slot_bounds(info_ref, step)

    @pl.when(step == 0)
    def _():
        rows_ref[...] = jnp.zeros_like(rows_ref)

    slot_to_rows(rows_ref, start, length, slot_ref[...])


def assemble_kernel(info_ref, *refs, layout):
    sources, outs, small_ref = refs[:2], refs[2:-1], refs[-1]
    group, own = my_place(info_ref)
    count, _, columns = sources[0].shape

    def one(position, carry):
        for core, source in enumerate(sources):
            index = (group ^ core) * count + (own ^ mask_at(info_ref, position))
            chunk = source[position].astype(F32)
            at, place = 0, 0
            for rows, wide in layout:
                if wide == 0:
                    small_ref[pl.ds(pl.multiple_of(index * rows, 8), rows), :] = chunk[at : at + rows]
                    at += rows
                    continue
                for block in range(wide):
                    outs[place][index, :, block * columns : (block + 1) * columns] = chunk[at : at + rows]
                    at += rows
                place += 1
        return carry

    lax.fori_loop(0, count, one, 0)
    place = sum(1 for _, wide in layout if wide)
    if place == len(layout):
        return
    vectors, (depth_ref, span_ref, bias_ref) = outs[place : place + 10], outs[place + 10 :]
    for i in range(6):
        pair = [small_ref[2 * i + g : 2 * i + g + 1, :] for g in range(2)]
        vectors[i][...] = jnp.concatenate(pair, 1).reshape(2 * columns)
    for i, row in enumerate((OWN_ROW, OWN_ROW + 2, SPAN_ROW + 128, SPAN_ROW + 130)):
        vectors[6 + i][...] = small_ref[row : row + 1, :].reshape(columns)
    first = SPAN_ROW + TAPS_ROW
    for g in range(2):
        rows = small_ref[first + g * KERNEL : first + (g + 1) * KERNEL, :]
        depth_ref[:, g * columns : (g + 1) * columns] = rows
    order = jnp.where(tap_order(), 1.0, 0.0).astype(BF16)
    span_ref[...] = product(order, small_ref[SPAN_ROW : SPAN_ROW + LANES, :].astype(BF16))
    bias = small_ref[SPAN_ROW + 129 : SPAN_ROW + 130, :LANES]
    bias = jnp.broadcast_to(bias, (16, LANES)).astype(BF16)
    bias_ref[...] = right_product(bias, order)[0:1].reshape(HEADS * KERNEL)


def resident(shape):
    zeros = (0,) * len(shape)
    return pl.BlockSpec(tuple(shape), lambda *_: zeros, pipeline_mode=pl.Buffered(1))


def slot_block(columns, rows=SLOT, column=0):
    return pl.BlockSpec((None, rows, columns), lambda i: (i, 0, column))


SCALARS = pl.BlockSpec(memory_space=pltpu.SMEM)
ANYWHERE = pl.BlockSpec(memory_space=pl.ANY)
LIMIT = 60 * 1024 * 1024


def shape_of(*dims, dtype=F32):
    return jax.ShapeDtypeStruct(dims, dtype)


def cost(flops, nbytes):
    return pl.CostEstimate(flops=int(flops), bytes_accessed=int(nbytes), transcendentals=0)


PARAMS = pltpu.CompilerParams(vmem_limit_bytes=LIMIT)
LARGE = pltpu.CompilerParams(vmem_limit_bytes=LIMIT + 3 * 1024 * 1024)
RATE = 1.15e9


def busy(us):
    return cost(us * RATE, us * 1e6)


def run_project(info, slots, x, *rest):
    total, width = x.shape
    half = width // 2
    return pl.pallas_call(
        project_kernel,
        grid=(slots,),
        in_specs=[SCALARS] + [resident(a.shape) for a in (x,) + rest],
        out_specs=[slot_block(width), slot_block(3 * half), slot_block(half)],
        out_shape=[
            shape_of(slots, SLOT, width, dtype=BF16),
            shape_of(slots, SLOT, 3 * half, dtype=BF16),
            shape_of(slots, SLOT, half, dtype=BF16),
        ],
        compiler_params=PARAMS,
        cost_estimate=busy(10),
        name="project",
    )(info, x, *rest)


def run_convolve(info, xs, qkv, cs, *rest):
    slots, _, width = xs.shape
    half = width // 2
    return pl.pallas_call(
        convolve_kernel,
        grid=(slots,),
        in_specs=[SCALARS, slot_block(width), slot_block(half), slot_block(half)]
        + [resident(a.shape) for a in rest],
        out_specs=[slot_block(width), slot_block(half), slot_block(LANES), slot_block(half)],
        out_shape=[
            shape_of(slots, SLOT, width, dtype=BF16),
            shape_of(slots, SLOT, half, dtype=BF16),
            shape_of(slots, SLOT, LANES),
            shape_of(slots, SLOT, half, dtype=BF16),
        ],
        scratch_shapes=[
            pltpu.VMEM((SLOT + 2 * EDGE, width), F32),
            pltpu.VMEM((SLOT + 2 * EDGE, half), F32),
        ],
        compiler_params=PARAMS,
        cost_estimate=busy(15),
        name="convolve",
    )(info, xs, qkv, cs, *rest)


def run_attend(info, qkv, conv):
    slots, _, half = conv.shape
    return pl.pallas_call(
        attend_kernel,
        grid=(slots,),
        in_specs=[SCALARS, slot_block(3 * half), slot_block(half)],
        out_specs=[slot_block(2 * half), slot_block(SLOT, 8)],
        out_shape=[shape_of(slots, SLOT, 2 * half, dtype=BF16), shape_of(slots, 8, SLOT)],
        scratch_shapes=[pltpu.VMEM((half, SLOT), F32)],
        compiler_params=PARAMS,
        cost_estimate=busy(16),
        name="attend",
    )(info, qkv, conv)


def run_middle(info, ctx, xs, upstream, vectors, wd, weights, shard, count):
    bits = offset_masks(digits_of(count, RADIX))
    order = [bits.index(mask) for mask in offset_masks(digits_of(count))]
    slots, _, width = xs.shape
    half = width // 2
    hidden = count * shard
    pieces = len(weights) // 2
    bd, g1, b1, ob, g2, b2 = vectors
    rows = 2 * shard + BIAS_ROWS
    return pl.pallas_call(
        functools.partial(middle_kernel, pieces=pieces, order=order),
        grid=(slots,),
        in_specs=[SCALARS, slot_block(width), slot_block(width)]
        + [resident(a.shape) for a in (upstream, wd, bd, g1, b1, ob, g2, b2)]
        + [ANYWHERE] * len(weights),
        out_specs=[slot_block(width), slot_block(width), slot_block(width)]
        + [resident((count, rows, half))] * 2
        + [resident((width, width)), resident((16, half))],
        out_shape=[
            shape_of(slots, SLOT, width, dtype=BF16),
            shape_of(slots, SLOT, width, dtype=BF16),
            shape_of(slots, SLOT, width, dtype=BF16),
        ]
        + [shape_of(count, rows, half, dtype=BF16)] * 2
        + [shape_of(width, width), shape_of(16, half)],
        scratch_shapes=[
            pltpu.VMEM((2, count, shard, half + EXTRA), BF16),
            pltpu.VMEM((2, count, shard, half), BF16),
            pltpu.VMEM((2, count, BIAS_ROWS, LANES), BF16),
            pltpu.VMEM((2, SLOT, hidden), BF16),
            pltpu.VMEM((2, SLOT, hidden), BF16),
            pltpu.VMEM((2, SLOT, half + EXTRA), BF16),
            pltpu.VMEM((2, SLOT, half), BF16),
            pltpu.VMEM((2, half + 16, SLOT), BF16),
            pltpu.VMEM((2, half, SLOT), BF16),
            pltpu.VMEM((2, SLOT, half), F32),
            pltpu.VMEM((2, half + 16, hidden), F32),
            pltpu.VMEM((2, half, hidden), F32),
            pltpu.SemaphoreType.DMA((6 * pieces,)),
        ],
        compiler_params=LARGE,
        cost_estimate=busy(64),
        name="feed_forward",
    )(info, ctx, xs, upstream, wd, bd, g1, b1, ob, g2, b2, *weights)


def run_span_backward(info, gctx, xs, qkv, cs, dw, kc, taps, ws, wp, dense, count, chunk_rows):
    slots, _, width = xs.shape
    half = width // 2
    return pl.pallas_call(
        functools.partial(span_backward_kernel, chunk_rows=chunk_rows),
        grid=(slots,),
        in_specs=[
            SCALARS, slot_block(half, column=1), slot_block(width), slot_block(half),
            slot_block(half), slot_block(width), slot_block(half), slot_block(LANES),
            resident(ws.shape), resident(wp.shape), resident(dense.shape),
        ],
        out_specs=[slot_block(half)] * 3
        + [resident((count, 4 * chunk_rows, half))] * 2
        + [resident((136, half))],
        out_shape=[
            shape_of(slots, SLOT, half, dtype=BF16),
            shape_of(slots, SLOT, half, dtype=BF16),
            shape_of(slots, SLOT, half, dtype=BF16),
        ]
        + [shape_of(count, 4 * chunk_rows, half, dtype=BF16)] * 2
        + [shape_of(136, half)],
        scratch_shapes=[
            pltpu.VMEM((SLOT + 2 * EDGE, half), F32),
            pltpu.VMEM((SLOT + 2 * EDGE, half), F32),
            pltpu.VMEM((SLOT + 2 * EDGE, LANES), F32),
            pltpu.VMEM((SLOT + 2 * EDGE, width), F32),
            pltpu.VMEM((KERNEL, GROUP, width), F32),
            pltpu.VMEM((width, width), F32),
        ],
        compiler_params=PARAMS,
        cost_estimate=busy(23),
        name="span_backward",
    )(info, gctx, xs, qkv, cs, dw, kc, taps, ws, wp, dense)


def run_attend_backward(info, gctx, ctx, xs, qkv, lse, extra, count, chunk_rows, before=None, smalls=()):
    slots, _, width = xs.shape
    half = width // 2
    ending = before is not None
    first = 1 if ending else 0
    small_rows = small_chunk(count)
    rows = 3 * chunk_rows + small_rows

    def block(columns, rows=SLOT):
        return pl.BlockSpec((None, rows, columns), lambda i: (i + first, 0, 0))

    more = list(smalls) + list(before) if ending else []
    more_specs = [resident(a.shape) for a in more]
    if ending:
        more_specs[len(smalls)] = ANYWHERE
    sums = [(width, 3 * half), (8, half)]
    return pl.pallas_call(
        functools.partial(
            attend_backward_kernel, first_slot=first, small=small_rows, chunks=chunk_rows if ending else None
        ),
        grid=(slots - 1 if ending else 1,),
        in_specs=[SCALARS, block(half), block(half), block(width), block(3 * half), block(SLOT, 8), block(half)]
        + more_specs,
        out_specs=[block(3 * half)]
        + ([resident((count, rows, half))] * 2 if ending else [resident(d) for d in sums]),
        out_shape=[shape_of(slots, SLOT, 3 * half, dtype=BF16)]
        + ([shape_of(count, rows, half, dtype=BF16)] * 2 if ending else [shape_of(*d) for d in sums]),
        scratch_shapes=[pltpu.VMEM((half, SLOT), F32)]
        + ([pltpu.VMEM(d, F32) for d in sums + [(SMALL_ROWS, half)]] if ending else []),
        input_output_aliases={7 + len(smalls): 0} if ending else {},
        compiler_params=PARAMS,
        cost_estimate=busy(14 if ending else 7),
        name="attend_backward",
    )(info, gctx, ctx, xs, qkv, lse, extra, *more)


def run_input(info, gm, flat, gs, gk, weights, dk, total, before=None):
    slots, _, width = gm.shape
    half = width // 2
    side = 0 if before is None else 1
    more = [] if before is None else [before]
    rows = pl.BlockSpec((half, half), lambda i: (side, 0))
    return pl.pallas_call(
        input_kernel,
        grid=(slots,),
        in_specs=[
            SCALARS, slot_block(half, column=side), slot_block(3 * half), slot_block(half),
            slot_block(half),
        ]
        + [rows] * len(weights)
        + [pl.BlockSpec((KERNEL, half), lambda i: (0, side))]
        + [ANYWHERE] * len(more),
        out_specs=pl.BlockSpec((total, half), lambda i: (0, side)),
        out_shape=shape_of(total, width, dtype=BF16),
        scratch_shapes=[
            pltpu.VMEM((SLOT, half), F32),
            pltpu.VMEM((SLOT + 2 * EDGE, half), F32),
            pltpu.VMEM((SLOT, half), BF16),
        ],
        input_output_aliases={6 + len(weights): 0} if more else {},
        compiler_params=PARAMS,
        cost_estimate=busy(8),
        name="input_gradient",
    )(info, gm, flat, gs, gk, *weights, dk, *more)


def run_restore(info, block, total):
    slots, _, width = block.shape
    return pl.pallas_call(
        restore_kernel,
        grid=(slots,),
        in_specs=[SCALARS, slot_block(width)],
        out_specs=resident((total, width)),
        out_shape=shape_of(total, width, dtype=BF16),
        compiler_params=PARAMS,
        cost_estimate=busy(4),
        name="restore_rows",
    )(info, block)


def run_assemble(info, sources, layout):
    count, _, half = sources[0].shape
    width, taps = 2 * half, HEADS * KERNEL
    shapes = [(2 * count, rows, wide * half) for rows, wide in layout if wide]
    whole = len(shapes)
    if whole < len(layout):
        shapes += [(width,)] * 6 + [(half,)] * 4 + [(KERNEL, width), (taps, half), (taps,)]
    outs = pl.pallas_call(
        functools.partial(assemble_kernel, layout=layout),
        in_specs=[SCALARS] + [pl.BlockSpec(memory_space=pltpu.VMEM)] * len(sources),
        out_specs=[pl.BlockSpec(memory_space=pltpu.VMEM)] * len(shapes),
        out_shape=[shape_of(*s) for s in shapes],
        scratch_shapes=[pltpu.VMEM((2 * count * small_chunk(count), half), F32)],
        compiler_params=PARAMS,
        cost_estimate=busy(3),
        name="assemble",
    )(info, *sources)
    return [o.reshape(2 * count * o.shape[1], -1) for o in outs[:whole]] + list(outs[whole:])


def small_chunk(count):
    return round_up(-(-SMALL_ROWS // (2 * count)), 8)


def swap_groups(block):
    return lax.ppermute(block, "grp", [(0, 1), (1, 0)])


def send_across(block, count, offset):
    return lax.ppermute(block, "dp", [(i, i ^ offset) for i in range(count)])


def tree_sum(parts):
    parts = [p.astype(F32) for p in parts]
    while len(parts) > 1:
        parts = [parts[i] + parts[i + 1] for i in range(0, len(parts), 2)]
    return parts[0].astype(BF16)


def tie(value, *others):
    return lax.optimization_barrier((value, others))[0]


def advance(done, *sums, held=()):
    both = sums + tuple(held)
    arrived = lax.optimization_barrier((done, [s.current for s in both]))[1]
    for one, current in zip(both, arrived):
        one.current = current
    sent = []
    for one in sums:
        sent += one.step()
    return sent


class ChunkSum:
    def __init__(self, keep, send, count, digits=None):
        self.count, self.digits = count, digits or digits_of(count)
        self.current, self.stage = [keep, swap_groups(send)], 0

    def step(self):
        if self.stage == len(self.digits):
            return []
        stride, radix = self.digits[self.stage]
        size = self.current[0].shape[0] // radix
        parts = [
            tree_sum([p[s * size : (s + 1) * size] for p in self.current]) for s in range(radix)
        ]
        self.current = [parts[0]] + [
            send_across(parts[s], self.count, s * stride) for s in range(1, radix)
        ]
        self.stage += 1
        return parts

    def finish(self):
        while self.stage < len(self.digits):
            self.step()
        return tree_sum(self.current)


class Gather:
    def __init__(self, own, count, digits):
        self.count, self.digits, self.stage, self.current = count, digits, 0, [own]

    def step(self):
        own = jnp.concatenate(self.current, 0)
        if self.stage == len(self.digits):
            self.current = [own]
            return [own]
        stride, radix = self.digits[self.stage]
        self.current = [own] + [send_across(own, self.count, s * stride) for s in range(1, radix)]
        self.stage += 1
        return [own]

    def finish(self, wanted=None):
        while self.stage < len(self.digits):
            self.step()
        whole = jnp.concatenate(self.current, 0)
        if wanted is None:
            return whole
        masks = [0]
        for stride, radix in self.digits:
            masks = [digit * stride ^ mask for digit in range(radix) for mask in masks]
        places = [masks.index(mask) for mask in wanted]
        return jnp.concatenate([whole[p : p + 1] for p in places], 0)


def round_up(value, unit):
    return -(-value // unit) * unit


def weight_shard(inter_weight, inter_bias, down_weight):
    columns = inter_weight.shape[2]
    shard = round_up(columns, 16)
    half = down_weight.shape[2]
    pad = ((0, shard - columns), (0, 0))
    first = jnp.pad(jnp.transpose(inter_weight[0]), pad)
    second = jnp.pad(down_weight[0], pad)
    rest, terms = inter_bias, []
    for _ in range(3):
        term = lax.reduce_precision(rest, 8, 7)
        terms.append(term)
        rest = rest - term
    terms = jnp.concatenate(terms, 0).astype(BF16)
    terms = jnp.pad(terms, ((0, BIAS_ROWS - 3), (0, half - columns)))
    return jnp.concatenate([first, second, terms], 0)[None], shard


def on_device(
    count, layer_input, lengths, query_weight, query_bias, key_weight, value_weight, value_bias,
    depth_kernel, point_weight, point_bias, span_weight, span_bias, conv_out_weight,
    conv_out_bias, dense_weight, dense_bias, first_gain, first_shift, inter_weight, inter_bias,
    grouped_down_weight, output_bias, second_gain, second_shift, upstream_grad,
):
    total, width = layer_input.shape
    half = width // 2
    slots = lengths.shape[1]
    chunk_rows = round_up(-(-width // (2 * count)), 8)
    info = jnp.concatenate(
        [
            lax.axis_index("grp").astype(jnp.int32).reshape(1),
            lax.axis_index("dp").astype(jnp.int32).reshape(1),
            lengths[0],
            jnp.array(offset_masks(digits_of(count)), jnp.int32),
        ]
    )
    own_weights, shard = weight_shard(inter_weight, inter_bias, grouped_down_weight)
    digits = digits_of(count)
    block = own_weights
    for stride, radix in reversed(digits[1:]):
        block = [block] + [send_across(block, count, s * stride) for s in range(1, radix)]
        if stride == digits[1][0]:
            break
        block = jnp.concatenate(block, 0)

    xs, qkv, cs = run_project(
        info, slots, tie(layer_input, own_weights), query_weight, key_weight, value_weight,
        conv_out_weight, query_bias, value_bias, conv_out_bias,
    )
    block = jnp.concatenate(tie(block, xs), 0)
    stride, radix = digits[0]
    block = [block] + [send_across(block, count, s * stride) for s in range(1, radix)]
    dw, kc, taps, conv = run_convolve(
        info, tie(xs, block[0]), qkv, cs, depth_kernel, point_weight, point_bias, span_weight, span_bias
    )
    ctx, lse = run_attend(info, qkv, conv)
    early = swap_groups(block[0])
    block = block[:1] + tie(block[1:], ctx)
    weights = block + [early] + [swap_groups(b) for b in block[1:]]
    vectors = (dense_bias, first_gain, first_shift, output_bias, second_gain, second_shift)
    out_slots, gm, gctx, keep, send, dense, small_m = run_middle(
        info, ctx, xs, upstream_grad, vectors, dense_weight, weights, shard, count
    )
    ffn_sum = ChunkSum(keep, send, count, digits_of(count, RADIX))
    layer_out = run_restore(info, tie(out_slots, send), total)
    sent = advance(layer_out, ffn_sum)
    gs, extra, gk, keep_c, send_c, small_c = run_span_backward(
        info, tie(gctx, sent), xs, qkv, cs, dw, kc, taps, span_weight, point_weight, dense, count, chunk_rows
    )
    span_sum = ChunkSum(keep_c, send_c, count)
    sent = advance(gs, ffn_sum)
    part = run_attend_backward(
        info, tie(gctx, send_c, sent), ctx, xs, qkv, lse, extra, count, chunk_rows
    )
    sent = advance(part, span_sum, ffn_sum)
    flat, keep_a, send_a = run_attend_backward(
        info, tie(gctx, sent), ctx, xs, qkv, lse, extra, count, chunk_rows, part, [small_m, small_c]
    )
    mixer_sum = ChunkSum(keep_a, send_a, count)
    sent = advance(flat, span_sum, held=[ffn_sum])
    matrices = [query_weight, key_weight, value_weight, conv_out_weight, point_weight]
    in_half = run_input(info, tie(gm, sent, send_a), flat, gs, gk, matrices, depth_kernel, total)
    digits, bits = digits_of(count), digits_of(count, RADIX)
    sent = advance(in_half, mixer_sum, held=[span_sum])
    wanted = offset_masks(digits[1:])
    span_all = Gather(span_sum.finish(), count, bits[:0:-1])
    sent += span_all.step()
    in_grad = run_input(info, tie(gm, sent), flat, gs, gk, matrices, depth_kernel, total, in_half)
    sent = advance(in_grad, mixer_sum, span_all)
    mixer_own = tie(mixer_sum.finish(), sent)
    span_plane = Gather(span_all.finish(wanted), count, digits[:1])
    mixer_all = Gather(mixer_own, count, bits[:0:-1])
    sent = mixer_all.step() + span_plane.step()
    for _ in bits[2:]:
        sent = advance(sent, mixer_all)
    advance(sent, held=[mixer_all, span_plane])
    mixer_plane = Gather(mixer_all.finish(wanted), count, digits[:1])
    sent = mixer_plane.step()
    span_all = tie(span_plane.finish(), sent)
    span_other = swap_groups(span_all)
    ffn = ffn_sum.finish()
    rows = chunk_rows
    span_outs = run_assemble(info, [span_all, span_other], ((rows, 1), (rows, 1), (rows, 2)))
    mixer_all = mixer_plane.finish()
    mixer_outs = run_assemble(
        info, [mixer_all, swap_groups(mixer_all)], ((rows, 1),) * 3 + ((small_chunk(count), 0),)
    )
    outs = mixer_outs[:3] + span_outs + mixer_outs[3:]
    grad_query, grad_key, grad_value, grad_point, grad_conv, grad_dense = [g[:width] for g in outs[:6]]
    vectors, (grad_depth, grad_span, grad_span_bias) = outs[6:16], outs[16:]
    ffn = ffn.astype(F32)
    columns = inter_weight.shape[2]
    return (
        layer_out,
        in_grad,
        grad_query,
        vectors[6],
        grad_key,
        grad_value,
        vectors[7],
        grad_depth,
        grad_point,
        vectors[8],
        jnp.transpose(grad_span),
        grad_span_bias,
        grad_conv,
        vectors[9],
        grad_dense,
        vectors[5],
        vectors[3],
        vectors[4],
        jnp.transpose(ffn[:, :columns], (0, 2, 1)),
        ffn[:, 2 * shard, :columns],
        ffn[:, shard : shard + columns],
        vectors[2],
        vectors[0],
        vectors[1],
    )


def solution(mesh):
    rows = P(("grp", "dp"), None)
    one = P()
    return jax.shard_map(
        functools.partial(on_device, mesh.shape["dp"]),
        mesh=mesh,
        in_specs=(rows, rows) + (one,) * 16
        + (P("grp", None, "dp"), P("grp", "dp"), P("grp", "dp", None)) + (one,) * 3 + (rows,),
        out_specs=(rows, rows) + (one,) * 16
        + (P("grp", None, "dp"), P("grp", "dp"), P("grp", "dp", None)) + (one,) * 3,
        check_vma=False,
    )
```
